32 devices in a mesh: cfg: 2 (over y), site: 4 (over z), vec: 2 (over x), tslice: 2 (over core).
Axes of the slice: x: 2, y: 2, z: 4, core: 2. Of those that a mesh axis runs over, the one named last changes fastest.
Arguments:
- eigvecs: float32 [4, 2, 3, 384, 4, 512], P(('cfg', 'tslice'), None, None, 'vec', 'site'), parts along dimension 0, may hold values from -1.5 to 1.5
- links: float32 [4, 3, 2, 3, 3, 4, 512], P(('cfg', 'tslice'), None, None, None, None, 'site'), parts along dimension 0, may hold values from -1 to 1, as said below
- peramb: bfloat16 [4, 8, 4, 2, 384, 384], P(('cfg', 'tslice'), 'site', None, None, 'vec'), parts along dimension 0, may hold values from -0.21875 to 0.21875
- block_owner: int32 [2], replicated, may hold values from 0 to 1, each once
- momenta: int32 [2, 3], replicated, may hold values from -2 to 2, as said below
Outputs:
- projected: bfloat16 [4, 8, 4, 2, 2, 384, 384], P(('cfg', 'tslice'), 'site', None, None, None, 'vec'), parts along dimension 0
The draws below stay inside these ranges and needn't reach their ends.
There are 2 independent parts, one for each index of `cfg`. The reference program is written for one: setup_inputs(seed, part) draws one part's arguments, and reference() takes and returns one part's arrays. A program takes and returns all parts, laid end to end along the dimension named above; an argument that names none is the same for every part. Nothing has to cross between parts.
Inputs may be any that keep to these rules, and one draw needn't show every extreme that they name: Block b of eigvecs holds the eigenvectors numbered from block_owner[b] * 192 on; every block number appears once. `momenta`: every component is -2, -1, 1 or 2, never zero. `links`: every 3 x 3 link matrix is unitary.
All inputs are finite; a program needn't handle non-finite values.
Results may differ from the reference program's by a relative error of at most 0.0065.
Values may be sent and summed in bfloat16 or wider, within the bound.
No kernel may reach another device: no remote copies, remote signals or barrier semaphores. Data moves between devices by JAX's collectives and lax.ppermute only.
A program may use at most 128 MiB of HBM per device.

```python
import math
import jax
import jax.numpy as jnp
from jax import lax

NVEC = 384
LX = 32
LY = 16
K = 2
P_SIZE = 2
SPINS = 4
LZ = 4
LXY = 512
NT = 2
NSINK = 8
NBLK = 2


def draw_momenta(key, part):
    raw = jax.random.randint(jax.random.fold_in(key, 11), (P_SIZE, 3), 0, 4, dtype=jnp.int32)
    return raw - 2 + (raw >= 2).astype(jnp.int32)


def complex_product(left_re, left_im, right_re, right_im):
    out_re = []
    out_im = []
    for row in range(3):
        line_re = []
        line_im = []
        for col in range(3):
            acc_re = left_re[row][0] * right_re[0][col] - left_im[row][0] * right_im[0][col]
            acc_im = left_re[row][0] * right_im[0][col] + left_im[row][0] * right_re[0][col]
            for mid in range(1, 3):
                acc_re = acc_re + left_re[row][mid] * right_re[mid][col] - left_im[row][mid] * right_im[mid][col]
                acc_im = acc_im + left_re[row][mid] * right_im[mid][col] + left_im[row][mid] * right_re[mid][col]
            line_re.append(acc_re)
            line_im.append(acc_im)
        out_re.append(line_re)
        out_im.append(line_im)
    return (out_re, out_im)


def givens(first, second, rotation, phase_a, phase_b):
    zeros = jnp.zeros_like(rotation)
    ones = jnp.ones_like(rotation)
    mat_re = [[ones if r == c else zeros for c in range(3)] for r in range(3)]
    mat_im = [[zeros for c in range(3)] for r in range(3)]
    cosine = jnp.cos(rotation)
    sine = jnp.sin(rotation)
    mat_re[first][first] = cosine * jnp.cos(phase_a)
    mat_im[first][first] = cosine * jnp.sin(phase_a)
    mat_re[first][second] = sine * jnp.cos(phase_b)
    mat_im[first][second] = sine * jnp.sin(phase_b)
    mat_re[second][first] = -sine * jnp.cos(phase_b)
    mat_im[second][first] = sine * jnp.sin(phase_b)
    mat_re[second][second] = cosine * jnp.cos(phase_a)
    mat_im[second][second] = -cosine * jnp.sin(phase_a)
    return (mat_re, mat_im)


def draw_links(key, part):
    shape = (12, NT, 3, LZ, LX * LY)
    angles = jax.random.uniform(jax.random.fold_in(key, 23), shape, jnp.float32, -3.14159265, 3.14159265)
    zeros = jnp.zeros_like(angles[0])
    diag_re = [[jnp.cos(angles[r]) if r == c else zeros for c in range(3)] for r in range(3)]
    diag_im = [[jnp.sin(angles[r]) if r == c else zeros for c in range(3)] for r in range(3)]
    total_re, total_im = (diag_re, diag_im)
    pairs = [(0, 1), (1, 2), (0, 2)]
    for index in range(3):
        first, second = pairs[index]
        base = 3 + 3 * index
        rot_re, rot_im = givens(first, second, angles[base], angles[base + 1], angles[base + 2])
        total_re, total_im = complex_product(total_re, total_im, rot_re, rot_im)
    real = jnp.stack([jnp.stack(row, axis=2) for row in total_re], axis=2)
    imag = jnp.stack([jnp.stack(row, axis=2) for row in total_im], axis=2)
    return jnp.stack([real, imag], axis=2)


def steps_of(key, dims, shards, low, largest):
    level, own = 1.0, jax.random.fold_in(key, 6)
    for position, shards_of in shards:
        draws = jnp.exp(jax.random.uniform(jax.random.fold_in(own, position), (shards_of,), jnp.float32, low / len(shards), largest / len(shards)))
        level = level * jnp.repeat(draws, dims[position] // shards_of).reshape([-1 if axis == position else 1 for axis in range(len(dims))])
    return level


def normal_values(own_key, shape, spread, bound, split=(), kind=jnp.bfloat16):
    values = jax.random.normal(own_key, shape, jnp.float32) * spread
    if len(split) > 0:
        values = steps_of(own_key, shape, split, -0.22, 0.18) * values
    return jnp.clip(values, min=-bound, max=bound).astype(kind)


def setup_inputs(seed: int = 0, part: int = 0) -> dict:
    keys = jax.random.split(jax.random.key(seed), 6)
    part_splits = jax.random.split(jax.random.fold_in(keys[5], part), 6)
    eigvecs = normal_values(part_splits[0], (NT, 2, 3, NVEC, LZ, LXY), ((6 * LX * LY * LZ) ** -0.25), 1.5, ((0, 2), (3, 2), (4, 4)), jnp.float32)
    links = draw_links(jax.random.fold_in(jax.random.fold_in(keys[5], part), 71), part)
    peramb = normal_values(part_splits[2], (NT, NSINK, SPINS, 2, NVEC, NVEC), (2 * NVEC) ** -0.5, 0.21875, ((0, 2), (1, 4), (4, 2)))
    block_owner = jax.random.permutation(keys[3], NBLK).astype(jnp.int32)
    momenta = draw_momenta(jax.random.fold_in(keys[5], 71), part)
    return {"eigvecs": eigvecs, "links": links, "peramb": peramb, "block_owner": block_owner, "momenta": momenta}


two_pi = 2.0 * math.pi


def along(field, direction, sense):
    width = field.shape[-1]
    column = lax.broadcasted_iota(jnp.int32, (width,), 0) % LX
    if direction == 0:
        if sense > 0:
            return jnp.where(column == LX - 1, jnp.roll(field, LX - 1, -1), jnp.roll(field, -1, -1))
        return jnp.where(column == 0, jnp.roll(field, 1 - LX, -1), jnp.roll(field, 1, -1))
    return jnp.roll(field, -sense * LX, -1)


def link_times(link_re, link_im, field_re, field_im, dagger):
    result_re = []
    result_im = []
    for target in range(3):
        summed_re = jnp.zeros_like(field_re[0])
        summed_im = jnp.zeros_like(field_re[0])
        for source in range(3):
            if dagger:
                entry_re = link_re[source, target][None]
                entry_im = -link_im[source, target][None]
            else:
                entry_re = link_re[target, source][None]
                entry_im = link_im[target, source][None]
            summed_re = summed_re + entry_re * field_re[source] - entry_im * field_im[source]
            summed_im = summed_im + entry_re * field_im[source] + entry_im * field_re[source]
        result_re.append(summed_re)
        result_im.append(summed_im)
    return jnp.stack(result_re), jnp.stack(result_im)


def chebyshev(initial, operate):
    previous = initial
    current = operate(initial)
    for repeat in range(K - 1):
        following = 2.0 * operate(current) - previous
        previous = current
        current = following
    return current


def phase_angle(momenta, across, upward, depth, extent):
    return two_pi * ((momenta[:, 0, None, None] * across[None]).astype(jnp.float32) / LX
                     + (momenta[:, 1, None, None] * upward[None]).astype(jnp.float32) / LY
                     + (momenta[:, 2, None, None] * depth[None]).astype(jnp.float32) / extent)


def hop_full(field, links_slice):
    total_re = jnp.zeros_like(field[0])
    total_im = jnp.zeros_like(field[0])
    for direction in range(3):
        link_re = links_slice[direction, 0]
        link_im = links_slice[direction, 1]
        if direction < 2:
            ahead = along(field, direction, 1)
            behind = along(field, direction, -1)
            back_re = along(link_re, direction, -1)
            back_im = along(link_im, direction, -1)
        else:
            ahead = jnp.roll(field, -1, 3)
            behind = jnp.roll(field, 1, 3)
            back_re = jnp.roll(link_re, 1, 2)
            back_im = jnp.roll(link_im, 1, 2)
        forward = link_times(link_re, link_im, ahead[0], ahead[1], False)
        backward = link_times(back_re, back_im, behind[0], behind[1], True)
        total_re = total_re + forward[0] + backward[0]
        total_im = total_im + forward[1] + backward[1]
    return jnp.stack([total_re, total_im]) * (-1.0 / 6.0)


def reference(eigvecs, links, peramb, block_owner, momenta):
    block = NVEC // NBLK
    ranks = jnp.arange(NBLK, dtype=jnp.int32)
    inverse = jnp.sum(ranks[:, None] * (block_owner[:, None] == ranks[None, :]).astype(jnp.int32), axis=0)
    flat = lax.broadcasted_iota(jnp.int32, (LZ, LXY), 1)
    depth = lax.broadcasted_iota(jnp.int32, (LZ, LXY), 0)
    theta = phase_angle(momenta, flat % LX, flat // LX, depth, LZ)

    def one_slice(operands):
        vectors, links_slice, perambulator = operands
        grouped = vectors.reshape(2, 3, NBLK, block, LZ, LXY)
        ordered = jnp.take(grouped, inverse, axis=2)
        blocks_first = jnp.moveaxis(ordered, 2, 0)
        filtered_blocks = lax.map(lambda field: chebyshev(field, lambda source_field: hop_full(source_field, links_slice)), blocks_first)
        filtered = jnp.moveaxis(filtered_blocks, 0, 2).reshape(2, 3, NVEC, LZ, LXY).astype(jnp.bfloat16)
        left = filtered.astype(jnp.float32)

        def elemental(angle):
            cosine = jnp.cos(angle)
            sine = jnp.sin(angle)
            shift_re = cosine * left[0] + sine * left[1]
            shift_im = cosine * left[1] - sine * left[0]
            shifted = jnp.stack([shift_re, shift_im]).astype(jnp.bfloat16)
            shifted_values = lax.optimization_barrier(shifted).astype(jnp.float32)
            product = jnp.einsum("acizs,bckzs->aibk", left, shifted_values, precision=lax.Precision.HIGHEST)
            real = product[0, :, 0] + product[1, :, 1]
            imag = product[0, :, 1] - product[1, :, 0]
            return jnp.stack([real, imag])

        phi = lax.map(elemental, theta)
        phi_rounded = phi.astype(jnp.bfloat16)
        phi_values = lax.optimization_barrier(phi_rounded).astype(jnp.float32)

        def one_sink(tau):
            tau_values = tau.astype(jnp.float32)
            real = (jnp.einsum("qij,pjk->qpik", tau_values[:, 0], phi_values[:, 0], precision=lax.Precision.HIGHEST)
                    - jnp.einsum("qij,pjk->qpik", tau_values[:, 1], phi_values[:, 1], precision=lax.Precision.HIGHEST))
            imag = (jnp.einsum("qij,pjk->qpik", tau_values[:, 0], phi_values[:, 1], precision=lax.Precision.HIGHEST)
                    + jnp.einsum("qij,pjk->qpik", tau_values[:, 1], phi_values[:, 0], precision=lax.Precision.HIGHEST))
            return jnp.stack([real, imag], axis=2).astype(jnp.bfloat16)

        return lax.map(one_sink, perambulator)

    return lax.map(one_slice, (eigvecs, links, peramb))
```

```python
import functools
import math

import jax
import jax.numpy as jnp
from jax import lax
from jax.experimental import pallas as pl
from jax.experimental.pallas import tpu as pltpu
from jax.sharding import PartitionSpec as P

LX = 32
LY = 16
LANES = 128

two_pi = 2.0 * math.pi


def phase_angle(momenta, across, upward, depth, extent):
    return two_pi * (
        (momenta[:, 0, None, None] * across[None]).astype(jnp.float32) / LX
        + (momenta[:, 1, None, None] * upward[None]).astype(jnp.float32) / LY
        + (momenta[:, 2, None, None] * depth[None]).astype(jnp.float32) / extent
    )


class Shifts:
    def __init__(self):
        lane = lax.broadcasted_iota(jnp.int32, (8, LANES), 1)
        row = lax.broadcasted_iota(jnp.int32, (8, LANES), 0) % 4
        column = lane % LX
        self.x_last = column == LX - 1
        self.x_first = column == 0
        self.y_high = lane >= LANES - LX
        self.y_low = lane < LX
        self.row_last = row == 3
        self.row_first = row == 0

    def ahead_x(self, v):
        return jnp.where(self.x_last, pltpu.roll(v, LX - 1, 1), pltpu.roll(v, LANES - 1, 1))

    def behind_x(self, v):
        return jnp.where(self.x_first, pltpu.roll(v, LANES - LX + 1, 1), pltpu.roll(v, 1, 1))

    def ahead_y(self, v):
        a = pltpu.roll(v, LANES - LX, 1)
        wrapped = jnp.where(self.row_last, pltpu.roll(a, 3, 0), pltpu.roll(a, 7, 0))
        return jnp.where(self.y_high, wrapped, a)

    def behind_y(self, v):
        a = pltpu.roll(v, LX, 1)
        wrapped = jnp.where(self.row_first, pltpu.roll(a, 5, 0), pltpu.roll(a, 1, 0))
        return jnp.where(self.y_low, wrapped, a)


def tables_kernel(own_ref, behind_ref, ahead_ref, far_ref, table_ref):
    shifts = Shifts()
    scale = jnp.float32(-1.0 / 6.0)
    behind = behind_ref[...].astype(jnp.float32)
    ahead = ahead_ref[...].astype(jnp.float32)
    far = far_ref[...].astype(jnp.float32)
    own = own_ref[...]

    def entry(source, direction, part, row, col):
        e = direction * 18 + part * 9 + row * 3 + col
        value = source[4 * e : 4 * e + 4] * scale
        return jnp.concatenate([value, value], axis=0)

    planes = ((behind, far, 0), (own, behind, 2), (ahead, own, 2))
    for plane, (here, below, below_direction) in enumerate(planes):
        for direction in range(3):
            for target in range(3):
                for source in range(3):
                    slot = (2 * direction) * 18 + (target * 3 + source) * 2
                    table_ref[plane, slot] = entry(here, direction, 0, target, source)
                    table_ref[plane, slot + 1] = entry(here, direction, 1, target, source)
                    slot = (2 * direction + 1) * 18 + (target * 3 + source) * 2
                    if direction < 2:
                        re = entry(here, direction, 0, source, target)
                        im = entry(here, direction, 1, source, target)
                        move = shifts.behind_x if direction == 0 else shifts.behind_y
                        re, im = move(re), move(im)
                    else:
                        re = entry(below, below_direction, 0, source, target)
                        im = entry(below, below_direction, 1, source, target)
                    table_ref[plane, slot] = re
                    table_ref[plane, slot + 1] = -im


def link_tables(own, behind, ahead, far):
    return pl.pallas_call(
        tables_kernel,
        out_shape=jax.ShapeDtypeStruct((3, 108, 8, LANES), jnp.float32),
        in_specs=[pl.BlockSpec(memory_space=pltpu.VMEM)] * 4,
        out_specs=pl.BlockSpec(memory_space=pltpu.VMEM),
        name="link_tables",
    )(own, behind, ahead, far)


def filter_kernel(own_ref, behind_ref, ahead_ref, far_up_ref, far_down_ref, table_ref, cosine_ref, sine_ref,
                  filtered_ref, shifted_ref, t1_ref, t2_ref):
    shifts = Shifts()
    rows = own_ref.shape[1]

    def hop(plane, here, ahead_z, behind_z):
        count = len(here(0))
        total = [[None] * count for _ in range(6)]
        moves = (shifts.ahead_x, shifts.behind_x, shifts.ahead_y, shifts.behind_y, None, None)
        for direction in range(6):
            if direction < 4:
                field = [[moves[direction](v) for v in here(c)] for c in range(6)]
            else:
                take = ahead_z if direction == 4 else behind_z
                field = [take(c) for c in range(6)]
            for target in range(3):
                for source in range(3):
                    slot = direction * 18 + (target * 3 + source) * 2
                    re = table_ref[plane, slot]
                    im = table_ref[plane, slot + 1]
                    for n in range(count):
                        f_re, f_im = field[source][n], field[3 + source][n]
                        add_re = re * f_re - im * f_im
                        add_im = re * f_im + im * f_re
                        if total[target][n] is None:
                            total[target][n], total[3 + target][n] = add_re, add_im
                        else:
                            total[target][n] = total[target][n] + add_re
                            total[3 + target][n] = total[3 + target][n] + add_im
        return total

    def step(index, carry):
        base = pl.multiple_of(index * 16, 16)

        def reader(ref):
            def read(c):
                value = ref[c, pl.ds(base, 16), :].astype(jnp.float32)
                return [value[0:8], value[8:16]]
            return read

        own, behind, ahead = reader(own_ref), reader(behind_ref), reader(ahead_ref)
        far_up, far_down = reader(far_up_ref), reader(far_down_ref)
        for plane, fields in enumerate(((behind, own, far_down), (own, ahead, behind), (ahead, far_up, own))):
            out = hop(plane, *fields)
            for c in range(6):
                for n in range(2):
                    t1_ref[plane, c, 8 * n : 8 * n + 8] = out[c][n]

        def first(plane):
            return lambda c: [t1_ref[plane, c, 0:8], t1_ref[plane, c, 8:16]]

        out = hop(1, first(1), first(2), first(0))
        for c in range(6):
            start = own(c)
            for n in range(2):
                t2_ref[c, pl.ds(pl.multiple_of(base + 8 * n, 8), 8), :] = 2.0 * out[c][n] - start[n]
        return carry

    lax.fori_loop(0, rows // 16, step, 0)
    vectors = rows // 4
    momenta = cosine_ref.shape[0]
    for color in range(3):
        for row in range(4):
            at = slice((color * 4 + row) * LANES, (color * 4 + row + 1) * LANES)
            re = t2_ref[color, pl.ds(row, vectors, stride=4), :].astype(jnp.bfloat16)
            im = t2_ref[3 + color, pl.ds(row, vectors, stride=4), :].astype(jnp.bfloat16)
            filtered_ref[0, :, at] = re
            filtered_ref[1, :, at] = im
            re, im = re.astype(jnp.float32), im.astype(jnp.float32)
            for p in range(momenta):
                cosine = cosine_ref[p, row : row + 1, :]
                sine = sine_ref[p, row : row + 1, :]
                shifted_ref[p, 0, :, at] = (cosine * re + sine * im).astype(jnp.bfloat16)
                shifted_ref[p, 1, :, at] = (cosine * im - sine * re).astype(jnp.bfloat16)


def filter_chunk(own, chunk, rows, neighbours, table, cosine, sine):
    momenta = cosine.shape[0]
    vectors = rows // 4
    whole = pl.BlockSpec((6, rows, LANES), lambda i: (0, 0, 0))
    return pl.pallas_call(
        filter_kernel,
        grid=(1,),
        out_shape=(
            jax.ShapeDtypeStruct((2, vectors, 12 * LANES), jnp.bfloat16),
            jax.ShapeDtypeStruct((momenta, 2, vectors, 12 * LANES), jnp.bfloat16),
        ),
        in_specs=[pl.BlockSpec((6, rows, LANES), lambda i: (0, chunk, 0))] + [whole] * 4
        + [pl.BlockSpec(table.shape, lambda i: (0, 0, 0, 0)),
           pl.BlockSpec(cosine.shape, lambda i: (0, 0, 0)),
           pl.BlockSpec(sine.shape, lambda i: (0, 0, 0))],
        out_specs=(
            pl.BlockSpec((2, vectors, 12 * LANES), lambda i: (0, 0, 0)),
            pl.BlockSpec((momenta, 2, vectors, 12 * LANES), lambda i: (0, 0, 0, 0)),
        ),
        scratch_shapes=[
            pltpu.VMEM((3, 6, 16, LANES), jnp.float32),
            pltpu.VMEM((6, rows, LANES), jnp.float32),
        ],
        cost_estimate=pl.CostEstimate(
            flops=1728 * 6 * rows * LANES // 6, bytes_accessed=6 * rows * LANES * 16, transcendentals=0),
        name=f"filter_chunk{chunk}",
    )(own, *neighbours, table, cosine, sine)


def elemental_kernel(segments, chunks, place_ref, *refs):
    own = refs[:chunks]
    other = refs[chunks : 2 * chunks]
    shifted = refs[2 * chunks : 3 * chunks]
    outs = refs[3 * chunks : 3 * chunks + segments]
    left_ref, right_ref, total_ref = refs[3 * chunks + segments :]
    size = own[0].shape[1]
    depth = own[0].shape[2]
    block = size * chunks
    for n, ref in enumerate(own + other):
        for part in range(2):
            left_ref[n * size : (n + 1) * size, part * depth : (part + 1) * depth] = ref[part]
    momenta = shifted[0].shape[0]
    for p in range(momenta):
        for n, ref in enumerate(shifted):
            re, im = ref[p, 0], ref[p, 1]
            at = n * size
            right_ref[at : at + size, :depth] = re
            right_ref[at : at + size, depth:] = im
            right_ref[block + at : block + at + size, :depth] = im
            right_ref[block + at : block + at + size, depth:] = -re
        product = lax.dot_general(
            left_ref[...], right_ref[...], (((1,), (1,)), ((), ())), preferred_element_type=jnp.float32)
        rows = product.shape[0] // segments
        for s in range(segments):
            total_ref[s, :, p * 2 * block : (p + 1) * 2 * block] = product[s * rows : (s + 1) * rows]
    place = place_ref[0]
    for d in range(segments):
        s = lax.rem(place + d, segments)
        outs[d][...] = total_ref[s].astype(outs[d].dtype)


def elementals(place, own, other, shifted, segments):
    chunks = len(own)
    _, size, depth = own[0].shape
    momenta = shifted[0].shape[0]
    block = size * chunks
    rows = 2 * block // segments
    columns = momenta * 2 * block
    vmem = pl.BlockSpec(memory_space=pltpu.VMEM)
    return pl.pallas_call(
        functools.partial(elemental_kernel, segments, chunks),
        out_shape=tuple(
            jax.ShapeDtypeStruct((rows, columns), jnp.float32 if d == 0 else jnp.bfloat16) for d in range(segments)),
        in_specs=[pl.BlockSpec(memory_space=pltpu.SMEM)] + [vmem] * (3 * chunks),
        out_specs=tuple(vmem for _ in range(segments)),
        scratch_shapes=[
            pltpu.VMEM((2 * block, 2 * depth), jnp.bfloat16),
            pltpu.VMEM((2 * block, 2 * depth), jnp.bfloat16),
            pltpu.VMEM((segments, rows, columns), jnp.float32),
        ],
        cost_estimate=pl.CostEstimate(
            flops=2 * 2 * block * columns * 2 * depth, bytes_accessed=8 * 2 * block * depth, transcendentals=0),
        name="elementals",
    )(place, *own, *other, *shifted)


def projection_kernel(count, where_ref, tau_ref, *refs):
    pieces = refs[:count]
    out_ref, parts_ref, right_ref = refs[count:]
    momenta, nvec = right_ref.shape[0], right_ref.shape[1] // 2
    block = nvec // 2

    @pl.when(pl.program_id(0) == 0)
    def assemble():
        rows = pieces[0].shape[0]
        for n, piece in enumerate(pieces):
            column, row = where_ref[2 * n], pl.multiple_of(where_ref[2 * n + 1], 32)
            for p in range(momenta):
                parts_ref[column, p, pl.ds(row, rows), :] = piece[:, p * 2 * block : (p + 1) * 2 * block]
        for p in range(momenta):
            low, high = parts_ref[0, p], parts_ref[1, p]
            re = jnp.concatenate([low[:, :block], high[:, :block]], axis=1)
            im = jnp.concatenate([low[:, block:], high[:, block:]], axis=1)
            right_ref[p, :nvec, :nvec] = re
            right_ref[p, :nvec, nvec:] = im
            right_ref[p, nvec:, :nvec] = -im
            right_ref[p, nvec:, nvec:] = re

    left = jnp.concatenate([tau_ref[0, 0], tau_ref[0, 1]], axis=1)
    for p in range(momenta):
        product = jnp.dot(left, right_ref[p], preferred_element_type=jnp.float32)
        out_ref[0, p, 0] = product[:, :nvec].astype(jnp.bfloat16)
        out_ref[0, p, 1] = product[:, nvec:].astype(jnp.bfloat16)


def projection(tau, where, pieces, momenta):
    outer, _, rows, nvec = tau.shape
    count = len(pieces)
    return pl.pallas_call(
        functools.partial(projection_kernel, count),
        grid=(outer,),
        out_shape=jax.ShapeDtypeStruct((outer, momenta, 2, rows, nvec), jnp.bfloat16),
        in_specs=[pl.BlockSpec(memory_space=pltpu.SMEM),
                  pl.BlockSpec((1, 2, rows, nvec), lambda i: (i, 0, 0, 0))]
        + [pl.BlockSpec(memory_space=pltpu.VMEM)] * count,
        out_specs=pl.BlockSpec((1, momenta, 2, rows, nvec), lambda i: (i, 0, 0, 0, 0)),
        scratch_shapes=[
            pltpu.VMEM((2, momenta, nvec, nvec), jnp.bfloat16),
            pltpu.VMEM((momenta, 2 * nvec, 2 * nvec), jnp.bfloat16),
        ],
        cost_estimate=pl.CostEstimate(
            flops=2 * outer * rows * 2 * nvec * 2 * nvec * momenta, bytes_accessed=outer * rows * nvec * 12,
            transcendentals=0),
        name="projection",
    )(where, tau, *pieces)


def from_place(block, up, across):
    sites, groups = lax.axis_size("site"), lax.axis_size("vec")
    route = []
    for z in range(sites):
        for v in range(groups):
            route.append((((z + up) % sites) * groups + (v + across) % groups, z * groups + v))
    return lax.ppermute(block, ("site", "vec"), route)


CHUNKS = 4


def per_device(eigvecs, links, peramb, block_owner, momenta):
    sites, groups = lax.axis_size("site"), lax.axis_size("vec")
    site, group = lax.axis_index("site"), lax.axis_index("vec")
    block = eigvecs.shape[3]
    momentum_count = momenta.shape[0]
    rows = block * 4 // CHUNKS
    own = eigvecs.reshape(6, block * 4, LANES)
    own_links = links.reshape(216, LANES)

    small = own.astype(jnp.bfloat16)
    small_links = own_links.astype(jnp.bfloat16)
    behind_links = from_place(small_links, -1, 0)
    ahead_links = from_place(small_links, 1, 0)
    far_links = from_place(small_links[144:], -2, 0)
    pieces = []
    for chunk in range(CHUNKS):
        piece = small[:, chunk * rows : (chunk + 1) * rows]
        pieces.append([from_place(piece, 1, 0), from_place(piece, -1, 0), from_place(piece, 2, 0)])

    flat = lax.broadcasted_iota(jnp.int32, (4, LANES), 0) * LANES + lax.broadcasted_iota(jnp.int32, (4, LANES), 1)
    theta = phase_angle(momenta, flat % LX, flat // LX, jnp.full_like(flat, site), sites)
    cosine, sine = jnp.cos(theta), jnp.sin(theta)

    table = link_tables(own_links, behind_links, ahead_links, far_links)
    filtered, shifted, received = [], [], []
    for chunk in range(CHUNKS):
        ahead, behind, far = pieces[chunk]
        f, s = filter_chunk(own, chunk, rows, (behind, ahead, far, far), table, cosine, sine)
        filtered.append(f)
        shifted.append(s)
        received.append(from_place(f, 0, 1))

    place = jnp.reshape(site, (1,)).astype(jnp.int32)
    parts = elementals(place, filtered, received, shifted, sites)
    total = parts[0]
    for d in range(1, sites):
        total = total + from_place(parts[d], -d, 0).astype(jnp.float32)
    mine = total.astype(jnp.bfloat16)

    gathered, where = [], []
    half = mine.shape[0]
    for up in range(sites):
        for across in range(groups):
            gathered.append(mine if up == 0 and across == 0 else from_place(mine, up, across))
            z, v = (site + up) % sites, (group + across) % groups
            per = block // half
            where.append(block_owner[v])
            where.append(block_owner[(v + z // per) % groups] * block + (z % per) * half)
    where = jnp.stack(where).astype(jnp.int32)
    sinks, spins = peramb.shape[1], peramb.shape[2]
    tau = peramb.reshape(sinks * spins, 2, block, peramb.shape[5])
    result = projection(tau, where, gathered, momentum_count)
    return result.reshape(1, sinks, spins, momentum_count, 2, block, peramb.shape[5])


def from_behind(block, axis, distance):
    devices = range(lax.axis_size(axis))
    route = [((i - distance) % len(devices), i) for i in devices]
    return lax.ppermute(block, axis, route)


def with_halo(block, sides, width):
    for axis, dim in sides:
        count = lax.axis_size(axis)
        forward = [(i, i + 1) for i in range(count - 1)]
        forward.append((count - 1, 0))
        backward = [(target, source) for source, target in forward]
        low = lax.ppermute(
            lax.slice_in_dim(block, block.shape[dim] - width, None, axis=dim), axis, forward
        )
        high = lax.ppermute(lax.slice_in_dim(block, 0, width, axis=dim), axis, backward)
        block = jnp.concatenate([low, block, high], axis=dim)
    return block


def along(field, direction, sense):
    width = field.shape[-1]
    column = lax.broadcasted_iota(jnp.int32, (width,), 0) % LX
    if direction == 0:
        if sense > 0:
            return jnp.where(column == LX - 1, jnp.roll(field, LX - 1, -1), jnp.roll(field, -1, -1))
        return jnp.where(column == 0, jnp.roll(field, 1 - LX, -1), jnp.roll(field, 1, -1))
    return jnp.roll(field, -sense * LX, -1)


def link_times(link_re, link_im, field_re, field_im, dagger):
    result_re = []
    result_im = []
    for target in range(3):
        summed_re = jnp.zeros_like(field_re[0])
        summed_im = jnp.zeros_like(field_re[0])
        for source in range(3):
            if dagger:
                entry_re = link_re[source, target][None]
                entry_im = -link_im[source, target][None]
            else:
                entry_re = link_re[target, source][None]
                entry_im = link_im[target, source][None]
            summed_re = summed_re + entry_re * field_re[source] - entry_im * field_im[source]
            summed_im = summed_im + entry_re * field_im[source] + entry_im * field_re[source]
        result_re.append(summed_re)
        result_im.append(summed_im)
    return (jnp.stack(result_re), jnp.stack(result_im))


def chebyshev(initial, operate):
    current = operate(initial)
    following = 2.0 * operate(current) - initial
    return following


def general_device(eigvecs, links, peramb, block_owner, momenta):
    vectors = eigvecs[0]
    links_here = links[0]
    block = vectors.shape[2]
    layers = vectors.shape[3]
    plane = vectors.shape[4]
    site_count = lax.axis_size("site")
    group_count = lax.axis_size("vec")
    site_rank = lax.axis_index("site")
    group_rank = lax.axis_index("vec")
    portion = plane // group_count
    top_plane = links_here[2, :, :, :, layers - 1 :, :]
    below = from_behind(top_plane, "site", 1)
    behind_links = jnp.concatenate([below, links_here[2, :, :, :, : layers - 1, :]], axis=3)
    back_links = []
    for direction in range(2):
        back_links.append(
            (
                along(links_here[direction, 0], direction, -1),
                along(links_here[direction, 1], direction, -1),
            )
        )
    back_links.append((behind_links[0], behind_links[1]))

    def operate(field):
        padded = with_halo(field, (("site", 3),), 1)
        total_re = jnp.zeros_like(field[0])
        total_im = jnp.zeros_like(field[0])
        for direction in range(3):
            if direction < 2:
                ahead = along(field, direction, 1)
                behind = along(field, direction, -1)
            else:
                ahead = padded[:, :, :, 2:]
                behind = padded[:, :, :, :-2]
            forward = link_times(
                links_here[direction, 0], links_here[direction, 1], ahead[0], ahead[1], False
            )
            backward = link_times(
                back_links[direction][0], back_links[direction][1], behind[0], behind[1], True
            )
            total_re = total_re + forward[0] + backward[0]
            total_im = total_im + forward[1] + backward[1]
        return jnp.stack([total_re, total_im]) * (-1.0 / 6.0)

    filtered = chebyshev(vectors, operate).astype(jnp.bfloat16)
    received = lax.all_to_all(filtered, "vec", split_axis=4, concat_axis=2, tiled=True)
    grouped = received.reshape(2, 3, group_count, block, layers, portion)
    ranks = jnp.arange(group_count, dtype=jnp.int32)
    inverse = jnp.sum(
        ranks[:, None] * (block_owner[:, None] == ranks[None, :]).astype(jnp.int32), axis=0
    )
    ordered = jnp.take(grouped, inverse, axis=2).reshape(2, 3, group_count * block, layers, portion)
    nvec = group_count * block
    flat = group_rank * portion + lax.broadcasted_iota(jnp.int32, (layers, portion), 1)
    depth = site_rank * layers + lax.broadcasted_iota(jnp.int32, (layers, portion), 0)
    theta = phase_angle(momenta, flat % LX, flat // LX, depth, layers * site_count)
    values = ordered.astype(jnp.float32)
    cosine = jnp.cos(theta)[:, None, None]
    sine = jnp.sin(theta)[:, None, None]
    shift_re = cosine * values[0] + sine * values[1]
    shift_im = cosine * values[1] - sine * values[0]
    shifted = jnp.stack([shift_re, shift_im], axis=1).astype(jnp.bfloat16)
    products = jnp.einsum(
        "acizs,pbckzs->aipbk", ordered, shifted, preferred_element_type=jnp.float32
    )
    real = products[0, :, :, 0] + products[1, :, :, 1]
    imag = products[0, :, :, 1] - products[1, :, :, 0]
    momentum_count = momenta.shape[0]
    partial_sum = jnp.stack([real, imag], axis=2).reshape(nvec, momentum_count * 2 * nvec)
    tau = peramb[0]
    tau_rows = tau.reshape(-1, nvec)
    summed = lax.psum(partial_sum, ("site", "vec")).astype(jnp.bfloat16)
    joined = jnp.dot(tau_rows, summed, preferred_element_type=jnp.float32)
    sinks = tau.shape[0]
    spins = tau.shape[1]
    layout = joined.reshape(sinks, spins, 2, block, momentum_count, 2, nvec)
    real_part = layout[:, :, 0, :, :, 0] - layout[:, :, 1, :, :, 1]
    imag_part = layout[:, :, 0, :, :, 1] + layout[:, :, 1, :, :, 0]
    stacked = jnp.stack([real_part, imag_part], axis=0)
    result = jnp.transpose(stacked, (1, 2, 4, 0, 3, 5))
    return result[None].astype(jnp.bfloat16)


def choose(eigvecs, links, peramb, block_owner, momenta):
    block, layers, plane = eigvecs.shape[3:]
    sites, groups = lax.axis_size("site"), lax.axis_size("vec")
    fits = layers == 1 and plane == LX * LY == 4 * LANES and sites == 4 and groups == 2
    fits = fits and block % (16 * CHUNKS) == 0 and (2 * block) % (32 * sites) == 0 and block % (2 * block // sites) == 0
    device = per_device if fits else general_device
    return device(eigvecs, links, peramb, block_owner, momenta)


def solution(mesh):
    placed = (
        P(("cfg", "tslice"), None, None, "vec", "site", None),
        P(("cfg", "tslice"), None, None, None, None, "site", None),
        P(("cfg", "tslice"), "site", None, None, "vec", None),
        P(),
        P(),
    )
    return jax.shard_map(
        choose,
        mesh=mesh,
        in_specs=placed,
        out_specs=P(("cfg", "tslice"), "site", None, None, None, "vec", None),
        check_vma=False,
    )
```

```python
import functools
import math

import jax
import jax.numpy as jnp
from jax import lax
from jax.experimental import pallas as pl
from jax.experimental.pallas import tpu as pltpu
from jax.sharding import PartitionSpec as P

LX = 32
LY = 16
LANES = 128

two_pi = 2.0 * math.pi


def phase_angle(momenta, across, upward, depth, extent):
    return two_pi * (
        (momenta[:, 0, None, None] * across[None]).astype(jnp.float32) / LX
        + (momenta[:, 1, None, None] * upward[None]).astype(jnp.float32) / LY
        + (momenta[:, 2, None, None] * depth[None]).astype(jnp.float32) / extent
    )


class Shifts:
    def __init__(self):
        lane = lax.broadcasted_iota(jnp.int32, (8, LANES), 1)
        row = lax.broadcasted_iota(jnp.int32, (8, LANES), 0) % 4
        column = lane % LX
        self.x_last = column == LX - 1
        self.x_first = column == 0
        self.y_high = lane >= LANES - LX
        self.y_low = lane < LX
        self.row_last = row == 3
        self.row_first = row == 0

    def ahead_x(self, v):
        return jnp.where(self.x_last, pltpu.roll(v, LX - 1, 1), pltpu.roll(v, LANES - 1, 1))

    def behind_x(self, v):
        return jnp.where(self.x_first, pltpu.roll(v, LANES - LX + 1, 1), pltpu.roll(v, 1, 1))

    def ahead_y(self, v):
        a = pltpu.roll(v, LANES - LX, 1)
        wrapped = jnp.where(self.row_last, pltpu.roll(a, 3, 0), pltpu.roll(a, 7, 0))
        return jnp.where(self.y_high, wrapped, a)

    def behind_y(self, v):
        a = pltpu.roll(v, LX, 1)
        wrapped = jnp.where(self.row_first, pltpu.roll(a, 5, 0), pltpu.roll(a, 1, 0))
        return jnp.where(self.y_low, wrapped, a)


def tables_kernel(*refs):
    table_ref = refs[-1]
    shifts = Shifts()
    scale = jnp.float32(-1.0 / 6.0)
    links = [ref[...].astype(jnp.float32) for ref in refs[:-1]]
    count = len(links)

    def entry(plane, direction, part, row, col):
        e = direction * 18 + part * 9 + row * 3 + col
        value = links[plane % count][4 * e : 4 * e + 4] * scale
        return jnp.concatenate([value, value], axis=0)

    for plane in range(count):
        for direction in range(3):
            for target in range(3):
                for source in range(3):
                    slot = (2 * direction) * 18 + (target * 3 + source) * 2
                    table_ref[plane, slot] = entry(plane, direction, 0, target, source)
                    table_ref[plane, slot + 1] = entry(plane, direction, 1, target, source)
                    slot = (2 * direction + 1) * 18 + (target * 3 + source) * 2
                    below = plane + 1 if direction == 2 else plane
                    re = entry(below, direction, 0, source, target)
                    im = entry(below, direction, 1, source, target)
                    if direction < 2:
                        move = shifts.behind_x if direction == 0 else shifts.behind_y
                        re, im = move(re), move(im)
                    table_ref[plane, slot] = re
                    table_ref[plane, slot + 1] = -im


def link_tables(links):
    return pl.pallas_call(
        tables_kernel,
        out_shape=jax.ShapeDtypeStruct((len(links), 108, 8, LANES), jnp.float32),
        in_specs=[pl.BlockSpec(memory_space=pltpu.VMEM)] * len(links),
        out_specs=pl.BlockSpec(memory_space=pltpu.VMEM),
        name="link_tables",
    )(*links)


def pack_kernel(place_ref, *refs):
    count = len(refs) // 2
    for n in range(count):
        refs[count + n][...] = refs[n][...].astype(jnp.bfloat16)


def pack(own, place, chunk, rows, sites):
    def block_of(d):
        return lambda i, place_ref: (0, lax.rem(place_ref[0] + d, sites) * CHUNKS + chunk, 0)

    return pl.pallas_call(
        pack_kernel,
        grid_spec=pltpu.PrefetchScalarGridSpec(
            num_scalar_prefetch=1,
            grid=(1,),
            in_specs=[pl.BlockSpec((6, rows, LANES), block_of(d)) for d in range(1, sites)],
            out_specs=[pl.BlockSpec((6, rows, LANES), lambda i, place_ref: (0, 0, 0))] * (sites - 1),
        ),
        out_shape=[jax.ShapeDtypeStruct((6, rows, LANES), jnp.bfloat16)] * (sites - 1),
        name=f"pack{chunk}",
    )(place, *([own] * (sites - 1)))


def filter_kernel(sites, place_ref, *refs):
    fields, table_ref = refs[:sites], refs[sites]
    outs, t1_ref = refs[sites + 1 : 2 * sites + 1], refs[2 * sites + 1]
    shifts = Shifts()
    rows = fields[0].shape[1]

    def hop(plane, here, ahead_z, behind_z):
        count = len(here(0))
        total = [[None] * count for _ in range(6)]
        moves = (shifts.ahead_x, shifts.behind_x, shifts.ahead_y, shifts.behind_y, None, None)
        for direction in range(6):
            if direction < 4:
                field = [[moves[direction](v) for v in here(c)] for c in range(6)]
            else:
                take = ahead_z if direction == 4 else behind_z
                field = [take(c) for c in range(6)]
            for target in range(3):
                for source in range(3):
                    slot = direction * 18 + (target * 3 + source) * 2
                    re = table_ref[plane, slot]
                    im = table_ref[plane, slot + 1]
                    for n in range(count):
                        f_re, f_im = field[source][n], field[3 + source][n]
                        add_re = re * f_re - im * f_im
                        add_im = re * f_im + im * f_re
                        if total[target][n] is None:
                            total[target][n], total[3 + target][n] = add_re, add_im
                        else:
                            total[target][n] = total[target][n] + add_re
                            total[3 + target][n] = total[3 + target][n] + add_im
        return total

    def step(index, carry):
        base = pl.multiple_of(index * 16, 16)

        def start(plane):
            def read(c):
                value = fields[plane % sites][c, pl.ds(base, 16), :].astype(jnp.float32)
                return [value[0:8], value[8:16]]
            return read

        def first(plane):
            return lambda c: [t1_ref[plane % sites, c, 0:8], t1_ref[plane % sites, c, 8:16]]

        for plane in range(sites):
            out = hop(plane, start(plane), start(plane - 1), start(plane + 1))
            for c in range(6):
                for n in range(2):
                    t1_ref[plane, c, 8 * n : 8 * n + 8] = out[c][n]
        for plane in range(sites):
            out = hop(plane, first(plane), first(plane - 1), first(plane + 1))
            for c in range(6):
                value = 2.0 * jnp.concatenate(out[c], axis=0)
                outs[plane][c, pl.ds(base, 16), :] = value.astype(jnp.bfloat16)
        return carry

    lax.fori_loop(0, rows // 16, step, 0)


def filter_chunk(own, place, chunk, rows, received, table):
    sites = len(received) + 1
    whole = pl.BlockSpec((6, rows, LANES), lambda i, place_ref: (0, 0, 0))
    return pl.pallas_call(
        functools.partial(filter_kernel, sites),
        grid_spec=pltpu.PrefetchScalarGridSpec(
            num_scalar_prefetch=1,
            grid=(1,),
            in_specs=[pl.BlockSpec((6, rows, LANES), lambda i, place_ref: (0, place_ref[0] * CHUNKS + chunk, 0))]
            + [whole] * (sites - 1)
            + [pl.BlockSpec(table.shape, lambda i, place_ref: (0, 0, 0, 0))],
            out_specs=[whole] * sites,
            scratch_shapes=[pltpu.VMEM((sites, 6, 16, LANES), jnp.float32)],
        ),
        out_shape=[jax.ShapeDtypeStruct((6, rows, LANES), jnp.bfloat16)] * sites,
        cost_estimate=pl.CostEstimate(
            flops=432 * 2 * sites * rows * LANES, bytes_accessed=6 * rows * LANES * 4 * sites, transcendentals=0),
        name=f"filter{chunk}",
    )(place, own, *received, table)


def finish_kernel(sites, place_ref, *refs):
    starts, hops = refs[:sites], refs[sites : 2 * sites]
    cosine_ref, sine_ref, filtered_ref, shifted_ref, work_ref = refs[2 * sites :]
    vectors = starts[0].shape[1] // 4
    momenta = cosine_ref.shape[0]
    for d in range(sites):
        slot = lax.rem(place_ref[0] + d, sites)
        for c in range(6):
            work_ref[d, c] = hops[d][c].astype(jnp.float32) - starts[d][c]
        for color in range(3):
            for row in range(4):
                at = slice((color * 4 + row) * LANES, (color * 4 + row + 1) * LANES)
                re = work_ref[d, color, pl.ds(row, vectors, stride=4), :].astype(jnp.bfloat16)
                im = work_ref[d, 3 + color, pl.ds(row, vectors, stride=4), :].astype(jnp.bfloat16)
                filtered_ref[slot, 0, :, at] = re
                filtered_ref[slot, 1, :, at] = im
                re, im = re.astype(jnp.float32), im.astype(jnp.float32)
                for p in range(momenta):
                    cosine = cosine_ref[p, row : row + 1, :]
                    sine = sine_ref[p, row : row + 1, :]
                    shifted_ref[p, slot, 0, :, at] = (cosine * re + sine * im).astype(jnp.bfloat16)
                    shifted_ref[p, slot, 1, :, at] = (cosine * im - sine * re).astype(jnp.bfloat16)


def finish(own, place, chunk, rows, hops, cosine, sine):
    sites, momenta = len(hops), cosine.shape[0]
    vectors = rows // 4
    whole = pl.BlockSpec((6, rows, LANES), lambda i, place_ref: (0, 0, 0))

    def block_of(d):
        return lambda i, place_ref: (0, lax.rem(place_ref[0] + d, sites) * CHUNKS + chunk, 0)

    shapes = ((sites, 2, vectors, 12 * LANES), (momenta, sites, 2, vectors, 12 * LANES))
    return pl.pallas_call(
        functools.partial(finish_kernel, sites),
        grid_spec=pltpu.PrefetchScalarGridSpec(
            num_scalar_prefetch=1,
            grid=(1,),
            in_specs=[pl.BlockSpec((6, rows, LANES), block_of(d)) for d in range(sites)] + [whole] * sites
            + [pl.BlockSpec(cosine.shape, lambda i, place_ref: (0, 0, 0)),
               pl.BlockSpec(sine.shape, lambda i, place_ref: (0, 0, 0))],
            out_specs=[pl.BlockSpec(shapes[0], lambda i, place_ref: (0, 0, 0, 0)),
                       pl.BlockSpec(shapes[1], lambda i, place_ref: (0, 0, 0, 0, 0))],
            scratch_shapes=[pltpu.VMEM((sites, 6, rows, LANES), jnp.float32)],
        ),
        out_shape=[jax.ShapeDtypeStruct(shape, jnp.bfloat16) for shape in shapes],
        cost_estimate=pl.CostEstimate(
            flops=20 * sites * 6 * rows * LANES, bytes_accessed=sites * 6 * rows * LANES * 12, transcendentals=0),
        name=f"finish{chunk}",
    )(place, *([own] * sites), *hops, cosine, sine)


def elemental_kernel(segments, chunks, place_ref, *refs):
    own = refs[:chunks]
    other = refs[chunks : 2 * chunks]
    shifted = refs[2 * chunks : 3 * chunks]
    outs = refs[3 * chunks : 3 * chunks + segments]
    left_ref, right_ref, total_ref = refs[3 * chunks + segments :]
    slots, _, size, depth = own[0].shape
    block = slots * size * chunks
    for n, ref in enumerate(own + other):
        for slot in range(slots):
            at = n // chunks * block + (slot * chunks + n % chunks) * size
            for part in range(2):
                left_ref[at : at + size, part * depth : (part + 1) * depth] = ref[slot, part]
    momenta = shifted[0].shape[0]
    for p in range(momenta):
        for n, ref in enumerate(shifted):
            for slot in range(slots):
                re, im = ref[p, slot, 0], ref[p, slot, 1]
                at = (slot * chunks + n) * size
                right_ref[at : at + size, :depth] = re
                right_ref[at : at + size, depth:] = im
                right_ref[block + at : block + at + size, :depth] = im
                right_ref[block + at : block + at + size, depth:] = -re
        product = lax.dot_general(
            left_ref[...], right_ref[...], (((1,), (1,)), ((), ())), preferred_element_type=jnp.float32)
        rows = product.shape[0] // segments
        for s in range(segments):
            total_ref[s, :, p * 2 * block : (p + 1) * 2 * block] = product[s * rows : (s + 1) * rows]
    place = place_ref[0]
    for d in range(segments):
        s = lax.rem(place + d, segments)
        outs[d][...] = total_ref[s].astype(outs[d].dtype)


def elementals(place, own, other, shifted, segments):
    chunks = len(own)
    slots, _, size, depth = own[0].shape
    momenta = shifted[0].shape[0]
    block = slots * size * chunks
    rows = 2 * block // segments
    columns = momenta * 2 * block
    vmem = pl.BlockSpec(memory_space=pltpu.VMEM)
    return pl.pallas_call(
        functools.partial(elemental_kernel, segments, chunks),
        out_shape=tuple(
            jax.ShapeDtypeStruct((rows, columns), jnp.float32 if d == 0 else jnp.bfloat16) for d in range(segments)),
        in_specs=[pl.BlockSpec(memory_space=pltpu.SMEM)] + [vmem] * (3 * chunks),
        out_specs=tuple(vmem for _ in range(segments)),
        scratch_shapes=[
            pltpu.VMEM((2 * block, 2 * depth), jnp.bfloat16),
            pltpu.VMEM((2 * block, 2 * depth), jnp.bfloat16),
            pltpu.VMEM((segments, rows, columns), jnp.float32),
        ],
        cost_estimate=pl.CostEstimate(
            flops=2 * 2 * block * columns * 2 * depth, bytes_accessed=8 * 2 * block * depth, transcendentals=0),
        name="elementals",
    )(place, *own, *other, *shifted)


def projection_kernel(sites, groups, place_ref, owner_ref, tau_ref, *refs):
    pieces = refs[: sites * groups]
    out_ref, parts_ref, right_ref = refs[sites * groups :]
    momenta, nvec = right_ref.shape[0], right_ref.shape[1] // 2
    block = nvec // 2

    @pl.when(pl.program_id(0) == 0)
    def assemble():
        rows = pieces[0].shape[0]
        for n, piece in enumerate(pieces):
            up, across = n // groups, n % groups
            z, v = lax.rem(place_ref[0] + up, sites), lax.rem(place_ref[1] + across, groups)
            per = block // rows
            column = owner_ref[v]
            row = owner_ref[lax.rem(v + lax.div(z, per), groups)] * block + lax.rem(z, per) * rows
            row = pl.multiple_of(row, 32)
            for p in range(momenta):
                parts_ref[column, p, pl.ds(row, rows), :] = piece[:, p * 2 * block : (p + 1) * 2 * block]
        for p in range(momenta):
            low, high = parts_ref[0, p], parts_ref[1, p]
            re = jnp.concatenate([low[:, :block], high[:, :block]], axis=1)
            im = jnp.concatenate([low[:, block:], high[:, block:]], axis=1)
            right_ref[p, :nvec, :nvec] = re
            right_ref[p, :nvec, nvec:] = im
            right_ref[p, nvec:, :nvec] = -im
            right_ref[p, nvec:, nvec:] = re

    left = jnp.concatenate([tau_ref[0, 0], tau_ref[0, 1]], axis=1)
    for p in range(momenta):
        product = jnp.dot(left, right_ref[p], preferred_element_type=jnp.float32)
        out_ref[0, p, 0] = product[:, :nvec].astype(jnp.bfloat16)
        out_ref[0, p, 1] = product[:, nvec:].astype(jnp.bfloat16)


def projection(tau, place, owner, pieces, momenta, sites, groups):
    outer, _, rows, nvec = tau.shape
    count = len(pieces)
    return pl.pallas_call(
        functools.partial(projection_kernel, sites, groups),
        grid=(outer,),
        out_shape=jax.ShapeDtypeStruct((outer, momenta, 2, rows, nvec), jnp.bfloat16),
        in_specs=[pl.BlockSpec(memory_space=pltpu.SMEM), pl.BlockSpec(memory_space=pltpu.SMEM),
                  pl.BlockSpec((1, 2, rows, nvec), lambda i: (i, 0, 0, 0))]
        + [pl.BlockSpec(memory_space=pltpu.VMEM)] * count,
        out_specs=pl.BlockSpec((1, momenta, 2, rows, nvec), lambda i: (i, 0, 0, 0, 0)),
        scratch_shapes=[
            pltpu.VMEM((2, momenta, nvec, nvec), jnp.bfloat16),
            pltpu.VMEM((momenta, 2 * nvec, 2 * nvec), jnp.bfloat16),
        ],
        cost_estimate=pl.CostEstimate(
            flops=2 * outer * rows * 2 * nvec * 2 * nvec * momenta, bytes_accessed=outer * rows * nvec * 12,
            transcendentals=0),
        name="projection",
    )(place, owner, tau, *pieces)


def from_place(block, up, across):
    sites, groups = lax.axis_size("site"), lax.axis_size("vec")
    route = []
    for z in range(sites):
        for v in range(groups):
            route.append((((z + up) % sites) * groups + (v + across) % groups, z * groups + v))
    return lax.ppermute(block, ("site", "vec"), route)


CHUNKS = 3


def per_device(eigvecs, links, peramb, block_owner, momenta):
    sites, groups = lax.axis_size("site"), lax.axis_size("vec")
    site, group = lax.axis_index("site"), lax.axis_index("vec")
    block = eigvecs.shape[3]
    rows = block * 4 // (sites * CHUNKS)
    own = eigvecs.reshape(6, block * 4, LANES)
    own_links = links.reshape(216, LANES)
    place = jnp.stack([site, group]).astype(jnp.int32)

    small_links = own_links.astype(jnp.bfloat16)
    links_by_plane = [own_links] + [from_place(small_links, -d, 0) for d in range(1, sites)]
    received = []
    for chunk in range(CHUNKS):
        packed = pack(own, place, chunk, rows, sites)
        received.append([from_place(packed[d - 1], -d, 0) for d in range(1, sites)])

    flat = lax.broadcasted_iota(jnp.int32, (4, LANES), 0) * LANES + lax.broadcasted_iota(jnp.int32, (4, LANES), 1)
    theta = phase_angle(momenta, flat % LX, flat // LX, jnp.full_like(flat, site), sites)
    cosine, sine = jnp.cos(theta), jnp.sin(theta)

    table = link_tables(links_by_plane)
    filtered, shifted, other = [], [], []
    for chunk in range(CHUNKS):
        hops = filter_chunk(own, place, chunk, rows, received[chunk], table)
        hops = [hops[0]] + [from_place(hops[d], d, 0) for d in range(1, sites)]
        f, s = finish(own, place, chunk, rows, hops, cosine, sine)
        filtered.append(f)
        shifted.append(s)
        other.append(from_place(f, 0, 1))

    parts = elementals(place, filtered, other, shifted, sites)
    total = parts[0]
    for d in range(1, sites):
        total = total + from_place(parts[d], -d, 0).astype(jnp.float32)
    mine = total.astype(jnp.bfloat16)

    gathered = []
    for up in range(sites):
        for across in range(groups):
            gathered.append(mine if up == 0 and across == 0 else from_place(mine, up, across))
    sinks, spins = peramb.shape[1], peramb.shape[2]
    tau = peramb.reshape(sinks * spins, 2, block, peramb.shape[5])
    result = projection(tau, place, block_owner, gathered, momenta.shape[0], sites, groups)
    return result.reshape(1, sinks, spins, momenta.shape[0], 2, block, peramb.shape[5])


def from_behind(block, axis, distance):
    devices = range(lax.axis_size(axis))
    route = [((i - distance) % len(devices), i) for i in devices]
    return lax.ppermute(block, axis, route)


def with_halo(block, sides, width):
    for axis, dim in sides:
        count = lax.axis_size(axis)
        forward = [(i, i + 1) for i in range(count - 1)]
        forward.append((count - 1, 0))
        backward = [(target, source) for source, target in forward]
        low = lax.ppermute(
            lax.slice_in_dim(block, block.shape[dim] - width, None, axis=dim), axis, forward
        )
        high = lax.ppermute(lax.slice_in_dim(block, 0, width, axis=dim), axis, backward)
        block = jnp.concatenate([low, block, high], axis=dim)
    return block


def along(field, direction, sense):
    width = field.shape[-1]
    column = lax.broadcasted_iota(jnp.int32, (width,), 0) % LX
    if direction == 0:
        if sense > 0:
            return jnp.where(column == LX - 1, jnp.roll(field, LX - 1, -1), jnp.roll(field, -1, -1))
        return jnp.where(column == 0, jnp.roll(field, 1 - LX, -1), jnp.roll(field, 1, -1))
    return jnp.roll(field, -sense * LX, -1)


def link_times(link_re, link_im, field_re, field_im, dagger):
    result_re = []
    result_im = []
    for target in range(3):
        summed_re = jnp.zeros_like(field_re[0])
        summed_im = jnp.zeros_like(field_re[0])
        for source in range(3):
            if dagger:
                entry_re = link_re[source, target][None]
                entry_im = -link_im[source, target][None]
            else:
                entry_re = link_re[target, source][None]
                entry_im = link_im[target, source][None]
            summed_re = summed_re + entry_re * field_re[source] - entry_im * field_im[source]
            summed_im = summed_im + entry_re * field_im[source] + entry_im * field_re[source]
        result_re.append(summed_re)
        result_im.append(summed_im)
    return (jnp.stack(result_re), jnp.stack(result_im))


def chebyshev(initial, operate):
    current = operate(initial)
    following = 2.0 * operate(current) - initial
    return following


def general_device(eigvecs, links, peramb, block_owner, momenta):
    vectors = eigvecs[0]
    links_here = links[0]
    block = vectors.shape[2]
    layers = vectors.shape[3]
    plane = vectors.shape[4]
    site_count = lax.axis_size("site")
    group_count = lax.axis_size("vec")
    site_rank = lax.axis_index("site")
    group_rank = lax.axis_index("vec")
    portion = plane // group_count
    top_plane = links_here[2, :, :, :, layers - 1 :, :]
    below = from_behind(top_plane, "site", 1)
    behind_links = jnp.concatenate([below, links_here[2, :, :, :, : layers - 1, :]], axis=3)
    back_links = []
    for direction in range(2):
        back_links.append(
            (
                along(links_here[direction, 0], direction, -1),
                along(links_here[direction, 1], direction, -1),
            )
        )
    back_links.append((behind_links[0], behind_links[1]))

    def operate(field):
        padded = with_halo(field, (("site", 3),), 1)
        total_re = jnp.zeros_like(field[0])
        total_im = jnp.zeros_like(field[0])
        for direction in range(3):
            if direction < 2:
                ahead = along(field, direction, 1)
                behind = along(field, direction, -1)
            else:
                ahead = padded[:, :, :, 2:]
                behind = padded[:, :, :, :-2]
            forward = link_times(
                links_here[direction, 0], links_here[direction, 1], ahead[0], ahead[1], False
            )
            backward = link_times(
                back_links[direction][0], back_links[direction][1], behind[0], behind[1], True
            )
            total_re = total_re + forward[0] + backward[0]
            total_im = total_im + forward[1] + backward[1]
        return jnp.stack([total_re, total_im]) * (-1.0 / 6.0)

    filtered = chebyshev(vectors, operate).astype(jnp.bfloat16)
    received = lax.all_to_all(filtered, "vec", split_axis=4, concat_axis=2, tiled=True)
    grouped = received.reshape(2, 3, group_count, block, layers, portion)
    ranks = jnp.arange(group_count, dtype=jnp.int32)
    inverse = jnp.sum(
        ranks[:, None] * (block_owner[:, None] == ranks[None, :]).astype(jnp.int32), axis=0
    )
    ordered = jnp.take(grouped, inverse, axis=2).reshape(2, 3, group_count * block, layers, portion)
    nvec = group_count * block
    flat = group_rank * portion + lax.broadcasted_iota(jnp.int32, (layers, portion), 1)
    depth = site_rank * layers + lax.broadcasted_iota(jnp.int32, (layers, portion), 0)
    theta = phase_angle(momenta, flat % LX, flat // LX, depth, layers * site_count)
    values = ordered.astype(jnp.float32)
    cosine = jnp.cos(theta)[:, None, None]
    sine = jnp.sin(theta)[:, None, None]
    shift_re = cosine * values[0] + sine * values[1]
    shift_im = cosine * values[1] - sine * values[0]
    shifted = jnp.stack([shift_re, shift_im], axis=1).astype(jnp.bfloat16)
    products = jnp.einsum(
        "acizs,pbckzs->aipbk", ordered, shifted, preferred_element_type=jnp.float32
    )
    real = products[0, :, :, 0] + products[1, :, :, 1]
    imag = products[0, :, :, 1] - products[1, :, :, 0]
    momentum_count = momenta.shape[0]
    partial_sum = jnp.stack([real, imag], axis=2).reshape(nvec, momentum_count * 2 * nvec)
    tau = peramb[0]
    tau_rows = tau.reshape(-1, nvec)
    summed = lax.psum(partial_sum, ("site", "vec")).astype(jnp.bfloat16)
    joined = jnp.dot(tau_rows, summed, preferred_element_type=jnp.float32)
    sinks = tau.shape[0]
    spins = tau.shape[1]
    layout = joined.reshape(sinks, spins, 2, block, momentum_count, 2, nvec)
    real_part = layout[:, :, 0, :, :, 0] - layout[:, :, 1, :, :, 1]
    imag_part = layout[:, :, 0, :, :, 1] + layout[:, :, 1, :, :, 0]
    stacked = jnp.stack([real_part, imag_part], axis=0)
    result = jnp.transpose(stacked, (1, 2, 4, 0, 3, 5))
    return result[None].astype(jnp.bfloat16)


def choose(eigvecs, links, peramb, block_owner, momenta):
    block, layers, plane = eigvecs.shape[3:]
    sites, groups = lax.axis_size("site"), lax.axis_size("vec")
    fits = layers == 1 and plane == LX * LY == 4 * LANES and sites == 4 and groups == 2
    fits = fits and block % (4 * sites * CHUNKS) == 0 and block // (sites * CHUNKS) % 8 == 0 and (2 * block) % (32 * sites) == 0 and block % (2 * block // sites) == 0
    device = per_device if fits else general_device
    return device(eigvecs, links, peramb, block_owner, momenta)


def solution(mesh):
    placed = (
        P(("cfg", "tslice"), None, None, "vec", "site", None),
        P(("cfg", "tslice"), None, None, None, None, "site", None),
        P(("cfg", "tslice"), "site", None, None, "vec", None),
        P(),
        P(),
    )
    return jax.shard_map(
        choose,
        mesh=mesh,
        in_specs=placed,
        out_specs=P(("cfg", "tslice"), "site", None, None, None, "vec", None),
        check_vma=False,
    )
```

```python
import functools
import math

import jax
import jax.numpy as jnp
from jax import lax
from jax.experimental import pallas as pl
from jax.experimental.pallas import tpu as pltpu
from jax.sharding import PartitionSpec as P

LX = 32
LY = 16
LANES = 128

two_pi = 2.0 * math.pi


def phase_angle(momenta, across, upward, depth, extent):
    return two_pi * (
        (momenta[:, 0, None, None] * across[None]).astype(jnp.float32) / LX
        + (momenta[:, 1, None, None] * upward[None]).astype(jnp.float32) / LY
        + (momenta[:, 2, None, None] * depth[None]).astype(jnp.float32) / extent
    )


class Shifts:
    def __init__(self):
        lane = lax.broadcasted_iota(jnp.int32, (8, LANES), 1)
        row = lax.broadcasted_iota(jnp.int32, (8, LANES), 0) % 4
        column = lane % LX
        self.x_last = column == LX - 1
        self.x_first = column == 0
        self.y_high = lane >= LANES - LX
        self.y_low = lane < LX
        self.row_last = row == 3
        self.row_first = row == 0

    def ahead_x(self, v):
        return jnp.where(self.x_last, pltpu.roll(v, LX - 1, 1), pltpu.roll(v, LANES - 1, 1))

    def behind_x(self, v):
        return jnp.where(self.x_first, pltpu.roll(v, LANES - LX + 1, 1), pltpu.roll(v, 1, 1))

    def ahead_y(self, v):
        a = pltpu.roll(v, LANES - LX, 1)
        wrapped = jnp.where(self.row_last, pltpu.roll(a, 3, 0), pltpu.roll(a, 7, 0))
        return jnp.where(self.y_high, wrapped, a)

    def behind_y(self, v):
        a = pltpu.roll(v, LX, 1)
        wrapped = jnp.where(self.row_first, pltpu.roll(a, 5, 0), pltpu.roll(a, 1, 0))
        return jnp.where(self.y_low, wrapped, a)


def tables_kernel(*refs):
    table_ref = refs[-1]
    shifts = Shifts()
    scale = jnp.float32(-1.0 / 6.0)
    size = refs[0].shape[0]
    links = [ref[ref.shape[0] - size :].astype(jnp.float32) for ref in refs[:-1]]
    count = len(links)

    def entry(plane, direction, part, row, col):
        e = direction * 18 + part * 9 + row * 3 + col
        value = links[plane % count][4 * e : 4 * e + 4] * scale
        return jnp.concatenate([value, value], axis=0)

    for plane in range(count):
        for direction in range(3):
            for target in range(3):
                for source in range(3):
                    slot = (2 * direction) * 18 + (target * 3 + source) * 2
                    table_ref[plane, slot] = entry(plane, direction, 0, target, source)
                    table_ref[plane, slot + 1] = entry(plane, direction, 1, target, source)
                    slot = (2 * direction + 1) * 18 + (target * 3 + source) * 2
                    below = plane + 1 if direction == 2 else plane
                    re = entry(below, direction, 0, source, target)
                    im = entry(below, direction, 1, source, target)
                    if direction < 2:
                        move = shifts.behind_x if direction == 0 else shifts.behind_y
                        re, im = move(re), move(im)
                    table_ref[plane, slot] = re
                    table_ref[plane, slot + 1] = -im


def link_tables(links):
    return pl.pallas_call(
        tables_kernel,
        out_shape=jax.ShapeDtypeStruct((len(links), 108, 8, LANES), jnp.float32),
        in_specs=[pl.BlockSpec(memory_space=pltpu.VMEM)] * len(links),
        out_specs=pl.BlockSpec(memory_space=pltpu.VMEM),
        name="link_tables",
    )(*links)


def pack_kernel(count, place_ref, *refs):
    blocks, extra, outs = refs[:count], refs[count:-count], refs[-count:]
    rows = blocks[0].shape[1]
    for n in range(count):
        for c in range(6):
            outs[n][c * rows : (c + 1) * rows] = blocks[n][c].astype(jnp.bfloat16)
        if outs[n].shape[0] > 6 * rows:
            outs[n][6 * rows :] = extra[0][...].astype(jnp.bfloat16)


def pack(own, place, chunk, rows, sites, links, after):
    def block_of(d):
        return lambda i, place_ref: (0, lax.rem(place_ref[0] + d, sites) * CHUNKS + chunk, 0)

    extra = [links] if chunk == 0 else []
    length = 6 * rows + sum(e.shape[0] for e in extra)
    return pl.pallas_call(
        functools.partial(pack_kernel, sites - 1),
        grid_spec=pltpu.PrefetchScalarGridSpec(
            num_scalar_prefetch=1,
            grid=(1,),
            in_specs=[pl.BlockSpec((6, rows, LANES), block_of(d)) for d in range(1, sites)]
            + [pl.BlockSpec(e.shape, lambda i, place_ref: (0, 0)) for e in extra]
            + [pl.BlockSpec(memory_space=pl.ANY)] * len(after),
            out_specs=[pl.BlockSpec((length, LANES), lambda i, place_ref: (0, 0))] * (sites - 1),
        ),
        out_shape=[jax.ShapeDtypeStruct((length, LANES), jnp.bfloat16)] * (sites - 1),
        name=f"pack{chunk}",
    )(place, *([own] * (sites - 1)), *extra, *after)


def filter_kernel(sites, place_ref, *refs):
    fields, table_ref = refs[:sites], refs[sites]
    outs, t1_ref = refs[-1 - sites : -1], refs[-1]
    shifts = Shifts()
    rows = fields[0].shape[1]

    def hop(plane, here, ahead_z, behind_z):
        count = len(here(0))
        total = [[None] * count for _ in range(6)]
        moves = (shifts.ahead_x, shifts.behind_x, shifts.ahead_y, shifts.behind_y, None, None)
        for direction in range(6):
            if direction < 4:
                field = [[moves[direction](v) for v in here(c)] for c in range(6)]
            else:
                take = ahead_z if direction == 4 else behind_z
                field = [take(c) for c in range(6)]
            for target in range(3):
                for source in range(3):
                    slot = direction * 18 + (target * 3 + source) * 2
                    re = table_ref[plane, slot]
                    im = table_ref[plane, slot + 1]
                    for n in range(count):
                        f_re, f_im = field[source][n], field[3 + source][n]
                        add_re = re * f_re - im * f_im
                        add_im = re * f_im + im * f_re
                        if total[target][n] is None:
                            total[target][n], total[3 + target][n] = add_re, add_im
                        else:
                            total[target][n] = total[target][n] + add_re
                            total[3 + target][n] = total[3 + target][n] + add_im
        return total

    def step(index, carry):
        base = pl.multiple_of(index * 16, 16)

        def start(plane):
            def read(c):
                ref = fields[plane % sites]
                if plane % sites == 0:
                    value = ref[c, pl.ds(base, 16), :]
                else:
                    value = ref[pl.ds(pl.multiple_of(c * rows + base, 16), 16), :].astype(jnp.float32)
                return [value[0:8], value[8:16]]
            return read

        def first(plane):
            return lambda c: [t1_ref[plane % sites, c, 0:8], t1_ref[plane % sites, c, 8:16]]

        for plane in range(sites):
            out = hop(plane, start(plane), start(plane - 1), start(plane + 1))
            for c in range(6):
                for n in range(2):
                    t1_ref[plane, c, 8 * n : 8 * n + 8] = out[c][n]
        for plane in range(sites):
            out = hop(plane, first(plane), first(plane - 1), first(plane + 1))
            for c in range(6):
                value = 2.0 * jnp.concatenate(out[c], axis=0)
                outs[plane][c, pl.ds(base, 16), :] = value.astype(jnp.bfloat16)
        return carry

    lax.fori_loop(0, rows // 16, step, 0)


def filter_chunk(own, place, chunk, rows, received, table, after):
    sites = len(received) + 1
    whole = pl.BlockSpec((6, rows, LANES), lambda i, place_ref: (0, 0, 0))
    return pl.pallas_call(
        functools.partial(filter_kernel, sites),
        grid_spec=pltpu.PrefetchScalarGridSpec(
            num_scalar_prefetch=1,
            grid=(1,),
            in_specs=[pl.BlockSpec((6, rows, LANES), lambda i, place_ref: (0, place_ref[0] * CHUNKS + chunk, 0))]
            + [pl.BlockSpec(r.shape, lambda i, place_ref: (0, 0)) for r in received]
            + [pl.BlockSpec(table.shape, lambda i, place_ref: (0, 0, 0, 0))]
            + [pl.BlockSpec(memory_space=pl.ANY)] * len(after),
            out_specs=[whole] * sites,
            scratch_shapes=[pltpu.VMEM((sites, 6, 16, LANES), jnp.float32)],
        ),
        out_shape=[jax.ShapeDtypeStruct((6, rows, LANES), jnp.bfloat16)] * sites,
        cost_estimate=pl.CostEstimate(
            flops=432 * 2 * sites * rows * LANES, bytes_accessed=6 * rows * LANES * 4 * sites, transcendentals=0),
        name=f"filter{chunk}",
    )(place, own, *received, table, *after)


def finish_kernel(sites, place_ref, *refs):
    starts, hops = refs[:sites], refs[sites : 2 * sites]
    cosine_ref, sine_ref = refs[2 * sites : 2 * sites + 2]
    filtered_ref, shifted_ref, work_ref = refs[-3:]
    vectors = starts[0].shape[1] // 4
    momenta = cosine_ref.shape[0]
    for d in range(sites):
        slot = lax.rem(place_ref[0] + d, sites)
        for c in range(6):
            work_ref[d, c] = hops[d][c].astype(jnp.float32) - starts[d][c]
        for color in range(3):
            for row in range(4):
                at = slice((color * 4 + row) * LANES, (color * 4 + row + 1) * LANES)
                re = work_ref[d, color, pl.ds(row, vectors, stride=4), :].astype(jnp.bfloat16)
                im = work_ref[d, 3 + color, pl.ds(row, vectors, stride=4), :].astype(jnp.bfloat16)
                filtered_ref[slot, 0, :, at] = re
                filtered_ref[slot, 1, :, at] = im
                re, im = re.astype(jnp.float32), im.astype(jnp.float32)
                for p in range(momenta):
                    cosine = cosine_ref[p, row : row + 1, :]
                    sine = sine_ref[p, row : row + 1, :]
                    shifted_ref[p, slot, 0, :, at] = (cosine * re + sine * im).astype(jnp.bfloat16)
                    shifted_ref[p, slot, 1, :, at] = (cosine * im - sine * re).astype(jnp.bfloat16)


def finish(own, place, chunk, rows, hops, cosine, sine, after):
    sites, momenta = len(hops), cosine.shape[0]
    vectors = rows // 4
    whole = pl.BlockSpec((6, rows, LANES), lambda i, place_ref: (0, 0, 0))

    def block_of(d):
        return lambda i, place_ref: (0, lax.rem(place_ref[0] + d, sites) * CHUNKS + chunk, 0)

    shapes = ((sites, 2, vectors, 12 * LANES), (momenta, sites, 2, vectors, 12 * LANES))
    return pl.pallas_call(
        functools.partial(finish_kernel, sites),
        grid_spec=pltpu.PrefetchScalarGridSpec(
            num_scalar_prefetch=1,
            grid=(1,),
            in_specs=[pl.BlockSpec((6, rows, LANES), block_of(d)) for d in range(sites)] + [whole] * sites
            + [pl.BlockSpec(cosine.shape, lambda i, place_ref: (0, 0, 0)),
               pl.BlockSpec(sine.shape, lambda i, place_ref: (0, 0, 0))]
            + [pl.BlockSpec(memory_space=pl.ANY)] * len(after),
            out_specs=[pl.BlockSpec(shapes[0], lambda i, place_ref: (0, 0, 0, 0)),
                       pl.BlockSpec(shapes[1], lambda i, place_ref: (0, 0, 0, 0, 0))],
            scratch_shapes=[pltpu.VMEM((sites, 6, rows, LANES), jnp.float32)],
        ),
        out_shape=[jax.ShapeDtypeStruct(shape, jnp.bfloat16) for shape in shapes],
        cost_estimate=pl.CostEstimate(
            flops=20 * sites * 6 * rows * LANES, bytes_accessed=sites * 6 * rows * LANES * 12, transcendentals=0),
        name=f"finish{chunk}",
    )(place, *([own] * sites), *hops, cosine, sine, *after)


def elemental_kernel(segments, chunks, place_ref, *refs):
    own = refs[:chunks]
    other = refs[chunks : 2 * chunks]
    shifted = refs[2 * chunks : 3 * chunks]
    outs = refs[3 * chunks : 3 * chunks + segments]
    left_ref, right_ref, total_ref = refs[3 * chunks + segments :]
    slots, _, size, depth = own[0].shape
    block = slots * size * chunks
    for n, ref in enumerate(own + other):
        for slot in range(slots):
            at = n // chunks * block + (slot * chunks + n % chunks) * size
            for part in range(2):
                left_ref[at : at + size, part * depth : (part + 1) * depth] = ref[slot, part]
    momenta = shifted[0].shape[0]
    for p in range(momenta):
        for n, ref in enumerate(shifted):
            for slot in range(slots):
                re, im = ref[p, slot, 0], ref[p, slot, 1]
                at = (slot * chunks + n) * size
                right_ref[at : at + size, :depth] = re
                right_ref[at : at + size, depth:] = im
                right_ref[block + at : block + at + size, :depth] = im
                right_ref[block + at : block + at + size, depth:] = -re
        product = lax.dot_general(
            left_ref[...], right_ref[...], (((1,), (1,)), ((), ())), preferred_element_type=jnp.float32)
        rows = product.shape[0] // segments
        for s in range(segments):
            total_ref[s, :, p * 2 * block : (p + 1) * 2 * block] = product[s * rows : (s + 1) * rows]
    place = place_ref[0]
    for d in range(segments):
        s = lax.rem(place + d, segments)
        outs[d][...] = total_ref[s].astype(outs[d].dtype)


def elementals(place, own, other, shifted, segments):
    chunks = len(own)
    slots, _, size, depth = own[0].shape
    momenta = shifted[0].shape[0]
    block = slots * size * chunks
    rows = 2 * block // segments
    columns = momenta * 2 * block
    vmem = pl.BlockSpec(memory_space=pltpu.VMEM)
    return pl.pallas_call(
        functools.partial(elemental_kernel, segments, chunks),
        out_shape=tuple(
            jax.ShapeDtypeStruct((rows, columns), jnp.float32 if d == 0 else jnp.bfloat16) for d in range(segments)),
        in_specs=[pl.BlockSpec(memory_space=pltpu.SMEM)] + [vmem] * (3 * chunks),
        out_specs=tuple(vmem for _ in range(segments)),
        scratch_shapes=[
            pltpu.VMEM((2 * block, 2 * depth), jnp.bfloat16),
            pltpu.VMEM((2 * block, 2 * depth), jnp.bfloat16),
            pltpu.VMEM((segments, rows, columns), jnp.float32),
        ],
        cost_estimate=pl.CostEstimate(
            flops=2 * 2 * block * columns * 2 * depth, bytes_accessed=8 * 2 * block * depth, transcendentals=0),
        name="elementals",
    )(place, *own, *other, *shifted)


def projection_kernel(sites, groups, place_ref, owner_ref, tau_ref, *refs):
    pieces = refs[: sites * groups]
    out_ref, parts_ref, right_ref = refs[sites * groups :]
    momenta, nvec = right_ref.shape[0], right_ref.shape[1] // 2
    block = nvec // 2

    @pl.when(pl.program_id(0) == 0)
    def assemble():
        rows = pieces[0].shape[0]
        for n, piece in enumerate(pieces):
            up, across = n // groups, n % groups
            z, v = lax.rem(place_ref[0] + up, sites), lax.rem(place_ref[1] + across, groups)
            per = block // rows
            column = owner_ref[v]
            row = owner_ref[lax.rem(v + lax.div(z, per), groups)] * block + lax.rem(z, per) * rows
            row = pl.multiple_of(row, 32)
            for p in range(momenta):
                parts_ref[column, p, pl.ds(row, rows), :] = piece[:, p * 2 * block : (p + 1) * 2 * block]
        for p in range(momenta):
            low, high = parts_ref[0, p], parts_ref[1, p]
            re = jnp.concatenate([low[:, :block], high[:, :block]], axis=1)
            im = jnp.concatenate([low[:, block:], high[:, block:]], axis=1)
            right_ref[p, :nvec, :nvec] = re
            right_ref[p, :nvec, nvec:] = im
            right_ref[p, nvec:, :nvec] = -im
            right_ref[p, nvec:, nvec:] = re

    left = jnp.concatenate([tau_ref[0, 0], tau_ref[0, 1]], axis=1)
    for p in range(momenta):
        product = jnp.dot(left, right_ref[p], preferred_element_type=jnp.float32)
        out_ref[0, p, 0] = product[:, :nvec].astype(jnp.bfloat16)
        out_ref[0, p, 1] = product[:, nvec:].astype(jnp.bfloat16)


def projection(tau, place, owner, pieces, momenta, sites, groups):
    outer, _, rows, nvec = tau.shape
    count = len(pieces)
    return pl.pallas_call(
        functools.partial(projection_kernel, sites, groups),
        grid=(outer,),
        out_shape=jax.ShapeDtypeStruct((outer, momenta, 2, rows, nvec), jnp.bfloat16),
        in_specs=[pl.BlockSpec(memory_space=pltpu.SMEM), pl.BlockSpec(memory_space=pltpu.SMEM),
                  pl.BlockSpec((1, 2, rows, nvec), lambda i: (i, 0, 0, 0))]
        + [pl.BlockSpec(memory_space=pltpu.VMEM)] * count,
        out_specs=pl.BlockSpec((1, momenta, 2, rows, nvec), lambda i: (i, 0, 0, 0, 0)),
        scratch_shapes=[
            pltpu.VMEM((2, momenta, nvec, nvec), jnp.bfloat16),
            pltpu.VMEM((momenta, 2 * nvec, 2 * nvec), jnp.bfloat16),
        ],
        cost_estimate=pl.CostEstimate(
            flops=2 * outer * rows * 2 * nvec * 2 * nvec * momenta, bytes_accessed=outer * rows * nvec * 12,
            transcendentals=0),
        name="projection",
    )(place, owner, tau, *pieces)


def from_place(block, up, across):
    sites, groups = lax.axis_size("site"), lax.axis_size("vec")
    route = []
    for z in range(sites):
        for v in range(groups):
            route.append((((z + up) % sites) * groups + (v + across) % groups, z * groups + v))
    return lax.ppermute(block, ("site", "vec"), route)


CHUNKS = 3
ORDER = (("filter", 0), ("filter", 1), ("finish", 0), ("filter", 2), ("finish", 1), ("finish", 2))


def per_device(eigvecs, links, peramb, block_owner, momenta):
    sites, groups = lax.axis_size("site"), lax.axis_size("vec")
    site, group = lax.axis_index("site"), lax.axis_index("vec")
    block = eigvecs.shape[3]
    rows = block * 4 // (sites * CHUNKS)
    own = eigvecs.reshape(6, block * 4, LANES)
    own_links = links.reshape(216, LANES)
    place = jnp.stack([site, group]).astype(jnp.int32)

    received, packed = [], []
    for chunk in range(CHUNKS):
        packed = pack(own, place, chunk, rows, sites, own_links, packed[:1])
        received.append([from_place(packed[d - 1], -d, 0) for d in range(1, sites)])

    flat = lax.broadcasted_iota(jnp.int32, (4, LANES), 0) * LANES + lax.broadcasted_iota(jnp.int32, (4, LANES), 1)
    theta = phase_angle(momenta, flat % LX, flat // LX, jnp.full_like(flat, site), sites)
    cosine, sine = jnp.cos(theta), jnp.sin(theta)

    table = link_tables([own_links] + received[0])
    hops, filtered, shifted, other = {}, {}, {}, {}
    last = None
    for kind, chunk in ORDER:
        after = [] if last is None else [last]
        if kind == "filter":
            out = filter_chunk(own, place, chunk, rows, received[chunk], table, after)
            hops[chunk] = [out[0]] + [from_place(out[d], d, 0) for d in range(1, sites)]
            last = out[0]
        else:
            f, s = finish(own, place, chunk, rows, hops[chunk], cosine, sine, after)
            filtered[chunk], shifted[chunk], other[chunk] = f, s, from_place(f, 0, 1)
            last = s
    filtered, shifted, other = ([group_of[n] for n in range(CHUNKS)] for group_of in (filtered, shifted, other))

    parts = elementals(place, filtered, other, shifted, sites)
    total = parts[0]
    for d in range(1, sites):
        total = total + from_place(parts[d], -d, 0).astype(jnp.float32)
    mine = total.astype(jnp.bfloat16)

    gathered = []
    for up in range(sites):
        piece = mine if up == 0 else from_place(mine, up, 0)
        gathered.append(piece)
        for across in range(1, groups):
            gathered.append(from_place(piece, 0, across))
    sinks, spins = peramb.shape[1], peramb.shape[2]
    tau = peramb.reshape(sinks * spins, 2, block, peramb.shape[5])
    result = projection(tau, place, block_owner, gathered, momenta.shape[0], sites, groups)
    return result.reshape(1, sinks, spins, momenta.shape[0], 2, block, peramb.shape[5])


def from_behind(block, axis, distance):
    devices = range(lax.axis_size(axis))
    route = [((i - distance) % len(devices), i) for i in devices]
    return lax.ppermute(block, axis, route)


def with_halo(block, sides, width):
    for axis, dim in sides:
        count = lax.axis_size(axis)
        forward = [(i, i + 1) for i in range(count - 1)]
        forward.append((count - 1, 0))
        backward = [(target, source) for source, target in forward]
        low = lax.ppermute(
            lax.slice_in_dim(block, block.shape[dim] - width, None, axis=dim), axis, forward
        )
        high = lax.ppermute(lax.slice_in_dim(block, 0, width, axis=dim), axis, backward)
        block = jnp.concatenate([low, block, high], axis=dim)
    return block


def along(field, direction, sense):
    width = field.shape[-1]
    column = lax.broadcasted_iota(jnp.int32, (width,), 0) % LX
    if direction == 0:
        if sense > 0:
            return jnp.where(column == LX - 1, jnp.roll(field, LX - 1, -1), jnp.roll(field, -1, -1))
        return jnp.where(column == 0, jnp.roll(field, 1 - LX, -1), jnp.roll(field, 1, -1))
    return jnp.roll(field, -sense * LX, -1)


def link_times(link_re, link_im, field_re, field_im, dagger):
    result_re = []
    result_im = []
    for target in range(3):
        summed_re = jnp.zeros_like(field_re[0])
        summed_im = jnp.zeros_like(field_re[0])
        for source in range(3):
            if dagger:
                entry_re = link_re[source, target][None]
                entry_im = -link_im[source, target][None]
            else:
                entry_re = link_re[target, source][None]
                entry_im = link_im[target, source][None]
            summed_re = summed_re + entry_re * field_re[source] - entry_im * field_im[source]
            summed_im = summed_im + entry_re * field_im[source] + entry_im * field_re[source]
        result_re.append(summed_re)
        result_im.append(summed_im)
    return (jnp.stack(result_re), jnp.stack(result_im))


def chebyshev(initial, operate):
    current = operate(initial)
    following = 2.0 * operate(current) - initial
    return following


def general_device(eigvecs, links, peramb, block_owner, momenta):
    vectors = eigvecs[0]
    links_here = links[0]
    block = vectors.shape[2]
    layers = vectors.shape[3]
    plane = vectors.shape[4]
    site_count = lax.axis_size("site")
    group_count = lax.axis_size("vec")
    site_rank = lax.axis_index("site")
    group_rank = lax.axis_index("vec")
    portion = plane // group_count
    top_plane = links_here[2, :, :, :, layers - 1 :, :]
    below = from_behind(top_plane, "site", 1)
    behind_links = jnp.concatenate([below, links_here[2, :, :, :, : layers - 1, :]], axis=3)
    back_links = []
    for direction in range(2):
        back_links.append(
            (
                along(links_here[direction, 0], direction, -1),
                along(links_here[direction, 1], direction, -1),
            )
        )
    back_links.append((behind_links[0], behind_links[1]))

    def operate(field):
        padded = with_halo(field, (("site", 3),), 1)
        total_re = jnp.zeros_like(field[0])
        total_im = jnp.zeros_like(field[0])
        for direction in range(3):
            if direction < 2:
                ahead = along(field, direction, 1)
                behind = along(field, direction, -1)
            else:
                ahead = padded[:, :, :, 2:]
                behind = padded[:, :, :, :-2]
            forward = link_times(
                links_here[direction, 0], links_here[direction, 1], ahead[0], ahead[1], False
            )
            backward = link_times(
                back_links[direction][0], back_links[direction][1], behind[0], behind[1], True
            )
            total_re = total_re + forward[0] + backward[0]
            total_im = total_im + forward[1] + backward[1]
        return jnp.stack([total_re, total_im]) * (-1.0 / 6.0)

    filtered = chebyshev(vectors, operate).astype(jnp.bfloat16)
    received = lax.all_to_all(filtered, "vec", split_axis=4, concat_axis=2, tiled=True)
    grouped = received.reshape(2, 3, group_count, block, layers, portion)
    ranks = jnp.arange(group_count, dtype=jnp.int32)
    inverse = jnp.sum(
        ranks[:, None] * (block_owner[:, None] == ranks[None, :]).astype(jnp.int32), axis=0
    )
    ordered = jnp.take(grouped, inverse, axis=2).reshape(2, 3, group_count * block, layers, portion)
    nvec = group_count * block
    flat = group_rank * portion + lax.broadcasted_iota(jnp.int32, (layers, portion), 1)
    depth = site_rank * layers + lax.broadcasted_iota(jnp.int32, (layers, portion), 0)
    theta = phase_angle(momenta, flat % LX, flat // LX, depth, layers * site_count)
    values = ordered.astype(jnp.float32)
    cosine = jnp.cos(theta)[:, None, None]
    sine = jnp.sin(theta)[:, None, None]
    shift_re = cosine * values[0] + sine * values[1]
    shift_im = cosine * values[1] - sine * values[0]
    shifted = jnp.stack([shift_re, shift_im], axis=1).astype(jnp.bfloat16)
    products = jnp.einsum(
        "acizs,pbckzs->aipbk", ordered, shifted, preferred_element_type=jnp.float32
    )
    real = products[0, :, :, 0] + products[1, :, :, 1]
    imag = products[0, :, :, 1] - products[1, :, :, 0]
    momentum_count = momenta.shape[0]
    partial_sum = jnp.stack([real, imag], axis=2).reshape(nvec, momentum_count * 2 * nvec)
    tau = peramb[0]
    tau_rows = tau.reshape(-1, nvec)
    summed = lax.psum(partial_sum, ("site", "vec")).astype(jnp.bfloat16)
    joined = jnp.dot(tau_rows, summed, preferred_element_type=jnp.float32)
    sinks = tau.shape[0]
    spins = tau.shape[1]
    layout = joined.reshape(sinks, spins, 2, block, momentum_count, 2, nvec)
    real_part = layout[:, :, 0, :, :, 0] - layout[:, :, 1, :, :, 1]
    imag_part = layout[:, :, 0, :, :, 1] + layout[:, :, 1, :, :, 0]
    stacked = jnp.stack([real_part, imag_part], axis=0)
    result = jnp.transpose(stacked, (1, 2, 4, 0, 3, 5))
    return result[None].astype(jnp.bfloat16)


def choose(eigvecs, links, peramb, block_owner, momenta):
    block, layers, plane = eigvecs.shape[3:]
    sites, groups = lax.axis_size("site"), lax.axis_size("vec")
    fits = layers == 1 and plane == LX * LY == 4 * LANES and sites == 4 and groups == 2
    fits = fits and block % (4 * sites * CHUNKS) == 0 and block // (sites * CHUNKS) % 8 == 0 and (2 * block) % (32 * sites) == 0 and block % (2 * block // sites) == 0
    device = per_device if fits else general_device
    return device(eigvecs, links, peramb, block_owner, momenta)


def solution(mesh):
    placed = (
        P(("cfg", "tslice"), None, None, "vec", "site", None),
        P(("cfg", "tslice"), None, None, None, None, "site", None),
        P(("cfg", "tslice"), "site", None, None, "vec", None),
        P(),
        P(),
    )
    return jax.shard_map(
        choose,
        mesh=mesh,
        in_specs=placed,
        out_specs=P(("cfg", "tslice"), "site", None, None, None, "vec", None),
        check_vma=False,
    )
```

```python
import functools
import math

import jax
import jax.numpy as jnp
from jax import lax
from jax.experimental import pallas as pl
from jax.experimental.pallas import tpu as pltpu
from jax.sharding import PartitionSpec as P


LX = 32
LY = 16
LANES = 128

two_pi = 2.0 * math.pi

CHUNKS = (16, 24, 8)


def phase_angle(momenta, across, upward, depth, extent):
    return two_pi * (
        (momenta[:, 0, None, None] * across[None]).astype(jnp.float32) / LX
        + (momenta[:, 1, None, None] * upward[None]).astype(jnp.float32) / LY
        + (momenta[:, 2, None, None] * depth[None]).astype(jnp.float32) / extent
    )


VMEM = pl.BlockSpec(memory_space=pltpu.VMEM)
SMEM = pl.BlockSpec(memory_space=pltpu.SMEM)
ANY = pl.BlockSpec(memory_space=pl.ANY)
GRANT = pltpu.CompilerParams(vmem_limit_bytes=16 * 2**20)


class Shifts:
    def __init__(self):
        lane = lax.broadcasted_iota(jnp.int32, (8, LANES), 1)
        row = lax.broadcasted_iota(jnp.int32, (8, LANES), 0) % 4
        column = lane % LX
        self.x_last = column == LX - 1
        self.x_first = column == 0
        self.y_high = lane >= LANES - LX
        self.y_low = lane < LX
        self.row_last = row == 3
        self.row_first = row == 0

    def ahead_x(self, v):
        return jnp.where(self.x_last, pltpu.roll(v, LX - 1, 1), pltpu.roll(v, LANES - 1, 1))

    def behind_x(self, v):
        return jnp.where(self.x_first, pltpu.roll(v, LANES - LX + 1, 1), pltpu.roll(v, 1, 1))

    def ahead_y(self, v):
        a = pltpu.roll(v, LANES - LX, 1)
        wrapped = jnp.where(self.row_last, pltpu.roll(a, 3, 0), pltpu.roll(a, 7, 0))
        return jnp.where(self.y_high, wrapped, a)

    def behind_y(self, v):
        a = pltpu.roll(v, LX, 1)
        wrapped = jnp.where(self.row_first, pltpu.roll(a, 5, 0), pltpu.roll(a, 1, 0))
        return jnp.where(self.y_low, wrapped, a)


def tables_kernel(*refs):
    table_ref = refs[-1]
    shifts = Shifts()
    scale = jnp.float32(-1.0 / 6.0)
    size = refs[0].shape[0]
    links = [ref[ref.shape[0] - size :].astype(jnp.float32) for ref in refs[:-1]]
    count = len(links)

    def entry(plane, direction, part, row, col):
        e = direction * 18 + part * 9 + row * 3 + col
        value = links[plane % count][4 * e : 4 * e + 4] * scale
        return jnp.concatenate([value, value], axis=0)

    for plane in range(count):
        for direction in range(3):
            for target in range(3):
                for source in range(3):
                    slot = (2 * direction) * 18 + (target * 3 + source) * 2
                    table_ref[plane, slot] = entry(plane, direction, 0, target, source)
                    table_ref[plane, slot + 1] = entry(plane, direction, 1, target, source)
                    slot = (2 * direction + 1) * 18 + (target * 3 + source) * 2
                    below = plane + 1 if direction == 2 else plane
                    re = entry(below, direction, 0, source, target)
                    im = entry(below, direction, 1, source, target)
                    if direction < 2:
                        move = shifts.behind_x if direction == 0 else shifts.behind_y
                        re, im = move(re), move(im)
                    table_ref[plane, slot] = re
                    table_ref[plane, slot + 1] = -im


def link_tables(links):
    return pl.pallas_call(
        tables_kernel,
        out_shape=pltpu.VMEM((len(links), 108, 8, LANES), jnp.float32),
        in_specs=[VMEM] * len(links),
        out_specs=VMEM,
        compiler_params=GRANT,
        name="link_tables",
    )(*links)


def pack_kernel(sites, chunk, place_ref, own_ref, *refs):
    outs = refs[1 - sites :]
    rows = CHUNKS[chunk] * 4
    for d in range(1, sites):
        start = row_of(lax.rem(place_ref[0] + d, sites), own_ref.shape[1] // sites, chunk)
        out = outs[d - 1]
        for c in range(6):
            out[c * rows : (c + 1) * rows] = own_ref[c, pl.ds(start, rows), :].astype(jnp.bfloat16)
        if out.shape[0] > 6 * rows:
            out[6 * rows :] = refs[0][...].astype(jnp.bfloat16)


def row_of(slot, rows_per_slot, chunk):
    return pl.multiple_of(slot * rows_per_slot + 4 * sum(CHUNKS[:chunk]), 32)


def pack(own, place, chunk, sites, links, after):
    extra = [links] if chunk == 0 else []
    length = 24 * CHUNKS[chunk] + sum(e.shape[0] for e in extra)
    return pl.pallas_call(
        functools.partial(pack_kernel, sites, chunk),
        out_shape=[pltpu.VMEM((length, LANES), jnp.bfloat16)] * (sites - 1),
        in_specs=[SMEM] + [VMEM] * (1 + len(extra)) + [ANY] * len(after),
        out_specs=[VMEM] * (sites - 1),
        compiler_params=GRANT,
    )(place, own, *extra, *after)


def filter_kernel(sites, chunk, place_ref, *refs):
    fields, table_ref = refs[:sites], refs[sites]
    outs, t1_ref = refs[-1 - sites : -1], refs[-1]
    shifts = Shifts()
    rows = CHUNKS[chunk] * 4
    home = row_of(place_ref[0], fields[0].shape[1] // sites, chunk)

    def hop(plane, here, ahead_z, behind_z):
        count = len(here(0))
        total = [[None] * count for _ in range(6)]
        moves = (shifts.ahead_x, shifts.behind_x, shifts.ahead_y, shifts.behind_y, None, None)
        for direction in range(6):
            if direction < 4:
                field = [[moves[direction](v) for v in here(c)] for c in range(6)]
            else:
                take = ahead_z if direction == 4 else behind_z
                field = [take(c) for c in range(6)]
            for target in range(3):
                for source in range(3):
                    slot = direction * 18 + (target * 3 + source) * 2
                    re = table_ref[plane, slot]
                    im = table_ref[plane, slot + 1]
                    for n in range(count):
                        f_re, f_im = field[source][n], field[3 + source][n]
                        add_re = re * f_re - im * f_im
                        add_im = re * f_im + im * f_re
                        if total[target][n] is None:
                            total[target][n], total[3 + target][n] = add_re, add_im
                        else:
                            total[target][n] = total[target][n] + add_re
                            total[3 + target][n] = total[3 + target][n] + add_im
        return total

    def step(index, carry):
        base = pl.multiple_of(index * 16, 16)

        def start(plane):
            def read(c):
                ref = fields[plane % sites]
                if plane % sites == 0:
                    value = ref[c, pl.ds(pl.multiple_of(home + base, 16), 16), :]
                else:
                    value = ref[pl.ds(pl.multiple_of(c * rows + base, 16), 16), :].astype(jnp.float32)
                return [value[0:8], value[8:16]]

            return read

        def first(plane):
            return lambda c: [t1_ref[plane % sites, c, 0:8], t1_ref[plane % sites, c, 8:16]]

        for plane in range(sites):
            out = hop(plane, start(plane), start(plane - 1), start(plane + 1))
            for c in range(6):
                for n in range(2):
                    t1_ref[plane, c, 8 * n : 8 * n + 8] = out[c][n]
        for plane in range(sites):
            out = hop(plane, first(plane), first(plane - 1), first(plane + 1))
            for c in range(6):
                value = 2.0 * jnp.concatenate(out[c], axis=0)
                outs[plane][c, pl.ds(base, 16), :] = value.astype(jnp.bfloat16)
        return carry

    lax.fori_loop(0, rows // 16, step, 0)


def filter_chunk(own, place, chunk, received, table, after):
    sites = len(received) + 1
    rows = CHUNKS[chunk] * 4
    return pl.pallas_call(
        functools.partial(filter_kernel, sites, chunk),
        out_shape=[pltpu.VMEM((6, rows, LANES), jnp.bfloat16)] * sites,
        in_specs=[SMEM] + [VMEM] * (sites + 1) + [ANY] * len(after),
        out_specs=[VMEM] * sites,
        scratch_shapes=[pltpu.VMEM((sites, 6, 16, LANES), jnp.float32)],
        cost_estimate=pl.CostEstimate(
            flops=432 * 2 * sites * rows * LANES, bytes_accessed=6 * rows * LANES * 4 * sites, transcendentals=0),
        compiler_params=GRANT,
    )(place, own, *received, table, *after)


def finish_kernel(sites, chunk, place_ref, own_ref, *refs):
    hops = refs[:sites]
    cosine_ref, sine_ref = refs[sites : sites + 2]
    filtered_ref, shifted_ref, work_ref = refs[-3:]
    vectors = CHUNKS[chunk]
    momenta = cosine_ref.shape[0]
    for d in range(sites):
        slot = lax.rem(place_ref[0] + d, sites)
        start = row_of(slot, own_ref.shape[1] // sites, chunk)
        for c in range(6):
            work_ref[d, c] = hops[d][c].astype(jnp.float32) - own_ref[c, pl.ds(start, 4 * vectors), :]
        for color in range(3):
            for row in range(4):
                at = slice((color * 4 + row) * LANES, (color * 4 + row + 1) * LANES)
                re = work_ref[d, color, pl.ds(row, vectors, stride=4), :].astype(jnp.bfloat16)
                im = work_ref[d, 3 + color, pl.ds(row, vectors, stride=4), :].astype(jnp.bfloat16)
                filtered_ref[slot, 0, :, at] = re
                filtered_ref[slot, 1, :, at] = im
                re, im = re.astype(jnp.float32), im.astype(jnp.float32)
                for p in range(momenta):
                    cosine = cosine_ref[p, row : row + 1, :]
                    sine = sine_ref[p, row : row + 1, :]
                    shifted_ref[p, slot, 0, :, at] = (cosine * re + sine * im).astype(jnp.bfloat16)
                    shifted_ref[p, slot, 1, :, at] = (cosine * im - sine * re).astype(jnp.bfloat16)


def finish(own, place, chunk, hops, cosine, sine, after):
    sites, momenta, vectors = len(hops), cosine.shape[0], CHUNKS[chunk]
    shapes = ((sites, 2, vectors, 12 * LANES), (momenta, sites, 2, vectors, 12 * LANES))
    return pl.pallas_call(
        functools.partial(finish_kernel, sites, chunk),
        out_shape=[pltpu.VMEM(shape, jnp.bfloat16) for shape in shapes],
        in_specs=[SMEM] + [VMEM] * (sites + 3) + [ANY] * len(after),
        out_specs=[VMEM, VMEM],
        scratch_shapes=[pltpu.VMEM((sites, 6, 4 * vectors, LANES), jnp.float32)],
        cost_estimate=pl.CostEstimate(
            flops=20 * sites * 24 * vectors * LANES, bytes_accessed=sites * 24 * vectors * LANES * 12,
            transcendentals=0),
        compiler_params=GRANT,
    )(place, own, *hops, cosine, sine, *after)


def elemental_kernel(segments, chunks, place_ref, *refs):
    own = refs[:chunks]
    other = refs[chunks : 2 * chunks]
    shifted = refs[2 * chunks : 3 * chunks]
    outs = refs[3 * chunks : 3 * chunks + segments]
    left_ref, right_ref, total_ref = refs[3 * chunks + segments :]
    slots, _, _, depth = own[0].shape
    per_slot = sum(CHUNKS)
    block = slots * per_slot
    for n, ref in enumerate(own + other):
        size = CHUNKS[n % chunks]
        for slot in range(slots):
            at = n // chunks * block + slot * per_slot + sum(CHUNKS[: n % chunks])
            for part in range(2):
                left_ref[at : at + size, part * depth : (part + 1) * depth] = ref[slot, part]
    momenta = shifted[0].shape[0]
    for p in range(momenta):
        for n, ref in enumerate(shifted):
            size = CHUNKS[n]
            for slot in range(slots):
                re, im = ref[p, slot, 0], ref[p, slot, 1]
                at = slot * per_slot + sum(CHUNKS[:n])
                right_ref[at : at + size, :depth] = re
                right_ref[at : at + size, depth:] = im
                right_ref[block + at : block + at + size, :depth] = im
                right_ref[block + at : block + at + size, depth:] = -re
        product = lax.dot_general(
            left_ref[...], right_ref[...], (((1,), (1,)), ((), ())), preferred_element_type=jnp.float32)
        rows = product.shape[0] // segments
        for s in range(segments):
            total_ref[s, :, p * 2 * block : (p + 1) * 2 * block] = product[s * rows : (s + 1) * rows]
    place = place_ref[0]
    for d in range(segments):
        s = lax.rem(place + d, segments)
        outs[d][...] = total_ref[s].astype(outs[d].dtype)


def elementals(place, own, other, shifted, segments):
    chunks = len(own)
    slots, _, _, depth = own[0].shape
    momenta = shifted[0].shape[0]
    block = slots * sum(CHUNKS)
    rows = 2 * block // segments
    columns = momenta * 2 * block
    return pl.pallas_call(
        functools.partial(elemental_kernel, segments, chunks),
        out_shape=tuple(
            pltpu.VMEM((rows, columns), jnp.float32 if d == 0 else jnp.bfloat16) for d in range(segments)),
        in_specs=[SMEM] + [VMEM] * (3 * chunks),
        out_specs=tuple(VMEM for _ in range(segments)),
        scratch_shapes=[
            pltpu.VMEM((2 * block, 2 * depth), jnp.bfloat16),
            pltpu.VMEM((2 * block, 2 * depth), jnp.bfloat16),
            pltpu.VMEM((segments, rows, columns), jnp.float32),
        ],
        cost_estimate=pl.CostEstimate(
            flops=2 * 2 * block * columns * 2 * depth, bytes_accessed=8 * 2 * block * depth, transcendentals=0),
        compiler_params=GRANT,
        name="elementals",
    )(place, *own, *other, *shifted)


def projection_kernel(sites, groups, place_ref, owner_ref, tau_ref, *refs):
    pieces = refs[: sites * groups]
    out_ref, parts_ref, right_ref = refs[sites * groups :]
    momenta, nvec = right_ref.shape[0], right_ref.shape[1] // 2
    block = nvec // 2

    @pl.when(pl.program_id(0) == 0)
    def assemble():
        rows = pieces[0].shape[0]
        for n, piece in enumerate(pieces):
            up, across = n // groups, n % groups
            z, v = lax.rem(place_ref[0] + up, sites), lax.rem(place_ref[1] + across, groups)
            per = block // rows
            column = owner_ref[v]
            row = owner_ref[lax.rem(v + lax.div(z, per), groups)] * block + lax.rem(z, per) * rows
            row = pl.multiple_of(row, 32)
            for p in range(momenta):
                parts_ref[column, p, pl.ds(row, rows), :] = piece[:, p * 2 * block : (p + 1) * 2 * block]
        for p in range(momenta):
            low, high = parts_ref[0, p], parts_ref[1, p]
            re = jnp.concatenate([low[:, :block], high[:, :block]], axis=1)
            im = jnp.concatenate([low[:, block:], high[:, block:]], axis=1)
            right_ref[p, :nvec, :nvec] = re
            right_ref[p, :nvec, nvec:] = im
            right_ref[p, nvec:, :nvec] = -im
            right_ref[p, nvec:, nvec:] = re

    left = jnp.concatenate([tau_ref[0, 0], tau_ref[0, 1]], axis=1)
    for p in range(momenta):
        product = jnp.dot(left, right_ref[p], preferred_element_type=jnp.float32)
        out_ref[0, p, 0] = product[:, :nvec].astype(jnp.bfloat16)
        out_ref[0, p, 1] = product[:, nvec:].astype(jnp.bfloat16)


def projection(tau, place, owner, pieces, momenta, sites, groups):
    outer, _, rows, nvec = tau.shape
    count = len(pieces)
    return pl.pallas_call(
        functools.partial(projection_kernel, sites, groups),
        grid=(outer,),
        out_shape=jax.ShapeDtypeStruct((outer, momenta, 2, rows, nvec), jnp.bfloat16),
        in_specs=[pl.BlockSpec(memory_space=pltpu.SMEM), pl.BlockSpec(memory_space=pltpu.SMEM),
                  pl.BlockSpec((1, 2, rows, nvec), lambda i: (i, 0, 0, 0))]
        + [pl.BlockSpec(memory_space=pltpu.VMEM)] * count,
        out_specs=pl.BlockSpec((1, momenta, 2, rows, nvec), lambda i: (i, 0, 0, 0, 0)),
        scratch_shapes=[
            pltpu.VMEM((2, momenta, nvec, nvec), jnp.bfloat16),
            pltpu.VMEM((momenta, 2 * nvec, 2 * nvec), jnp.bfloat16),
        ],
        cost_estimate=pl.CostEstimate(
            flops=2 * outer * rows * 2 * nvec * 2 * nvec * momenta, bytes_accessed=outer * rows * nvec * 12,
            transcendentals=0),
        compiler_params=GRANT,
        name="projection",
    )(place, owner, tau, *pieces)


def from_place(block, up, across):
    sites, groups = lax.axis_size("site"), lax.axis_size("vec")
    route = []
    for z in range(sites):
        for v in range(groups):
            route.append((((z + up) % sites) * groups + (v + across) % groups, z * groups + v))
    return lax.ppermute(block, ("site", "vec"), route)


ORDER = (("filter", 0), ("filter", 1), ("finish", 0), ("filter", 2), ("finish", 1), ("finish", 2))


def per_device(eigvecs, links, peramb, block_owner, momenta):
    sites, groups = lax.axis_size("site"), lax.axis_size("vec")
    site, group = lax.axis_index("site"), lax.axis_index("vec")
    block = eigvecs.shape[3]
    own = eigvecs.reshape(6, block * 4, LANES)
    own_links = links.reshape(216, LANES)
    place = jnp.stack([site, group]).astype(jnp.int32)

    received, packed = [], []
    for chunk in range(len(CHUNKS)):
        packed = pack(own, place, chunk, sites, own_links, packed[:1])
        received.append([from_place(packed[d - 1], -d, 0) for d in range(1, sites)])

    flat = lax.broadcasted_iota(jnp.int32, (4, LANES), 0) * LANES + lax.broadcasted_iota(jnp.int32, (4, LANES), 1)
    theta = phase_angle(momenta, flat % LX, flat // LX, jnp.full_like(flat, site), sites)
    cosine, sine = jnp.cos(theta), jnp.sin(theta)

    table = link_tables([own_links] + received[0])
    hops, filtered, shifted, other = {}, {}, {}, {}
    last = None
    for kind, chunk in ORDER:
        after = [] if last is None else [last]
        if kind == "filter":
            out = filter_chunk(own, place, chunk, received[chunk], table, after)
            hops[chunk] = [out[0]] + [from_place(out[d], d, 0) for d in range(1, sites)]
            last = out[0]
        else:
            f, s = finish(own, place, chunk, hops[chunk], cosine, sine, after)
            other[chunk] = from_place(f, 0, 1)
            filtered[chunk], shifted[chunk] = f, s
            last = s
    filtered, shifted, other = ([group_of[n] for n in range(len(CHUNKS))] for group_of in (filtered, shifted, other))

    parts = elementals(place, filtered, other, shifted, sites)
    total = parts[0]
    for d in range(1, sites):
        total = total + from_place(parts[d], -d, 0).astype(jnp.float32)
    mine = total.astype(jnp.bfloat16)

    gathered = []
    for up in range(sites):
        piece = mine if up == 0 else from_place(mine, up, 0)
        gathered.append(piece)
        for across in range(1, groups):
            gathered.append(from_place(piece, 0, across))
    sinks, spins = peramb.shape[1], peramb.shape[2]
    tau = peramb.reshape(sinks * spins, 2, block, peramb.shape[5])
    result = projection(tau, place, block_owner, gathered, momenta.shape[0], sites, groups)
    return result.reshape(1, sinks, spins, momenta.shape[0], 2, block, peramb.shape[5])


def from_behind(block, axis, distance):
    devices = range(lax.axis_size(axis))
    route = [((i - distance) % len(devices), i) for i in devices]
    return lax.ppermute(block, axis, route)


def with_halo(block, sides, width):
    for axis, dim in sides:
        count = lax.axis_size(axis)
        forward = [(i, i + 1) for i in range(count - 1)]
        forward.append((count - 1, 0))
        backward = [(target, source) for source, target in forward]
        low = lax.ppermute(
            lax.slice_in_dim(block, block.shape[dim] - width, None, axis=dim), axis, forward
        )
        high = lax.ppermute(lax.slice_in_dim(block, 0, width, axis=dim), axis, backward)
        block = jnp.concatenate([low, block, high], axis=dim)
    return block


def along(field, direction, sense):
    width = field.shape[-1]
    column = lax.broadcasted_iota(jnp.int32, (width,), 0) % LX
    if direction == 0:
        if sense > 0:
            return jnp.where(column == LX - 1, jnp.roll(field, LX - 1, -1), jnp.roll(field, -1, -1))
        return jnp.where(column == 0, jnp.roll(field, 1 - LX, -1), jnp.roll(field, 1, -1))
    return jnp.roll(field, -sense * LX, -1)


def link_times(link_re, link_im, field_re, field_im, dagger):
    result_re = []
    result_im = []
    for target in range(3):
        summed_re = jnp.zeros_like(field_re[0])
        summed_im = jnp.zeros_like(field_re[0])
        for source in range(3):
            if dagger:
                entry_re = link_re[source, target][None]
                entry_im = -link_im[source, target][None]
            else:
                entry_re = link_re[target, source][None]
                entry_im = link_im[target, source][None]
            summed_re = summed_re + entry_re * field_re[source] - entry_im * field_im[source]
            summed_im = summed_im + entry_re * field_im[source] + entry_im * field_re[source]
        result_re.append(summed_re)
        result_im.append(summed_im)
    return (jnp.stack(result_re), jnp.stack(result_im))


def chebyshev(initial, operate):
    current = operate(initial)
    following = 2.0 * operate(current) - initial
    return following


def general_device(eigvecs, links, peramb, block_owner, momenta):
    vectors = eigvecs[0]
    links_here = links[0]
    block = vectors.shape[2]
    layers = vectors.shape[3]
    plane = vectors.shape[4]
    site_count = lax.axis_size("site")
    group_count = lax.axis_size("vec")
    site_rank = lax.axis_index("site")
    group_rank = lax.axis_index("vec")
    portion = plane // group_count
    top_plane = links_here[2, :, :, :, layers - 1 :, :]
    below = from_behind(top_plane, "site", 1)
    behind_links = jnp.concatenate([below, links_here[2, :, :, :, : layers - 1, :]], axis=3)
    back_links = []
    for direction in range(2):
        back_links.append(
            (
                along(links_here[direction, 0], direction, -1),
                along(links_here[direction, 1], direction, -1),
            )
        )
    back_links.append((behind_links[0], behind_links[1]))

    def operate(field):
        padded = with_halo(field, (("site", 3),), 1)
        total_re = jnp.zeros_like(field[0])
        total_im = jnp.zeros_like(field[0])
        for direction in range(3):
            if direction < 2:
                ahead = along(field, direction, 1)
                behind = along(field, direction, -1)
            else:
                ahead = padded[:, :, :, 2:]
                behind = padded[:, :, :, :-2]
            forward = link_times(
                links_here[direction, 0], links_here[direction, 1], ahead[0], ahead[1], False
            )
            backward = link_times(
                back_links[direction][0], back_links[direction][1], behind[0], behind[1], True
            )
            total_re = total_re + forward[0] + backward[0]
            total_im = total_im + forward[1] + backward[1]
        return jnp.stack([total_re, total_im]) * (-1.0 / 6.0)

    filtered = chebyshev(vectors, operate).astype(jnp.bfloat16)
    received = lax.all_to_all(filtered, "vec", split_axis=4, concat_axis=2, tiled=True)
    grouped = received.reshape(2, 3, group_count, block, layers, portion)
    ranks = jnp.arange(group_count, dtype=jnp.int32)
    inverse = jnp.sum(
        ranks[:, None] * (block_owner[:, None] == ranks[None, :]).astype(jnp.int32), axis=0
    )
    ordered = jnp.take(grouped, inverse, axis=2).reshape(2, 3, group_count * block, layers, portion)
    nvec = group_count * block
    flat = group_rank * portion + lax.broadcasted_iota(jnp.int32, (layers, portion), 1)
    depth = site_rank * layers + lax.broadcasted_iota(jnp.int32, (layers, portion), 0)
    theta = phase_angle(momenta, flat % LX, flat // LX, depth, layers * site_count)
    values = ordered.astype(jnp.float32)
    cosine = jnp.cos(theta)[:, None, None]
    sine = jnp.sin(theta)[:, None, None]
    shift_re = cosine * values[0] + sine * values[1]
    shift_im = cosine * values[1] - sine * values[0]
    shifted = jnp.stack([shift_re, shift_im], axis=1).astype(jnp.bfloat16)
    products = jnp.einsum(
        "acizs,pbckzs->aipbk", ordered, shifted, preferred_element_type=jnp.float32
    )
    real = products[0, :, :, 0] + products[1, :, :, 1]
    imag = products[0, :, :, 1] - products[1, :, :, 0]
    momentum_count = momenta.shape[0]
    partial_sum = jnp.stack([real, imag], axis=2).reshape(nvec, momentum_count * 2 * nvec)
    tau = peramb[0]
    tau_rows = tau.reshape(-1, nvec)
    summed = lax.psum(partial_sum, ("site", "vec")).astype(jnp.bfloat16)
    joined = jnp.dot(tau_rows, summed, preferred_element_type=jnp.float32)
    sinks = tau.shape[0]
    spins = tau.shape[1]
    layout = joined.reshape(sinks, spins, 2, block, momentum_count, 2, nvec)
    real_part = layout[:, :, 0, :, :, 0] - layout[:, :, 1, :, :, 1]
    imag_part = layout[:, :, 0, :, :, 1] + layout[:, :, 1, :, :, 0]
    stacked = jnp.stack([real_part, imag_part], axis=0)
    result = jnp.transpose(stacked, (1, 2, 4, 0, 3, 5))
    return result[None].astype(jnp.bfloat16)


def choose(eigvecs, links, peramb, block_owner, momenta):
    block, layers, plane = eigvecs.shape[3:]
    sites, groups = lax.axis_size("site"), lax.axis_size("vec")
    fits = layers == 1 and plane == LX * LY == 4 * LANES and sites == 4 and groups == 2
    fits = fits and block == sites * sum(CHUNKS) and (2 * block) % (32 * sites) == 0 and block % (2 * block // sites) == 0
    device = per_device if fits else general_device
    return device(eigvecs, links, peramb, block_owner, momenta)


def solution(mesh):
    placed = (
        P(("cfg", "tslice"), None, None, "vec", "site", None),
        P(("cfg", "tslice"), None, None, None, None, "site", None),
        P(("cfg", "tslice"), "site", None, None, "vec", None),
        P(),
        P(),
    )
    return jax.shard_map(
        choose,
        mesh=mesh,
        in_specs=placed,
        out_specs=P(("cfg", "tslice"), "site", None, None, None, "vec", None),
        check_vma=False,
    )
```

```python
import functools
import math

import jax
import jax.numpy as jnp
from jax import lax
from jax.experimental import pallas as pl
from jax.experimental.pallas import tpu as pltpu
from jax.sharding import PartitionSpec as P


LX = 32
LY = 16
LANES = 128

two_pi = 2.0 * math.pi

CHUNKS = (16, 16, 16)


def phase_angle(momenta, across, upward, depth, extent):
    return two_pi * (
        (momenta[:, 0, None, None] * across[None]).astype(jnp.float32) / LX
        + (momenta[:, 1, None, None] * upward[None]).astype(jnp.float32) / LY
        + (momenta[:, 2, None, None] * depth[None]).astype(jnp.float32) / extent
    )


VMEM = pl.BlockSpec(memory_space=pltpu.VMEM)
SMEM = pl.BlockSpec(memory_space=pltpu.SMEM)
ANY = pl.BlockSpec(memory_space=pl.ANY)
GRANT = pltpu.CompilerParams(vmem_limit_bytes=16 * 2**20)


class Shifts:
    def __init__(self):
        lane = lax.broadcasted_iota(jnp.int32, (8, LANES), 1)
        row = lax.broadcasted_iota(jnp.int32, (8, LANES), 0) % 4
        column = lane % LX
        self.x_last = column == LX - 1
        self.x_first = column == 0
        self.y_high = lane >= LANES - LX
        self.y_low = lane < LX
        self.row_last = row == 3
        self.row_first = row == 0

    def ahead_x(self, v):
        return jnp.where(self.x_last, pltpu.roll(v, LX - 1, 1), pltpu.roll(v, LANES - 1, 1))

    def behind_x(self, v):
        return jnp.where(self.x_first, pltpu.roll(v, LANES - LX + 1, 1), pltpu.roll(v, 1, 1))

    def ahead_y(self, v):
        a = pltpu.roll(v, LANES - LX, 1)
        wrapped = jnp.where(self.row_last, pltpu.roll(a, 3, 0), pltpu.roll(a, 7, 0))
        return jnp.where(self.y_high, wrapped, a)

    def behind_y(self, v):
        a = pltpu.roll(v, LX, 1)
        wrapped = jnp.where(self.row_first, pltpu.roll(a, 5, 0), pltpu.roll(a, 1, 0))
        return jnp.where(self.y_low, wrapped, a)


def tables_kernel(*refs):
    table_ref = refs[-1]
    shifts = Shifts()
    scale = jnp.float32(-1.0 / 6.0)
    size = refs[0].shape[0]
    links = [ref[ref.shape[0] - size :].astype(jnp.float32) for ref in refs[:-1]]
    count = len(links)

    def entry(plane, direction, part, row, col):
        e = direction * 18 + part * 9 + row * 3 + col
        value = links[plane % count][4 * e : 4 * e + 4] * scale
        return jnp.concatenate([value, value], axis=0)

    for plane in range(count):
        for direction in range(3):
            for target in range(3):
                for source in range(3):
                    slot = (2 * direction) * 18 + (target * 3 + source) * 2
                    table_ref[plane, slot] = entry(plane, direction, 0, target, source)
                    table_ref[plane, slot + 1] = entry(plane, direction, 1, target, source)
                    slot = (2 * direction + 1) * 18 + (target * 3 + source) * 2
                    below = plane + 1 if direction == 2 else plane
                    re = entry(below, direction, 0, source, target)
                    im = entry(below, direction, 1, source, target)
                    if direction < 2:
                        move = shifts.behind_x if direction == 0 else shifts.behind_y
                        re, im = move(re), move(im)
                    table_ref[plane, slot] = re
                    table_ref[plane, slot + 1] = -im


def link_tables(links):
    return pl.pallas_call(
        tables_kernel,
        out_shape=pltpu.VMEM((len(links), 108, 8, LANES), jnp.float32),
        in_specs=[VMEM] * len(links),
        out_specs=VMEM,
        compiler_params=GRANT,
        name="link_tables",
    )(*links)


def pack_kernel(sites, chunk, place_ref, own_ref, *refs):
    outs = refs[1 - sites :]
    rows = CHUNKS[chunk] * 4
    for d in range(1, sites):
        start = row_of(lax.rem(place_ref[0] + d, sites), own_ref.shape[1] // sites, chunk)
        out = outs[d - 1]
        for c in range(6):
            out[c * rows : (c + 1) * rows] = own_ref[c, pl.ds(start, rows), :].astype(jnp.bfloat16)
        if out.shape[0] > 6 * rows:
            out[6 * rows :] = refs[0][...].astype(jnp.bfloat16)


def row_of(slot, rows_per_slot, chunk):
    return pl.multiple_of(slot * rows_per_slot + 4 * sum(CHUNKS[:chunk]), 32)


def pack(own, place, chunk, sites, links, after):
    extra = [links] if chunk == 0 else []
    length = 24 * CHUNKS[chunk] + sum(e.shape[0] for e in extra)
    return pl.pallas_call(
        functools.partial(pack_kernel, sites, chunk),
        out_shape=[pltpu.VMEM((length, LANES), jnp.bfloat16)] * (sites - 1),
        in_specs=[SMEM] + [VMEM] * (1 + len(extra)) + [ANY] * len(after),
        out_specs=[VMEM] * (sites - 1),
        compiler_params=GRANT,
    )(place, own, *extra, *after)


def filter_kernel(sites, chunk, place_ref, *refs):
    fields, table_ref = refs[:sites], refs[sites]
    outs, t1_ref = refs[-1 - sites : -1], refs[-1]
    shifts = Shifts()
    rows = CHUNKS[chunk] * 4
    home = row_of(place_ref[0], fields[0].shape[1] // sites, chunk)

    def hop(plane, here, ahead_z, behind_z):
        count = len(here(0))
        total = [[None] * count for _ in range(6)]
        moves = (shifts.ahead_x, shifts.behind_x, shifts.ahead_y, shifts.behind_y, None, None)
        for direction in range(6):
            if direction < 4:
                field = [[moves[direction](v) for v in here(c)] for c in range(6)]
            else:
                take = ahead_z if direction == 4 else behind_z
                field = [take(c) for c in range(6)]
            for target in range(3):
                for source in range(3):
                    slot = direction * 18 + (target * 3 + source) * 2
                    re = table_ref[plane, slot]
                    im = table_ref[plane, slot + 1]
                    for n in range(count):
                        f_re, f_im = field[source][n], field[3 + source][n]
                        add_re = re * f_re - im * f_im
                        add_im = re * f_im + im * f_re
                        if total[target][n] is None:
                            total[target][n], total[3 + target][n] = add_re, add_im
                        else:
                            total[target][n] = total[target][n] + add_re
                            total[3 + target][n] = total[3 + target][n] + add_im
        return total

    def step(index, carry):
        base = pl.multiple_of(index * 16, 16)

        def start(plane):
            def read(c):
                ref = fields[plane % sites]
                if plane % sites == 0:
                    value = ref[c, pl.ds(pl.multiple_of(home + base, 16), 16), :]
                else:
                    value = ref[pl.ds(pl.multiple_of(c * rows + base, 16), 16), :].astype(jnp.float32)
                return [value[0:8], value[8:16]]

            return read

        def first(plane):
            return lambda c: [t1_ref[plane % sites, c, 0:8], t1_ref[plane % sites, c, 8:16]]

        for plane in range(sites):
            out = hop(plane, start(plane), start(plane - 1), start(plane + 1))
            for c in range(6):
                for n in range(2):
                    t1_ref[plane, c, 8 * n : 8 * n + 8] = out[c][n]
        for plane in range(sites):
            out = hop(plane, first(plane), first(plane - 1), first(plane + 1))
            for c in range(6):
                value = 2.0 * jnp.concatenate(out[c], axis=0)
                outs[plane][c, pl.ds(base, 16), :] = value.astype(jnp.bfloat16)
        return carry

    lax.fori_loop(0, rows // 16, step, 0)


def filter_chunk(own, place, chunk, received, table, after):
    sites = len(received) + 1
    rows = CHUNKS[chunk] * 4
    return pl.pallas_call(
        functools.partial(filter_kernel, sites, chunk),
        out_shape=[pltpu.VMEM((6, rows, LANES), jnp.bfloat16)] * sites,
        in_specs=[SMEM] + [VMEM] * (sites + 1) + [ANY] * len(after),
        out_specs=[VMEM] * sites,
        scratch_shapes=[pltpu.VMEM((sites, 6, 16, LANES), jnp.float32)],
        cost_estimate=pl.CostEstimate(
            flops=432 * 2 * sites * rows * LANES, bytes_accessed=6 * rows * LANES * 4 * sites, transcendentals=0),
        compiler_params=GRANT,
    )(place, own, *received, table, *after)


def finish_kernel(sites, chunk, place_ref, own_ref, *refs):
    hops = refs[:sites]
    cosine_ref, sine_ref = refs[sites : sites + 2]
    filtered_ref, shifted_ref, work_ref = refs[-3:]
    vectors = CHUNKS[chunk]
    momenta = cosine_ref.shape[0]
    for d in range(sites):
        slot = lax.rem(place_ref[0] + d, sites)
        start = row_of(slot, own_ref.shape[1] // sites, chunk)
        for c in range(6):
            work_ref[d, c] = hops[d][c].astype(jnp.float32) - own_ref[c, pl.ds(start, 4 * vectors), :]
        for color in range(3):
            for row in range(4):
                at = slice((color * 4 + row) * LANES, (color * 4 + row + 1) * LANES)
                re = work_ref[d, color, pl.ds(row, vectors, stride=4), :].astype(jnp.bfloat16)
                im = work_ref[d, 3 + color, pl.ds(row, vectors, stride=4), :].astype(jnp.bfloat16)
                filtered_ref[slot, 0, :, at] = re
                filtered_ref[slot, 1, :, at] = im
                re, im = re.astype(jnp.float32), im.astype(jnp.float32)
                for p in range(momenta):
                    cosine = cosine_ref[p, row : row + 1, :]
                    sine = sine_ref[p, row : row + 1, :]
                    shifted_ref[p, slot, 0, :, at] = (cosine * re + sine * im).astype(jnp.bfloat16)
                    shifted_ref[p, slot, 1, :, at] = (cosine * im - sine * re).astype(jnp.bfloat16)


def finish(own, place, chunk, hops, cosine, sine, after):
    sites, momenta, vectors = len(hops), cosine.shape[0], CHUNKS[chunk]
    shapes = ((sites, 2, vectors, 12 * LANES), (momenta, sites, 2, vectors, 12 * LANES))
    return pl.pallas_call(
        functools.partial(finish_kernel, sites, chunk),
        out_shape=[pltpu.VMEM(shape, jnp.bfloat16) for shape in shapes],
        in_specs=[SMEM] + [VMEM] * (sites + 3) + [ANY] * len(after),
        out_specs=[VMEM, VMEM],
        scratch_shapes=[pltpu.VMEM((sites, 6, 4 * vectors, LANES), jnp.float32)],
        cost_estimate=pl.CostEstimate(
            flops=20 * sites * 24 * vectors * LANES, bytes_accessed=sites * 24 * vectors * LANES * 12,
            transcendentals=0),
        compiler_params=GRANT,
    )(place, own, *hops, cosine, sine, *after)


def fill_left(left_ref, chunks):
    slots, _, _, depth = chunks[0].shape
    for n, ref in enumerate(chunks):
        for slot in range(slots):
            at = slot * sum(CHUNKS) + sum(CHUNKS[:n])
            for part in range(2):
                left_ref[at : at + CHUNKS[n], part * depth : (part + 1) * depth] = ref[slot, part]


def multiply(left_ref, right_ref, total_ref, place_ref, outs):
    segments, rows, _ = total_ref.shape
    for p in range(right_ref.shape[0]):
        product = lax.dot_general(
            left_ref[...], right_ref[p], (((1,), (1,)), ((), ())), preferred_element_type=jnp.float32)
        width = product.shape[1]
        for s in range(segments):
            total_ref[s, :, p * width : (p + 1) * width] = product[s * rows : (s + 1) * rows]
    for d in range(segments):
        outs[d][...] = total_ref[lax.rem(place_ref[0] + d, segments)].astype(outs[d].dtype)


def own_kernel(segments, place_ref, *refs):
    chunks = len(CHUNKS)
    own, shifted = refs[:chunks], refs[chunks : 2 * chunks]
    outs = refs[2 * chunks : 2 * chunks + segments]
    right_ref, left_ref, total_ref = refs[2 * chunks + segments :]
    slots, _, _, depth = own[0].shape
    block = left_ref.shape[0]
    fill_left(left_ref, own)
    for p in range(right_ref.shape[0]):
        for n, ref in enumerate(shifted):
            for slot in range(slots):
                re, im = ref[p, slot, 0], ref[p, slot, 1]
                at = slot * sum(CHUNKS) + sum(CHUNKS[:n])
                low, high = slice(at, at + CHUNKS[n]), slice(block + at, block + at + CHUNKS[n])
                right_ref[p, low, :depth] = re
                right_ref[p, low, depth:] = im
                right_ref[p, high, :depth] = im
                right_ref[p, high, depth:] = -re
    multiply(left_ref, right_ref, total_ref, place_ref, outs)


def other_kernel(segments, place_ref, *refs):
    chunks = len(CHUNKS)
    other, right_ref = refs[:chunks], refs[chunks]
    outs = refs[chunks + 1 : chunks + 1 + segments]
    left_ref, total_ref = refs[chunks + 1 + segments :]
    fill_left(left_ref, other)
    multiply(left_ref, right_ref, total_ref, place_ref, outs)


def elementals(place, left, shifted, right, segments):
    _, _, _, depth = left[0].shape
    block = segments * sum(CHUNKS)
    own = right is None
    momenta = shifted[0].shape[0] if own else right.shape[0]
    rows, columns = block // segments, momenta * 2 * block
    shapes = [pltpu.VMEM((rows, columns), jnp.float32 if d == 0 else jnp.bfloat16) for d in range(segments)]
    if own:
        shapes.append(pltpu.VMEM((momenta, 2 * block, 2 * depth), jnp.bfloat16))
    operands = [*left, *shifted] if own else [*left, right]
    return pl.pallas_call(
        functools.partial(own_kernel if own else other_kernel, segments),
        out_shape=shapes,
        in_specs=[SMEM] + [VMEM] * len(operands),
        out_specs=[VMEM] * len(shapes),
        scratch_shapes=[
            pltpu.VMEM((block, 2 * depth), jnp.bfloat16),
            pltpu.VMEM((segments, rows, columns), jnp.float32),
        ],
        cost_estimate=pl.CostEstimate(
            flops=2 * block * columns * 2 * depth, bytes_accessed=8 * block * depth, transcendentals=0),
        compiler_params=GRANT,
        name="elementals_own" if own else "elementals_other",
    )(place, *operands)


def fill_right(right_ref, pieces, across, place_ref, owner_ref):
    sites = len(pieces)
    momenta, nvec, block = right_ref.shape[0], right_ref.shape[1] // 2, right_ref.shape[2] // 2
    rows = block // sites
    v = lax.rem(place_ref[1] + across, 2)
    for up, piece in enumerate(pieces):
        z = lax.rem(place_ref[0] + up, sites)
        for part, owner in ((0, owner_ref[v]), (1, owner_ref[1 - v])):
            row = pl.multiple_of(owner * block + z * rows, 16)
            low = pl.multiple_of(nvec + owner * block + z * rows, 16)
            for p in range(momenta):
                value = piece[part * rows : (part + 1) * rows, p * 2 * block : (p + 1) * 2 * block]
                right_ref[p, pl.ds(row, rows), :] = value
                turned = jnp.concatenate([-value[:, block:], value[:, :block]], axis=1)
                right_ref[p, pl.ds(low, rows), :] = turned


def first_kernel(sites, place_ref, owner_ref, tau_ref, *refs):
    pieces, (out_ref, right_ref) = refs[:sites], refs[sites:]
    fill_right(right_ref, pieces, 0, place_ref, owner_ref)

    def step(n, carry):
        left = jnp.concatenate([tau_ref[n, 0], tau_ref[n, 1]], axis=1)
        for p in range(right_ref.shape[0]):
            product = jnp.dot(left, right_ref[p], preferred_element_type=jnp.float32)
            out_ref[n, p] = product.astype(jnp.bfloat16)
        return carry

    lax.fori_loop(0, tau_ref.shape[0], step, 0)


def second_kernel(sites, place_ref, owner_ref, tau_ref, first_ref, *refs):
    pieces, (out_ref, right_ref) = refs[:sites], refs[sites:]

    @pl.when(pl.program_id(0) == 0)
    def assemble():
        fill_right(right_ref, pieces, 1, place_ref, owner_ref)

    block = right_ref.shape[2] // 2
    left = jnp.concatenate([tau_ref[0, 0], tau_ref[0, 1]], axis=1)
    leads = owner_ref[place_ref[1]] == 0
    for p in range(right_ref.shape[0]):
        mine = first_ref[0, p]
        product = jnp.dot(left, right_ref[p], preferred_element_type=jnp.float32).astype(jnp.bfloat16)
        low, high = jnp.where(leads, mine, product), jnp.where(leads, product, mine)
        out_ref[0, p, 0] = jnp.concatenate([low[:, :block], high[:, :block]], axis=1)
        out_ref[0, p, 1] = jnp.concatenate([low[:, block:], high[:, block:]], axis=1)


def project_first(tau, place, owner, pieces, momenta):
    outer, _, rows, nvec = tau.shape
    block = nvec // 2
    return pl.pallas_call(
        functools.partial(first_kernel, len(pieces)),
        out_shape=pltpu.VMEM((outer, momenta, rows, 2 * block), jnp.bfloat16),
        in_specs=[SMEM, SMEM] + [VMEM] * (1 + len(pieces)),
        out_specs=VMEM,
        scratch_shapes=[pltpu.VMEM((momenta, 2 * nvec, 2 * block), jnp.bfloat16)],
        cost_estimate=pl.CostEstimate(
            flops=2 * outer * rows * 2 * nvec * nvec * momenta, bytes_accessed=outer * rows * nvec * 8,
            transcendentals=0),
        compiler_params=GRANT,
        name="project_first",
    )(place, owner, tau, *pieces)


def project_second(tau, place, owner, first, pieces, momenta):
    outer, _, rows, nvec = tau.shape
    return pl.pallas_call(
        functools.partial(second_kernel, len(pieces)),
        grid=(outer,),
        out_shape=jax.ShapeDtypeStruct((outer, momenta, 2, rows, nvec), jnp.bfloat16),
        in_specs=[SMEM, SMEM, pl.BlockSpec((1, 2, rows, nvec), lambda i: (i, 0, 0, 0)),
                  pl.BlockSpec((1, *first.shape[1:]), lambda i: (i, 0, 0, 0))] + [VMEM] * len(pieces),
        out_specs=pl.BlockSpec((1, momenta, 2, rows, nvec), lambda i: (i, 0, 0, 0, 0)),
        scratch_shapes=[pltpu.VMEM((momenta, 2 * nvec, nvec), jnp.bfloat16)],
        cost_estimate=pl.CostEstimate(
            flops=2 * outer * rows * 2 * nvec * nvec * momenta, bytes_accessed=outer * rows * nvec * 12,
            transcendentals=0),
        compiler_params=GRANT,
        name="project_second",
    )(place, owner, tau, first, *pieces)


def from_place(block, up, across):
    sites, groups = lax.axis_size("site"), lax.axis_size("vec")
    route = []
    for z in range(sites):
        for v in range(groups):
            route.append((((z + up) % sites) * groups + (v + across) % groups, z * groups + v))
    return lax.ppermute(block, ("site", "vec"), route)


ORDER = (("filter", 0), ("filter", 1), ("finish", 0), ("filter", 2), ("finish", 1), ("finish", 2))


def per_device(eigvecs, links, peramb, block_owner, momenta):
    sites = lax.axis_size("site")
    site, group = lax.axis_index("site"), lax.axis_index("vec")
    block = eigvecs.shape[3]
    own = eigvecs.reshape(6, block * 4, LANES)
    own_links = links.reshape(216, LANES)
    place = jnp.stack([site, group]).astype(jnp.int32)

    received, packed = [], []
    for chunk in range(len(CHUNKS)):
        packed = pack(own, place, chunk, sites, own_links, packed[:1])
        received.append([from_place(packed[d - 1], -d, 0) for d in range(1, sites)])

    flat = lax.broadcasted_iota(jnp.int32, (4, LANES), 0) * LANES + lax.broadcasted_iota(jnp.int32, (4, LANES), 1)
    theta = phase_angle(momenta, flat % LX, flat // LX, jnp.full_like(flat, site), sites)
    cosine, sine = jnp.cos(theta), jnp.sin(theta)

    table = link_tables([own_links] + received[0])
    hops, filtered, shifted, other = {}, {}, {}, {}
    last = None
    for kind, chunk in ORDER:
        after = [] if last is None else [last]
        if kind == "filter":
            out = filter_chunk(own, place, chunk, received[chunk], table, after)
            hops[chunk] = [out[0]] + [from_place(out[d], d, 0) for d in range(1, sites)]
            last = out[0]
        else:
            f, s = finish(own, place, chunk, hops[chunk], cosine, sine, after)
            other[chunk] = from_place(f, 0, 1)
            filtered[chunk], shifted[chunk] = f, s
            last = s
    filtered, shifted, other = ([group_of[n] for n in range(len(CHUNKS))] for group_of in (filtered, shifted, other))

    *parts, right = elementals(place, filtered, shifted, None, sites)
    sent = [from_place(parts[d], -d, 0) for d in range(1, sites)]
    own_sum = functools.reduce(lambda total, part: total + part.astype(jnp.float32), sent, parts[0])
    parts = elementals(place, other, None, right, sites)
    sent = [from_place(parts[d], -d, 0) for d in range(1, sites)]
    other_sum = functools.reduce(lambda total, part: total + part.astype(jnp.float32), sent, parts[0])
    mine = jnp.concatenate([own_sum, other_sum], axis=0).astype(jnp.bfloat16)

    across = [from_place(mine, 0, 1)]
    pieces = [mine] + [from_place(mine, up, 0) for up in range(1, sites)]
    across += [from_place(piece, 0, 1) for piece in pieces[1:]]
    sinks, spins = peramb.shape[1], peramb.shape[2]
    tau = peramb.reshape(sinks * spins, 2, block, peramb.shape[5])
    first = project_first(tau, place, block_owner, pieces, momenta.shape[0])
    result = project_second(tau, place, block_owner, first, across, momenta.shape[0])
    return result.reshape(1, sinks, spins, momenta.shape[0], 2, block, peramb.shape[5])


def from_behind(block, axis, distance):
    devices = range(lax.axis_size(axis))
    route = [((i - distance) % len(devices), i) for i in devices]
    return lax.ppermute(block, axis, route)


def with_halo(block, sides, width):
    for axis, dim in sides:
        count = lax.axis_size(axis)
        forward = [(i, i + 1) for i in range(count - 1)]
        forward.append((count - 1, 0))
        backward = [(target, source) for source, target in forward]
        low = lax.ppermute(
            lax.slice_in_dim(block, block.shape[dim] - width, None, axis=dim), axis, forward
        )
        high = lax.ppermute(lax.slice_in_dim(block, 0, width, axis=dim), axis, backward)
        block = jnp.concatenate([low, block, high], axis=dim)
    return block


def along(field, direction, sense):
    width = field.shape[-1]
    column = lax.broadcasted_iota(jnp.int32, (width,), 0) % LX
    if direction == 0:
        if sense > 0:
            return jnp.where(column == LX - 1, jnp.roll(field, LX - 1, -1), jnp.roll(field, -1, -1))
        return jnp.where(column == 0, jnp.roll(field, 1 - LX, -1), jnp.roll(field, 1, -1))
    return jnp.roll(field, -sense * LX, -1)


def link_times(link_re, link_im, field_re, field_im, dagger):
    result_re = []
    result_im = []
    for target in range(3):
        summed_re = jnp.zeros_like(field_re[0])
        summed_im = jnp.zeros_like(field_re[0])
        for source in range(3):
            if dagger:
                entry_re = link_re[source, target][None]
                entry_im = -link_im[source, target][None]
            else:
                entry_re = link_re[target, source][None]
                entry_im = link_im[target, source][None]
            summed_re = summed_re + entry_re * field_re[source] - entry_im * field_im[source]
            summed_im = summed_im + entry_re * field_im[source] + entry_im * field_re[source]
        result_re.append(summed_re)
        result_im.append(summed_im)
    return (jnp.stack(result_re), jnp.stack(result_im))


def chebyshev(initial, operate):
    current = operate(initial)
    following = 2.0 * operate(current) - initial
    return following


def general_device(eigvecs, links, peramb, block_owner, momenta):
    vectors = eigvecs[0]
    links_here = links[0]
    block = vectors.shape[2]
    layers = vectors.shape[3]
    plane = vectors.shape[4]
    site_count = lax.axis_size("site")
    group_count = lax.axis_size("vec")
    site_rank = lax.axis_index("site")
    group_rank = lax.axis_index("vec")
    portion = plane // group_count
    top_plane = links_here[2, :, :, :, layers - 1 :, :]
    below = from_behind(top_plane, "site", 1)
    behind_links = jnp.concatenate([below, links_here[2, :, :, :, : layers - 1, :]], axis=3)
    back_links = []
    for direction in range(2):
        back_links.append(
            (
                along(links_here[direction, 0], direction, -1),
                along(links_here[direction, 1], direction, -1),
            )
        )
    back_links.append((behind_links[0], behind_links[1]))

    def operate(field):
        padded = with_halo(field, (("site", 3),), 1)
        total_re = jnp.zeros_like(field[0])
        total_im = jnp.zeros_like(field[0])
        for direction in range(3):
            if direction < 2:
                ahead = along(field, direction, 1)
                behind = along(field, direction, -1)
            else:
                ahead = padded[:, :, :, 2:]
                behind = padded[:, :, :, :-2]
            forward = link_times(
                links_here[direction, 0], links_here[direction, 1], ahead[0], ahead[1], False
            )
            backward = link_times(
                back_links[direction][0], back_links[direction][1], behind[0], behind[1], True
            )
            total_re = total_re + forward[0] + backward[0]
            total_im = total_im + forward[1] + backward[1]
        return jnp.stack([total_re, total_im]) * (-1.0 / 6.0)

    filtered = chebyshev(vectors, operate).astype(jnp.bfloat16)
    received = lax.all_to_all(filtered, "vec", split_axis=4, concat_axis=2, tiled=True)
    grouped = received.reshape(2, 3, group_count, block, layers, portion)
    ranks = jnp.arange(group_count, dtype=jnp.int32)
    inverse = jnp.sum(
        ranks[:, None] * (block_owner[:, None] == ranks[None, :]).astype(jnp.int32), axis=0
    )
    ordered = jnp.take(grouped, inverse, axis=2).reshape(2, 3, group_count * block, layers, portion)
    nvec = group_count * block
    flat = group_rank * portion + lax.broadcasted_iota(jnp.int32, (layers, portion), 1)
    depth = site_rank * layers + lax.broadcasted_iota(jnp.int32, (layers, portion), 0)
    theta = phase_angle(momenta, flat % LX, flat // LX, depth, layers * site_count)
    values = ordered.astype(jnp.float32)
    cosine = jnp.cos(theta)[:, None, None]
    sine = jnp.sin(theta)[:, None, None]
    shift_re = cosine * values[0] + sine * values[1]
    shift_im = cosine * values[1] - sine * values[0]
    shifted = jnp.stack([shift_re, shift_im], axis=1).astype(jnp.bfloat16)
    products = jnp.einsum(
        "acizs,pbckzs->aipbk", ordered, shifted, preferred_element_type=jnp.float32
    )
    real = products[0, :, :, 0] + products[1, :, :, 1]
    imag = products[0, :, :, 1] - products[1, :, :, 0]
    momentum_count = momenta.shape[0]
    partial_sum = jnp.stack([real, imag], axis=2).reshape(nvec, momentum_count * 2 * nvec)
    tau = peramb[0]
    tau_rows = tau.reshape(-1, nvec)
    summed = lax.psum(partial_sum, ("site", "vec")).astype(jnp.bfloat16)
    joined = jnp.dot(tau_rows, summed, preferred_element_type=jnp.float32)
    sinks = tau.shape[0]
    spins = tau.shape[1]
    layout = joined.reshape(sinks, spins, 2, block, momentum_count, 2, nvec)
    real_part = layout[:, :, 0, :, :, 0] - layout[:, :, 1, :, :, 1]
    imag_part = layout[:, :, 0, :, :, 1] + layout[:, :, 1, :, :, 0]
    stacked = jnp.stack([real_part, imag_part], axis=0)
    result = jnp.transpose(stacked, (1, 2, 4, 0, 3, 5))
    return result[None].astype(jnp.bfloat16)


def choose(eigvecs, links, peramb, block_owner, momenta):
    block, layers, plane = eigvecs.shape[3:]
    sites, groups = lax.axis_size("site"), lax.axis_size("vec")
    fits = layers == 1 and plane == LX * LY == 4 * LANES and sites == 4 and groups == 2
    fits = fits and block == sites * sum(CHUNKS) and (2 * block) % (32 * sites) == 0 and block % (2 * block // sites) == 0
    device = per_device if fits else general_device
    return device(eigvecs, links, peramb, block_owner, momenta)


def solution(mesh):
    placed = (
        P(("cfg", "tslice"), None, None, "vec", "site", None),
        P(("cfg", "tslice"), None, None, None, None, "site", None),
        P(("cfg", "tslice"), "site", None, None, "vec", None),
        P(),
        P(),
    )
    return jax.shard_map(
        choose,
        mesh=mesh,
        in_specs=placed,
        out_specs=P(("cfg", "tslice"), "site", None, None, None, "vec", None),
        check_vma=False,
    )
```

```python
import functools
import math

import jax
import jax.numpy as jnp
from jax import lax
from jax.experimental import pallas as pl
from jax.experimental.pallas import tpu as pltpu
from jax.sharding import PartitionSpec as P


LX = 32
LY = 16
LANES = 128

two_pi = 2.0 * math.pi

CHUNKS = (16, 16, 16)


def phase_angle(momenta, across, upward, depth, extent):
    return two_pi * (
        (momenta[:, 0, None, None] * across[None]).astype(jnp.float32) / LX
        + (momenta[:, 1, None, None] * upward[None]).astype(jnp.float32) / LY
        + (momenta[:, 2, None, None] * depth[None]).astype(jnp.float32) / extent
    )


VMEM = pl.BlockSpec(memory_space=pltpu.VMEM)
SMEM = pl.BlockSpec(memory_space=pltpu.SMEM)
ANY = pl.BlockSpec(memory_space=pl.ANY)
GRANT = pltpu.CompilerParams(vmem_limit_bytes=16 * 2**20)


class Shifts:
    def __init__(self):
        lane = lax.broadcasted_iota(jnp.int32, (8, LANES), 1)
        row = lax.broadcasted_iota(jnp.int32, (8, LANES), 0) % 4
        column = lane % LX
        self.x_last = column == LX - 1
        self.x_first = column == 0
        self.y_high = lane >= LANES - LX
        self.y_low = lane < LX
        self.row_last = row == 3
        self.row_first = row == 0

    def ahead_x(self, v):
        return jnp.where(self.x_last, pltpu.roll(v, LX - 1, 1), pltpu.roll(v, LANES - 1, 1))

    def behind_x(self, v):
        return jnp.where(self.x_first, pltpu.roll(v, LANES - LX + 1, 1), pltpu.roll(v, 1, 1))

    def ahead_y(self, v):
        a = pltpu.roll(v, LANES - LX, 1)
        wrapped = jnp.where(self.row_last, pltpu.roll(a, 3, 0), pltpu.roll(a, 7, 0))
        return jnp.where(self.y_high, wrapped, a)

    def behind_y(self, v):
        a = pltpu.roll(v, LX, 1)
        wrapped = jnp.where(self.row_first, pltpu.roll(a, 5, 0), pltpu.roll(a, 1, 0))
        return jnp.where(self.y_low, wrapped, a)


def tables_kernel(*refs):
    table_ref = refs[-1]
    shifts = Shifts()
    scale = jnp.float32(-1.0 / 6.0)
    size = refs[0].shape[0]
    links = [ref[ref.shape[0] - size :].astype(jnp.float32) for ref in refs[:-1]]
    count = len(links)

    def entry(plane, direction, part, row, col):
        e = direction * 18 + part * 9 + row * 3 + col
        value = links[plane % count][4 * e : 4 * e + 4] * scale
        return jnp.concatenate([value, value], axis=0)

    for plane in range(count):
        for direction in range(3):
            for target in range(3):
                for source in range(3):
                    slot = (2 * direction) * 18 + (target * 3 + source) * 2
                    table_ref[plane, slot] = entry(plane, direction, 0, target, source)
                    table_ref[plane, slot + 1] = entry(plane, direction, 1, target, source)
                    slot = (2 * direction + 1) * 18 + (target * 3 + source) * 2
                    below = plane + 1 if direction == 2 else plane
                    re = entry(below, direction, 0, source, target)
                    im = entry(below, direction, 1, source, target)
                    if direction < 2:
                        move = shifts.behind_x if direction == 0 else shifts.behind_y
                        re, im = move(re), move(im)
                    table_ref[plane, slot] = re
                    table_ref[plane, slot + 1] = -im


def link_tables(links):
    return pl.pallas_call(
        tables_kernel,
        out_shape=pltpu.VMEM((len(links), 108, 8, LANES), jnp.float32),
        in_specs=[VMEM] * len(links),
        out_specs=VMEM,
        compiler_params=GRANT,
        name="link_tables",
    )(*links)


def pack_kernel(sites, chunk, place_ref, own_ref, *refs):
    outs = refs[1 - sites :]
    rows = CHUNKS[chunk] * 4
    for d in range(1, sites):
        start = row_of(lax.rem(place_ref[0] + d, sites), own_ref.shape[1] // sites, chunk)
        out = outs[d - 1]
        for c in range(6):
            out[c * rows : (c + 1) * rows] = own_ref[c, pl.ds(start, rows), :].astype(jnp.bfloat16)
        if out.shape[0] > 6 * rows:
            out[6 * rows :] = refs[0][...].astype(jnp.bfloat16)


def row_of(slot, rows_per_slot, chunk):
    return pl.multiple_of(slot * rows_per_slot + 4 * sum(CHUNKS[:chunk]), 32)


def pack(own, place, chunk, sites, links, after):
    extra = [links] if chunk == 0 else []
    length = 24 * CHUNKS[chunk] + sum(e.shape[0] for e in extra)
    return pl.pallas_call(
        functools.partial(pack_kernel, sites, chunk),
        out_shape=[pltpu.VMEM((length, LANES), jnp.bfloat16)] * (sites - 1),
        in_specs=[SMEM] + [VMEM] * (1 + len(extra)) + [ANY] * len(after),
        out_specs=[VMEM] * (sites - 1),
        compiler_params=GRANT,
    )(place, own, *extra, *after)


def filter_kernel(sites, chunk, place_ref, *refs):
    fields, table_ref = refs[:sites], refs[sites]
    outs, t1_ref = refs[-1 - sites : -1], refs[-1]
    shifts = Shifts()
    rows = CHUNKS[chunk] * 4
    home = row_of(place_ref[0], fields[0].shape[1] // sites, chunk)

    def hop(plane, here, ahead_z, behind_z):
        count = len(here(0))
        total = [[None] * count for _ in range(6)]
        moves = (shifts.ahead_x, shifts.behind_x, shifts.ahead_y, shifts.behind_y, None, None)
        for direction in range(6):
            if direction < 4:
                field = [[moves[direction](v) for v in here(c)] for c in range(6)]
            else:
                take = ahead_z if direction == 4 else behind_z
                field = [take(c) for c in range(6)]
            for target in range(3):
                for source in range(3):
                    slot = direction * 18 + (target * 3 + source) * 2
                    re = table_ref[plane, slot]
                    im = table_ref[plane, slot + 1]
                    for n in range(count):
                        f_re, f_im = field[source][n], field[3 + source][n]
                        add_re = re * f_re - im * f_im
                        add_im = re * f_im + im * f_re
                        if total[target][n] is None:
                            total[target][n], total[3 + target][n] = add_re, add_im
                        else:
                            total[target][n] = total[target][n] + add_re
                            total[3 + target][n] = total[3 + target][n] + add_im
        return total

    def step(index, carry):
        base = pl.multiple_of(index * 16, 16)

        def start(plane):
            def read(c):
                ref = fields[plane % sites]
                if plane % sites == 0:
                    value = ref[c, pl.ds(pl.multiple_of(home + base, 16), 16), :]
                else:
                    value = ref[pl.ds(pl.multiple_of(c * rows + base, 16), 16), :].astype(jnp.float32)
                return [value[0:8], value[8:16]]

            return read

        def first(plane):
            return lambda c: [t1_ref[plane % sites, c, 0:8], t1_ref[plane % sites, c, 8:16]]

        for plane in range(sites):
            out = hop(plane, start(plane), start(plane - 1), start(plane + 1))
            for c in range(6):
                for n in range(2):
                    t1_ref[plane, c, 8 * n : 8 * n + 8] = out[c][n]
        for plane in range(sites):
            out = hop(plane, first(plane), first(plane - 1), first(plane + 1))
            for c in range(6):
                value = 2.0 * jnp.concatenate(out[c], axis=0)
                outs[plane][c, pl.ds(base, 16), :] = value.astype(jnp.bfloat16)
        return carry

    lax.fori_loop(0, rows // 16, step, 0)


def filter_chunk(own, place, chunk, received, table, after):
    sites = len(received) + 1
    rows = CHUNKS[chunk] * 4
    return pl.pallas_call(
        functools.partial(filter_kernel, sites, chunk),
        out_shape=[pltpu.VMEM((6, rows, LANES), jnp.bfloat16)] * sites,
        in_specs=[SMEM] + [VMEM] * (sites + 1) + [ANY] * len(after),
        out_specs=[VMEM] * sites,
        scratch_shapes=[pltpu.VMEM((sites, 6, 16, LANES), jnp.float32)],
        cost_estimate=pl.CostEstimate(
            flops=432 * 2 * sites * rows * LANES, bytes_accessed=6 * rows * LANES * 4 * sites, transcendentals=0),
        compiler_params=GRANT,
    )(place, own, *received, table, *after)


def finish_kernel(sites, chunk, place_ref, own_ref, *refs):
    hops = refs[:sites]
    cosine_ref, sine_ref = refs[sites : sites + 2]
    filtered_ref, shifted_ref, work_ref = refs[-3:]
    vectors = CHUNKS[chunk]
    momenta = cosine_ref.shape[0]
    for d in range(sites):
        slot = lax.rem(place_ref[0] + d, sites)
        start = row_of(slot, own_ref.shape[1] // sites, chunk)
        for c in range(6):
            work_ref[d, c] = hops[d][c].astype(jnp.float32) - own_ref[c, pl.ds(start, 4 * vectors), :]
        for color in range(3):
            for row in range(4):
                at = slice((color * 4 + row) * LANES, (color * 4 + row + 1) * LANES)
                re = work_ref[d, color, pl.ds(row, vectors, stride=4), :].astype(jnp.bfloat16)
                im = work_ref[d, 3 + color, pl.ds(row, vectors, stride=4), :].astype(jnp.bfloat16)
                filtered_ref[slot, 0, :, at] = re
                filtered_ref[slot, 1, :, at] = im
                re, im = re.astype(jnp.float32), im.astype(jnp.float32)
                for p in range(momenta):
                    cosine = cosine_ref[p, row : row + 1, :]
                    sine = sine_ref[p, row : row + 1, :]
                    shifted_ref[p, slot, 0, :, at] = (cosine * re + sine * im).astype(jnp.bfloat16)
                    shifted_ref[p, slot, 1, :, at] = (cosine * im - sine * re).astype(jnp.bfloat16)


def finish(own, place, chunk, hops, cosine, sine, after):
    sites, momenta, vectors = len(hops), cosine.shape[0], CHUNKS[chunk]
    shapes = ((sites, 2, vectors, 12 * LANES), (momenta, sites, 2, vectors, 12 * LANES))
    return pl.pallas_call(
        functools.partial(finish_kernel, sites, chunk),
        out_shape=[pltpu.VMEM(shape, jnp.bfloat16) for shape in shapes],
        in_specs=[SMEM] + [VMEM] * (sites + 3) + [ANY] * len(after),
        out_specs=[VMEM, VMEM],
        scratch_shapes=[pltpu.VMEM((sites, 6, 4 * vectors, LANES), jnp.float32)],
        cost_estimate=pl.CostEstimate(
            flops=20 * sites * 24 * vectors * LANES, bytes_accessed=sites * 24 * vectors * LANES * 12,
            transcendentals=0),
        compiler_params=GRANT,
    )(place, own, *hops, cosine, sine, *after)


def fill_left(left_ref, chunks):
    slots, _, _, depth = chunks[0].shape
    for n, ref in enumerate(chunks):
        for slot in range(slots):
            at = slot * sum(CHUNKS) + sum(CHUNKS[:n])
            for part in range(2):
                left_ref[at : at + CHUNKS[n], part * depth : (part + 1) * depth] = ref[slot, part]


def multiply(left_ref, right_ref, total_ref, place_ref, outs):
    segments, rows, _ = total_ref.shape
    for p in range(right_ref.shape[0]):
        product = lax.dot_general(
            left_ref[...], right_ref[p], (((1,), (1,)), ((), ())), preferred_element_type=jnp.float32)
        width = product.shape[1]
        for s in range(segments):
            total_ref[s, :, p * width : (p + 1) * width] = product[s * rows : (s + 1) * rows]
    for d in range(segments):
        outs[d][...] = total_ref[lax.rem(place_ref[0] + d, segments)].astype(outs[d].dtype)


def own_kernel(segments, place_ref, *refs):
    chunks = len(CHUNKS)
    own, shifted = refs[:chunks], refs[chunks : 2 * chunks]
    outs = refs[2 * chunks : 2 * chunks + segments]
    right_ref, left_ref, total_ref = refs[2 * chunks + segments :]
    slots, _, _, depth = own[0].shape
    block = left_ref.shape[0]
    fill_left(left_ref, own)
    for p in range(right_ref.shape[0]):
        for n, ref in enumerate(shifted):
            for slot in range(slots):
                re, im = ref[p, slot, 0], ref[p, slot, 1]
                at = slot * sum(CHUNKS) + sum(CHUNKS[:n])
                low, high = slice(at, at + CHUNKS[n]), slice(block + at, block + at + CHUNKS[n])
                right_ref[p, low, :depth] = re
                right_ref[p, low, depth:] = im
                right_ref[p, high, :depth] = im
                right_ref[p, high, depth:] = -re
    multiply(left_ref, right_ref, total_ref, place_ref, outs)


def other_kernel(segments, place_ref, *refs):
    chunks = len(CHUNKS)
    other, right_ref = refs[:chunks], refs[chunks]
    outs = refs[chunks + 1 : chunks + 1 + segments]
    left_ref, total_ref = refs[chunks + 1 + segments :]
    fill_left(left_ref, other)
    multiply(left_ref, right_ref, total_ref, place_ref, outs)


def elementals(place, left, shifted, right, segments):
    _, _, _, depth = left[0].shape
    block = segments * sum(CHUNKS)
    own = right is None
    momenta = shifted[0].shape[0] if own else right.shape[0]
    rows, columns = block // segments, momenta * 2 * block
    shapes = [pltpu.VMEM((rows, columns), jnp.float32 if d == 0 else jnp.bfloat16) for d in range(segments)]
    if own:
        shapes.append(pltpu.VMEM((momenta, 2 * block, 2 * depth), jnp.bfloat16))
    operands = [*left, *shifted] if own else [*left, right]
    return pl.pallas_call(
        functools.partial(own_kernel if own else other_kernel, segments),
        out_shape=shapes,
        in_specs=[SMEM] + [VMEM] * len(operands),
        out_specs=[VMEM] * len(shapes),
        scratch_shapes=[
            pltpu.VMEM((block, 2 * depth), jnp.bfloat16),
            pltpu.VMEM((segments, rows, columns), jnp.float32),
        ],
        cost_estimate=pl.CostEstimate(
            flops=2 * block * columns * 2 * depth, bytes_accessed=8 * block * depth, transcendentals=0),
        compiler_params=GRANT,
        name="elementals_own" if own else "elementals_other",
    )(place, *operands)


def fill_right(right_ref, pieces, across, place_ref, owner_ref):
    sites = len(pieces)
    momenta, nvec = right_ref.shape[0], right_ref.shape[1] // 2
    block = nvec // 2
    half = block - LANES
    rows = block // sites
    v = lax.rem(place_ref[1] + across, 2)
    leads = owner_ref[v] == 0

    def tiles(value):
        zeros = jnp.zeros((value.shape[0], LANES - half), value.dtype)
        first = jnp.concatenate([value[:, :LANES], value[:, LANES:], zeros], axis=1)
        second = jnp.concatenate([value[:, half:], zeros, value[:, :half]], axis=1)
        return jnp.where(leads, first, second)

    for up, piece in enumerate(pieces):
        z = lax.rem(place_ref[0] + up, sites)
        for part, owner in ((0, owner_ref[v]), (1, owner_ref[1 - v])):
            row = pl.multiple_of(owner * block + z * rows, 16)
            low = pl.multiple_of(nvec + owner * block + z * rows, 16)
            for p in range(momenta):
                value = piece[part * rows : (part + 1) * rows, p * 2 * block : (p + 1) * 2 * block]
                re, im = tiles(value[:, :block]), tiles(value[:, block:])
                right_ref[p, pl.ds(row, rows), : 2 * LANES] = re
                right_ref[p, pl.ds(row, rows), 2 * LANES :] = im
                right_ref[p, pl.ds(low, rows), : 2 * LANES] = -im
                right_ref[p, pl.ds(low, rows), 2 * LANES :] = re


def first_kernel(sites, place_ref, owner_ref, tau_ref, *refs):
    pieces, (out_ref, right_ref) = refs[:sites], refs[sites:]
    fill_right(right_ref, pieces, 0, place_ref, owner_ref)

    def step(n, carry):
        left = jnp.concatenate([tau_ref[n, 0], tau_ref[n, 1]], axis=1)
        for p in range(right_ref.shape[0]):
            product = jnp.dot(left, right_ref[p], preferred_element_type=jnp.float32)
            out_ref[n, p] = product.astype(jnp.bfloat16)
        return carry

    lax.fori_loop(0, tau_ref.shape[0], step, 0)


def second_kernel(sites, place_ref, owner_ref, tau_ref, first_ref, *refs):
    pieces, (out_ref, right_ref) = refs[:sites], refs[sites:]

    @pl.when(pl.program_id(0) == 0)
    def assemble():
        fill_right(right_ref, pieces, 1, place_ref, owner_ref)

    leads = owner_ref[place_ref[1]] == 0
    left = jnp.concatenate([tau_ref[0, 0], tau_ref[0, 1]], axis=1)
    for p in range(right_ref.shape[0]):
        product = jnp.dot(left, right_ref[p], preferred_element_type=jnp.float32).astype(jnp.bfloat16)
        for c in range(2):
            at = 2 * c * LANES
            mine, theirs = first_ref[0, p, :, at : at + LANES], product[:, at : at + LANES]
            middle = first_ref[0, p, :, at + LANES : at + 2 * LANES] + product[:, at + LANES : at + 2 * LANES]
            out_ref[0, p, c, :, :LANES] = jnp.where(leads, mine, theirs)
            out_ref[0, p, c, :, LANES : 2 * LANES] = middle
            out_ref[0, p, c, :, 2 * LANES :] = jnp.where(leads, theirs, mine)


def project_first(tau, place, owner, pieces, momenta):
    outer, _, rows, nvec = tau.shape
    return pl.pallas_call(
        functools.partial(first_kernel, len(pieces)),
        out_shape=pltpu.VMEM((outer, momenta, rows, 4 * LANES), jnp.bfloat16),
        in_specs=[SMEM, SMEM] + [VMEM] * (1 + len(pieces)),
        out_specs=VMEM,
        scratch_shapes=[pltpu.VMEM((momenta, 2 * nvec, 4 * LANES), jnp.bfloat16)],
        cost_estimate=pl.CostEstimate(
            flops=2 * outer * rows * 2 * nvec * nvec * momenta, bytes_accessed=outer * rows * nvec * 8,
            transcendentals=0),
        compiler_params=GRANT,
        name="project_first",
    )(place, owner, tau, *pieces)


def project_second(tau, place, owner, first, pieces, momenta):
    outer, _, rows, nvec = tau.shape
    return pl.pallas_call(
        functools.partial(second_kernel, len(pieces)),
        grid=(outer,),
        out_shape=jax.ShapeDtypeStruct((outer, momenta, 2, rows, nvec), jnp.bfloat16),
        in_specs=[SMEM, SMEM, pl.BlockSpec((1, 2, rows, nvec), lambda i: (i, 0, 0, 0)),
                  pl.BlockSpec((1, *first.shape[1:]), lambda i: (i, 0, 0, 0))] + [VMEM] * len(pieces),
        out_specs=pl.BlockSpec((1, momenta, 2, rows, nvec), lambda i: (i, 0, 0, 0, 0)),
        scratch_shapes=[pltpu.VMEM((momenta, 2 * nvec, 4 * LANES), jnp.bfloat16)],
        cost_estimate=pl.CostEstimate(
            flops=2 * outer * rows * 2 * nvec * nvec * momenta, bytes_accessed=outer * rows * nvec * 12,
            transcendentals=0),
        compiler_params=GRANT,
        name="project_second",
    )(place, owner, tau, first, *pieces)


def from_place(block, up, across):
    sites, groups = lax.axis_size("site"), lax.axis_size("vec")
    route = []
    for z in range(sites):
        for v in range(groups):
            route.append((((z + up) % sites) * groups + (v + across) % groups, z * groups + v))
    return lax.ppermute(block, ("site", "vec"), route)


ORDER = (("filter", 0), ("filter", 1), ("finish", 0), ("filter", 2), ("finish", 1), ("finish", 2))


def per_device(eigvecs, links, peramb, block_owner, momenta):
    sites = lax.axis_size("site")
    site, group = lax.axis_index("site"), lax.axis_index("vec")
    block = eigvecs.shape[3]
    own = eigvecs.reshape(6, block * 4, LANES)
    own_links = links.reshape(216, LANES)
    place = jnp.stack([site, group]).astype(jnp.int32)

    received, packed = [], []
    for chunk in range(len(CHUNKS)):
        after = packed[:1]
        if chunk == 1:
            after = received[0][:1]
        if chunk == 2:
            after = [*received[0], packed[0]]
        packed = pack(own, place, chunk, sites, own_links, after)
        received.append([from_place(packed[d - 1], -d, 0) for d in range(1, sites)])

    flat = lax.broadcasted_iota(jnp.int32, (4, LANES), 0) * LANES + lax.broadcasted_iota(jnp.int32, (4, LANES), 1)
    theta = phase_angle(momenta, flat % LX, flat // LX, jnp.full_like(flat, site), sites)
    cosine, sine = jnp.cos(theta), jnp.sin(theta)

    table = link_tables([own_links] + received[0])
    hops, filtered, shifted, other = {}, {}, {}, {}
    last = None
    for kind, chunk in ORDER:
        after = [] if last is None else [last]
        if kind == "filter":
            out = filter_chunk(own, place, chunk, received[chunk], table, after)
            hops[chunk] = [out[0]] + [from_place(out[d], d, 0) for d in range(1, sites)]
            last = out[0]
        else:
            f, s = finish(own, place, chunk, hops[chunk], cosine, sine, after)
            other[chunk] = from_place(f, 0, 1)
            filtered[chunk], shifted[chunk] = f, s
            last = s
    filtered, shifted, other = ([group_of[n] for n in range(len(CHUNKS))] for group_of in (filtered, shifted, other))

    *parts, right = elementals(place, filtered, shifted, None, sites)
    sent = [from_place(parts[d], -d, 0) for d in range(1, sites)]
    own_sum = functools.reduce(lambda total, part: total + part.astype(jnp.float32), sent, parts[0])
    parts = elementals(place, other, None, right, sites)
    sent = [from_place(parts[d], -d, 0) for d in range(1, sites)]
    other_sum = functools.reduce(lambda total, part: total + part.astype(jnp.float32), sent, parts[0])
    mine = jnp.concatenate([own_sum, other_sum], axis=0).astype(jnp.bfloat16)

    across = [from_place(mine, 0, 1)]
    pieces = [mine] + [from_place(mine, up, 0) for up in range(1, sites)]
    across += [from_place(piece, 0, 1) for piece in pieces[1:]]
    sinks, spins = peramb.shape[1], peramb.shape[2]
    tau = peramb.reshape(sinks * spins, 2, block, peramb.shape[5])
    first = project_first(tau, place, block_owner, pieces, momenta.shape[0])
    result = project_second(tau, place, block_owner, first, across, momenta.shape[0])
    return result.reshape(1, sinks, spins, momenta.shape[0], 2, block, peramb.shape[5])


def from_behind(block, axis, distance):
    devices = range(lax.axis_size(axis))
    route = [((i - distance) % len(devices), i) for i in devices]
    return lax.ppermute(block, axis, route)


def with_halo(block, sides, width):
    for axis, dim in sides:
        count = lax.axis_size(axis)
        forward = [(i, i + 1) for i in range(count - 1)]
        forward.append((count - 1, 0))
        backward = [(target, source) for source, target in forward]
        low = lax.ppermute(
            lax.slice_in_dim(block, block.shape[dim] - width, None, axis=dim), axis, forward
        )
        high = lax.ppermute(lax.slice_in_dim(block, 0, width, axis=dim), axis, backward)
        block = jnp.concatenate([low, block, high], axis=dim)
    return block


def along(field, direction, sense):
    width = field.shape[-1]
    column = lax.broadcasted_iota(jnp.int32, (width,), 0) % LX
    if direction == 0:
        if sense > 0:
            return jnp.where(column == LX - 1, jnp.roll(field, LX - 1, -1), jnp.roll(field, -1, -1))
        return jnp.where(column == 0, jnp.roll(field, 1 - LX, -1), jnp.roll(field, 1, -1))
    return jnp.roll(field, -sense * LX, -1)


def link_times(link_re, link_im, field_re, field_im, dagger):
    result_re = []
    result_im = []
    for target in range(3):
        summed_re = jnp.zeros_like(field_re[0])
        summed_im = jnp.zeros_like(field_re[0])
        for source in range(3):
            if dagger:
                entry_re = link_re[source, target][None]
                entry_im = -link_im[source, target][None]
            else:
                entry_re = link_re[target, source][None]
                entry_im = link_im[target, source][None]
            summed_re = summed_re + entry_re * field_re[source] - entry_im * field_im[source]
            summed_im = summed_im + entry_re * field_im[source] + entry_im * field_re[source]
        result_re.append(summed_re)
        result_im.append(summed_im)
    return (jnp.stack(result_re), jnp.stack(result_im))


def chebyshev(initial, operate):
    current = operate(initial)
    following = 2.0 * operate(current) - initial
    return following


def general_device(eigvecs, links, peramb, block_owner, momenta):
    vectors = eigvecs[0]
    links_here = links[0]
    block = vectors.shape[2]
    layers = vectors.shape[3]
    plane = vectors.shape[4]
    site_count = lax.axis_size("site")
    group_count = lax.axis_size("vec")
    site_rank = lax.axis_index("site")
    group_rank = lax.axis_index("vec")
    portion = plane // group_count
    top_plane = links_here[2, :, :, :, layers - 1 :, :]
    below = from_behind(top_plane, "site", 1)
    behind_links = jnp.concatenate([below, links_here[2, :, :, :, : layers - 1, :]], axis=3)
    back_links = []
    for direction in range(2):
        back_links.append(
            (
                along(links_here[direction, 0], direction, -1),
                along(links_here[direction, 1], direction, -1),
            )
        )
    back_links.append((behind_links[0], behind_links[1]))

    def operate(field):
        padded = with_halo(field, (("site", 3),), 1)
        total_re = jnp.zeros_like(field[0])
        total_im = jnp.zeros_like(field[0])
        for direction in range(3):
            if direction < 2:
                ahead = along(field, direction, 1)
                behind = along(field, direction, -1)
            else:
                ahead = padded[:, :, :, 2:]
                behind = padded[:, :, :, :-2]
            forward = link_times(
                links_here[direction, 0], links_here[direction, 1], ahead[0], ahead[1], False
            )
            backward = link_times(
                back_links[direction][0], back_links[direction][1], behind[0], behind[1], True
            )
            total_re = total_re + forward[0] + backward[0]
            total_im = total_im + forward[1] + backward[1]
        return jnp.stack([total_re, total_im]) * (-1.0 / 6.0)

    filtered = chebyshev(vectors, operate).astype(jnp.bfloat16)
    received = lax.all_to_all(filtered, "vec", split_axis=4, concat_axis=2, tiled=True)
    grouped = received.reshape(2, 3, group_count, block, layers, portion)
    ranks = jnp.arange(group_count, dtype=jnp.int32)
    inverse = jnp.sum(
        ranks[:, None] * (block_owner[:, None] == ranks[None, :]).astype(jnp.int32), axis=0
    )
    ordered = jnp.take(grouped, inverse, axis=2).reshape(2, 3, group_count * block, layers, portion)
    nvec = group_count * block
    flat = group_rank * portion + lax.broadcasted_iota(jnp.int32, (layers, portion), 1)
    depth = site_rank * layers + lax.broadcasted_iota(jnp.int32, (layers, portion), 0)
    theta = phase_angle(momenta, flat % LX, flat // LX, depth, layers * site_count)
    values = ordered.astype(jnp.float32)
    cosine = jnp.cos(theta)[:, None, None]
    sine = jnp.sin(theta)[:, None, None]
    shift_re = cosine * values[0] + sine * values[1]
    shift_im = cosine * values[1] - sine * values[0]
    shifted = jnp.stack([shift_re, shift_im], axis=1).astype(jnp.bfloat16)
    products = jnp.einsum(
        "acizs,pbckzs->aipbk", ordered, shifted, preferred_element_type=jnp.float32
    )
    real = products[0, :, :, 0] + products[1, :, :, 1]
    imag = products[0, :, :, 1] - products[1, :, :, 0]
    momentum_count = momenta.shape[0]
    partial_sum = jnp.stack([real, imag], axis=2).reshape(nvec, momentum_count * 2 * nvec)
    tau = peramb[0]
    tau_rows = tau.reshape(-1, nvec)
    summed = lax.psum(partial_sum, ("site", "vec")).astype(jnp.bfloat16)
    joined = jnp.dot(tau_rows, summed, preferred_element_type=jnp.float32)
    sinks = tau.shape[0]
    spins = tau.shape[1]
    layout = joined.reshape(sinks, spins, 2, block, momentum_count, 2, nvec)
    real_part = layout[:, :, 0, :, :, 0] - layout[:, :, 1, :, :, 1]
    imag_part = layout[:, :, 0, :, :, 1] + layout[:, :, 1, :, :, 0]
    stacked = jnp.stack([real_part, imag_part], axis=0)
    result = jnp.transpose(stacked, (1, 2, 4, 0, 3, 5))
    return result[None].astype(jnp.bfloat16)


def choose(eigvecs, links, peramb, block_owner, momenta):
    block, layers, plane = eigvecs.shape[3:]
    sites, groups = lax.axis_size("site"), lax.axis_size("vec")
    fits = layers == 1 and plane == LX * LY == 4 * LANES and sites == 4 and groups == 2
    fits = fits and block == sites * sum(CHUNKS) and LANES < block < 2 * LANES and (2 * block) % (32 * sites) == 0 and block % (2 * block // sites) == 0
    device = per_device if fits else general_device
    return device(eigvecs, links, peramb, block_owner, momenta)


def solution(mesh):
    placed = (
        P(("cfg", "tslice"), None, None, "vec", "site", None),
        P(("cfg", "tslice"), None, None, None, None, "site", None),
        P(("cfg", "tslice"), "site", None, None, "vec", None),
        P(),
        P(),
    )
    return jax.shard_map(
        choose,
        mesh=mesh,
        in_specs=placed,
        out_specs=P(("cfg", "tslice"), "site", None, None, None, "vec", None),
        check_vma=False,
    )
```

```python
import functools
import math

import jax
import jax.numpy as jnp
from jax import lax
from jax.experimental import pallas as pl
from jax.experimental.pallas import tpu as pltpu
from jax.sharding import PartitionSpec as P


LX = 32
LY = 16
LANES = 128

two_pi = 2.0 * math.pi

CHUNKS = (16, 16, 16)


def phase_angle(momenta, across, upward, depth, extent):
    return two_pi * (
        (momenta[:, 0, None, None] * across[None]).astype(jnp.float32) / LX
        + (momenta[:, 1, None, None] * upward[None]).astype(jnp.float32) / LY
        + (momenta[:, 2, None, None] * depth[None]).astype(jnp.float32) / extent
    )


VMEM = pl.BlockSpec(memory_space=pltpu.VMEM)
SMEM = pl.BlockSpec(memory_space=pltpu.SMEM)
ANY = pl.BlockSpec(memory_space=pl.ANY)
GRANT = pltpu.CompilerParams(vmem_limit_bytes=16 * 2**20)


class Shifts:
    def __init__(self):
        lane = lax.broadcasted_iota(jnp.int32, (8, LANES), 1)
        row = lax.broadcasted_iota(jnp.int32, (8, LANES), 0) % 4
        column = lane % LX
        self.x_last = column == LX - 1
        self.x_first = column == 0
        self.y_high = lane >= LANES - LX
        self.y_low = lane < LX
        self.row_last = row == 3
        self.row_first = row == 0

    def ahead_x(self, v):
        return jnp.where(self.x_last, pltpu.roll(v, LX - 1, 1), pltpu.roll(v, LANES - 1, 1))

    def behind_x(self, v):
        return jnp.where(self.x_first, pltpu.roll(v, LANES - LX + 1, 1), pltpu.roll(v, 1, 1))

    def ahead_y(self, v):
        a = pltpu.roll(v, LANES - LX, 1)
        wrapped = jnp.where(self.row_last, pltpu.roll(a, 3, 0), pltpu.roll(a, 7, 0))
        return jnp.where(self.y_high, wrapped, a)

    def behind_y(self, v):
        a = pltpu.roll(v, LX, 1)
        wrapped = jnp.where(self.row_first, pltpu.roll(a, 5, 0), pltpu.roll(a, 1, 0))
        return jnp.where(self.y_low, wrapped, a)


def tables_kernel(*refs):
    table_ref = refs[-1]
    shifts = Shifts()
    scale = jnp.float32(-1.0 / 6.0)
    size = refs[0].shape[0]
    links = [ref[ref.shape[0] - size :].astype(jnp.float32) for ref in refs[:-1]]
    count = len(links)

    def entry(plane, direction, part, row, col):
        e = direction * 18 + part * 9 + row * 3 + col
        value = links[plane % count][4 * e : 4 * e + 4] * scale
        return jnp.concatenate([value, value], axis=0)

    for plane in range(count):
        for direction in range(3):
            for target in range(3):
                for source in range(3):
                    slot = (2 * direction) * 18 + (target * 3 + source) * 2
                    table_ref[plane, slot] = entry(plane, direction, 0, target, source)
                    table_ref[plane, slot + 1] = entry(plane, direction, 1, target, source)
                    slot = (2 * direction + 1) * 18 + (target * 3 + source) * 2
                    below = plane + 1 if direction == 2 else plane
                    re = entry(below, direction, 0, source, target)
                    im = entry(below, direction, 1, source, target)
                    if direction < 2:
                        move = shifts.behind_x if direction == 0 else shifts.behind_y
                        re, im = move(re), move(im)
                    table_ref[plane, slot] = re
                    table_ref[plane, slot + 1] = -im


def link_tables(links):
    return pl.pallas_call(
        tables_kernel,
        out_shape=pltpu.VMEM((len(links), 108, 8, LANES), jnp.float32),
        in_specs=[VMEM] * len(links),
        out_specs=VMEM,
        compiler_params=GRANT,
        name="link_tables",
    )(*links)


def pack_kernel(sites, chunk, place_ref, own_ref, *refs):
    outs = refs[1 - sites :]
    rows = CHUNKS[chunk] * 4
    for d in range(1, sites):
        start = row_of(lax.rem(place_ref[0] + d, sites), own_ref.shape[1] // sites, chunk)
        out = outs[d - 1]
        for c in range(6):
            out[c * rows : (c + 1) * rows] = own_ref[c, pl.ds(start, rows), :].astype(jnp.bfloat16)
        if out.shape[0] > 6 * rows:
            out[6 * rows :] = refs[0][...].astype(jnp.bfloat16)


def row_of(slot, rows_per_slot, chunk):
    return pl.multiple_of(slot * rows_per_slot + 4 * sum(CHUNKS[:chunk]), 32)


def pack(own, place, chunk, sites, links, after):
    extra = [links] if chunk == 0 else []
    length = 24 * CHUNKS[chunk] + sum(e.shape[0] for e in extra)
    return pl.pallas_call(
        functools.partial(pack_kernel, sites, chunk),
        out_shape=[pltpu.VMEM((length, LANES), jnp.bfloat16)] * (sites - 1),
        in_specs=[SMEM] + [VMEM] * (1 + len(extra)) + [ANY] * len(after),
        out_specs=[VMEM] * (sites - 1),
        compiler_params=GRANT,
    )(place, own, *extra, *after)


def filter_kernel(sites, chunk, place_ref, *refs):
    fields, table_ref = refs[:sites], refs[sites]
    outs, t1_ref = refs[-1 - sites : -1], refs[-1]
    shifts = Shifts()
    rows = CHUNKS[chunk] * 4
    home = row_of(place_ref[0], fields[0].shape[1] // sites, chunk)

    def hop(plane, here, ahead_z, behind_z):
        count = len(here(0))
        total = [[None] * count for _ in range(6)]
        moves = (shifts.ahead_x, shifts.behind_x, shifts.ahead_y, shifts.behind_y, None, None)
        for direction in range(6):
            if direction < 4:
                field = [[moves[direction](v) for v in here(c)] for c in range(6)]
            else:
                take = ahead_z if direction == 4 else behind_z
                field = [take(c) for c in range(6)]
            for target in range(3):
                for source in range(3):
                    slot = direction * 18 + (target * 3 + source) * 2
                    re = table_ref[plane, slot]
                    im = table_ref[plane, slot + 1]
                    for n in range(count):
                        f_re, f_im = field[source][n], field[3 + source][n]
                        add_re = re * f_re - im * f_im
                        add_im = re * f_im + im * f_re
                        if total[target][n] is None:
                            total[target][n], total[3 + target][n] = add_re, add_im
                        else:
                            total[target][n] = total[target][n] + add_re
                            total[3 + target][n] = total[3 + target][n] + add_im
        return total

    def step(index, carry):
        base = pl.multiple_of(index * 16, 16)

        def start(plane):
            def read(c):
                ref = fields[plane % sites]
                if plane % sites == 0:
                    value = ref[c, pl.ds(pl.multiple_of(home + base, 16), 16), :]
                else:
                    value = ref[pl.ds(pl.multiple_of(c * rows + base, 16), 16), :].astype(jnp.float32)
                return [value[0:8], value[8:16]]

            return read

        def first(plane):
            return lambda c: [t1_ref[plane % sites, c, 0:8], t1_ref[plane % sites, c, 8:16]]

        for plane in range(sites):
            out = hop(plane, start(plane), start(plane - 1), start(plane + 1))
            for c in range(6):
                for n in range(2):
                    t1_ref[plane, c, 8 * n : 8 * n + 8] = out[c][n]
        for plane in range(sites):
            out = hop(plane, first(plane), first(plane - 1), first(plane + 1))
            for c in range(6):
                value = 2.0 * jnp.concatenate(out[c], axis=0)
                outs[plane][c, pl.ds(base, 16), :] = value.astype(jnp.bfloat16)
        return carry

    lax.fori_loop(0, rows // 16, step, 0)


def filter_chunk(own, place, chunk, received, table, after):
    sites = len(received) + 1
    rows = CHUNKS[chunk] * 4
    return pl.pallas_call(
        functools.partial(filter_kernel, sites, chunk),
        out_shape=[pltpu.VMEM((6, rows, LANES), jnp.bfloat16)] * sites,
        in_specs=[SMEM] + [VMEM] * (sites + 1) + [ANY] * len(after),
        out_specs=[VMEM] * sites,
        scratch_shapes=[pltpu.VMEM((sites, 6, 16, LANES), jnp.float32)],
        cost_estimate=pl.CostEstimate(
            flops=432 * 2 * sites * rows * LANES, bytes_accessed=6 * rows * LANES * 4 * sites, transcendentals=0),
        compiler_params=GRANT,
    )(place, own, *received, table, *after)


def finish_kernel(sites, chunk, place_ref, own_ref, *refs):
    hops = refs[:sites]
    cosine_ref, sine_ref = refs[sites : sites + 2]
    filtered_ref, shifted_ref, work_ref = refs[-3:]
    vectors = CHUNKS[chunk]
    momenta = cosine_ref.shape[0]
    for d in range(sites):
        slot = lax.rem(place_ref[0] + d, sites)
        start = row_of(slot, own_ref.shape[1] // sites, chunk)
        for c in range(6):
            work_ref[d, c] = hops[d][c].astype(jnp.float32) - own_ref[c, pl.ds(start, 4 * vectors), :]
        for color in range(3):
            for row in range(4):
                at = slice((color * 4 + row) * LANES, (color * 4 + row + 1) * LANES)
                re = work_ref[d, color, pl.ds(row, vectors, stride=4), :].astype(jnp.bfloat16)
                im = work_ref[d, 3 + color, pl.ds(row, vectors, stride=4), :].astype(jnp.bfloat16)
                filtered_ref[slot, 0, :, at] = re
                filtered_ref[slot, 1, :, at] = im
                re, im = re.astype(jnp.float32), im.astype(jnp.float32)
                for p in range(momenta):
                    cosine = cosine_ref[p, row : row + 1, :]
                    sine = sine_ref[p, row : row + 1, :]
                    shifted_ref[p, slot, 0, :, at] = (cosine * re + sine * im).astype(jnp.bfloat16)
                    shifted_ref[p, slot, 1, :, at] = (cosine * im - sine * re).astype(jnp.bfloat16)


def finish(own, place, chunk, hops, cosine, sine, after):
    sites, momenta, vectors = len(hops), cosine.shape[0], CHUNKS[chunk]
    shapes = ((sites, 2, vectors, 12 * LANES), (momenta, sites, 2, vectors, 12 * LANES))
    return pl.pallas_call(
        functools.partial(finish_kernel, sites, chunk),
        out_shape=[pltpu.VMEM(shape, jnp.bfloat16) for shape in shapes],
        in_specs=[SMEM] + [VMEM] * (sites + 3) + [ANY] * len(after),
        out_specs=[VMEM, VMEM],
        scratch_shapes=[pltpu.VMEM((sites, 6, 4 * vectors, LANES), jnp.float32)],
        cost_estimate=pl.CostEstimate(
            flops=20 * sites * 24 * vectors * LANES, bytes_accessed=sites * 24 * vectors * LANES * 12,
            transcendentals=0),
        compiler_params=GRANT,
    )(place, own, *hops, cosine, sine, *after)


def fill_left(left_ref, chunks):
    slots, _, _, depth = chunks[0].shape
    sizes = [ref.shape[2] for ref in chunks]
    for n, ref in enumerate(chunks):
        for slot in range(slots):
            at = slot * sum(sizes) + sum(sizes[:n])
            for part in range(2):
                left_ref[at : at + sizes[n], part * depth : (part + 1) * depth] = ref[slot, part]


def multiply(left_ref, right_ref, total_ref, place_ref, outs):
    segments, rows, _ = total_ref.shape
    for p in range(right_ref.shape[0]):
        product = lax.dot_general(
            left_ref[...], right_ref[p], (((1,), (1,)), ((), ())), preferred_element_type=jnp.float32)
        width = product.shape[1]
        for s in range(segments):
            total_ref[s, :, p * width : (p + 1) * width] = product[s * rows : (s + 1) * rows]
    for d in range(segments):
        outs[d][...] = total_ref[lax.rem(place_ref[0] + d, segments)].astype(outs[d].dtype)


def early_kernel(segments, count, place_ref, *refs):
    chunks = len(CHUNKS)
    left, shifted = refs[:count], refs[count : count + chunks]
    outs = refs[count + chunks : count + chunks + segments]
    right_ref, left_ref, total_ref = refs[count + chunks + segments :]
    slots, _, _, depth = left[0].shape
    block = right_ref.shape[1] // 2
    fill_left(left_ref, left)
    for p in range(right_ref.shape[0]):
        for n, ref in enumerate(shifted):
            for slot in range(slots):
                re, im = ref[p, slot, 0], ref[p, slot, 1]
                at = slot * sum(CHUNKS) + sum(CHUNKS[:n])
                low, high = slice(at, at + CHUNKS[n]), slice(block + at, block + at + CHUNKS[n])
                right_ref[p, low, :depth] = re
                right_ref[p, low, depth:] = im
                right_ref[p, high, :depth] = im
                right_ref[p, high, depth:] = -re
    multiply(left_ref, right_ref, total_ref, place_ref, outs)


def late_kernel(segments, count, place_ref, *refs):
    left, right_ref = refs[:count], refs[count]
    outs = refs[count + 1 : count + 1 + segments]
    left_ref, total_ref = refs[count + 1 + segments :]
    fill_left(left_ref, left)
    multiply(left_ref, right_ref, total_ref, place_ref, outs)


def elementals(place, left, shifted, right, segments):
    _, _, _, depth = left[0].shape
    block = segments * sum(CHUNKS)
    rows = sum(ref.shape[2] for ref in left)
    early = right is None
    momenta = shifted[0].shape[0] if early else right.shape[0]
    columns = momenta * 2 * block
    shapes = [pltpu.VMEM((rows, columns), jnp.float32 if d == 0 else jnp.bfloat16) for d in range(segments)]
    if early:
        shapes.append(pltpu.VMEM((momenta, 2 * block, 2 * depth), jnp.bfloat16))
    operands = [*left, *shifted] if early else [*left, right]
    return pl.pallas_call(
        functools.partial(early_kernel if early else late_kernel, segments, len(left)),
        out_shape=shapes,
        in_specs=[SMEM] + [VMEM] * len(operands),
        out_specs=[VMEM] * len(shapes),
        scratch_shapes=[
            pltpu.VMEM((segments * rows, 2 * depth), jnp.bfloat16),
            pltpu.VMEM((segments, rows, columns), jnp.float32),
        ],
        cost_estimate=pl.CostEstimate(
            flops=2 * segments * rows * columns * 2 * depth, bytes_accessed=8 * block * depth, transcendentals=0),
        compiler_params=GRANT,
        name="elementals_early" if early else "elementals_late",
    )(place, *operands)


def add_kernel(count, *refs):
    out_ref, at = refs[-1], 0
    for group in (refs[:count], refs[count:-1]):
        total = group[0][...]
        for ref in group[1:]:
            total = total + ref[...].astype(jnp.float32)
        out_ref[at : at + total.shape[0]] = total.astype(jnp.bfloat16)
        at += total.shape[0]


def add_parts(early, late):
    rows = early[0].shape[0] + late[0].shape[0]
    return pl.pallas_call(
        functools.partial(add_kernel, len(early)),
        out_shape=pltpu.VMEM((rows, early[0].shape[1]), jnp.bfloat16),
        in_specs=[VMEM] * (len(early) + len(late)),
        out_specs=VMEM,
        compiler_params=GRANT,
        name="add_parts",
    )(*early, *late)


def fill_right(right_ref, pieces, across, place_ref, owner_ref):
    sites = len(pieces)
    momenta, nvec = right_ref.shape[0], right_ref.shape[1] // 2
    block = nvec // 2
    half = block - LANES
    rows = block // sites
    v = lax.rem(place_ref[1] + across, 2)
    leads = owner_ref[v] == 0

    def tiles(value):
        zeros = jnp.zeros((value.shape[0], LANES - half), value.dtype)
        first = jnp.concatenate([value[:, :LANES], value[:, LANES:], zeros], axis=1)
        second = jnp.concatenate([value[:, half:], zeros, value[:, :half]], axis=1)
        return jnp.where(leads, first, second)

    for up, piece in enumerate(pieces):
        z = lax.rem(place_ref[0] + up, sites)
        for part, owner in ((0, owner_ref[v]), (1, owner_ref[1 - v])):
            row = pl.multiple_of(owner * block + z * rows, 16)
            low = pl.multiple_of(nvec + owner * block + z * rows, 16)
            for p in range(momenta):
                value = piece[part * rows : (part + 1) * rows, p * 2 * block : (p + 1) * 2 * block]
                re, im = tiles(value[:, :block]), tiles(value[:, block:])
                right_ref[p, pl.ds(row, rows), : 2 * LANES] = re
                right_ref[p, pl.ds(row, rows), 2 * LANES :] = im
                right_ref[p, pl.ds(low, rows), : 2 * LANES] = -im
                right_ref[p, pl.ds(low, rows), 2 * LANES :] = re


def pair_of(tau_ref, n):
    left = [jnp.concatenate([tau_ref[n + k, 0], tau_ref[n + k, 1]], axis=1) for k in range(2)]
    return jnp.concatenate(left, axis=0)


def first_kernel(sites, place_ref, owner_ref, tau_ref, *refs):
    pieces, (out_ref, right_ref) = refs[:sites], refs[sites:]
    fill_right(right_ref, pieces, 0, place_ref, owner_ref)

    def step(n, carry):
        left = pair_of(tau_ref, 2 * n)
        for p in range(right_ref.shape[0]):
            product = jnp.dot(left, right_ref[p], preferred_element_type=jnp.float32).astype(jnp.bfloat16)
            for k in range(2):
                out_ref[2 * n + k, p] = product[k * rows : (k + 1) * rows]
        return carry

    rows = tau_ref.shape[2]
    lax.fori_loop(0, tau_ref.shape[0] // 2, step, 0)


def second_kernel(sites, place_ref, owner_ref, tau_ref, first_ref, *refs):
    pieces, (out_ref, right_ref) = refs[:sites], refs[sites:]

    @pl.when(pl.program_id(0) == 0)
    def assemble():
        fill_right(right_ref, pieces, 1, place_ref, owner_ref)

    leads = owner_ref[place_ref[1]] == 0
    left = pair_of(tau_ref, 0)
    rows = tau_ref.shape[2]
    for p in range(right_ref.shape[0]):
        both = jnp.dot(left, right_ref[p], preferred_element_type=jnp.float32).astype(jnp.bfloat16)
        for k in range(2):
            product = both[k * rows : (k + 1) * rows]
            for c in range(2):
                at = 2 * c * LANES
                mine, theirs = first_ref[k, p, :, at : at + LANES], product[:, at : at + LANES]
                middle = first_ref[k, p, :, at + LANES : at + 2 * LANES] + product[:, at + LANES : at + 2 * LANES]
                out_ref[k, p, c, :, :LANES] = jnp.where(leads, mine, theirs)
                out_ref[k, p, c, :, LANES : 2 * LANES] = middle
                out_ref[k, p, c, :, 2 * LANES :] = jnp.where(leads, theirs, mine)


def project_first(tau, place, owner, pieces, momenta):
    outer, _, rows, nvec = tau.shape
    return pl.pallas_call(
        functools.partial(first_kernel, len(pieces)),
        out_shape=pltpu.VMEM((outer, momenta, rows, 4 * LANES), jnp.bfloat16),
        in_specs=[SMEM, SMEM] + [VMEM] * (1 + len(pieces)),
        out_specs=VMEM,
        scratch_shapes=[pltpu.VMEM((momenta, 2 * nvec, 4 * LANES), jnp.bfloat16)],
        cost_estimate=pl.CostEstimate(
            flops=2 * outer * rows * 2 * nvec * nvec * momenta, bytes_accessed=outer * rows * nvec * 8,
            transcendentals=0),
        compiler_params=GRANT,
        name="project_first",
    )(place, owner, tau, *pieces)


def project_second(tau, place, owner, first, pieces, momenta):
    outer, _, rows, nvec = tau.shape
    return pl.pallas_call(
        functools.partial(second_kernel, len(pieces)),
        grid=(outer // 2,),
        out_shape=jax.ShapeDtypeStruct((outer, momenta, 2, rows, nvec), jnp.bfloat16),
        in_specs=[SMEM, SMEM, pl.BlockSpec((2, 2, rows, nvec), lambda i: (i, 0, 0, 0)),
                  pl.BlockSpec((2, *first.shape[1:]), lambda i: (i, 0, 0, 0))] + [VMEM] * len(pieces),
        out_specs=pl.BlockSpec((2, momenta, 2, rows, nvec), lambda i: (i, 0, 0, 0, 0)),
        scratch_shapes=[pltpu.VMEM((momenta, 2 * nvec, 4 * LANES), jnp.bfloat16)],
        cost_estimate=pl.CostEstimate(
            flops=2 * outer * rows * 2 * nvec * nvec * momenta, bytes_accessed=outer * rows * nvec * 12,
            transcendentals=0),
        compiler_params=GRANT,
        name="project_second",
    )(place, owner, tau, first, *pieces)


def from_place(block, up, across):
    sites, groups = lax.axis_size("site"), lax.axis_size("vec")
    route = []
    for z in range(sites):
        for v in range(groups):
            route.append((((z + up) % sites) * groups + (v + across) % groups, z * groups + v))
    return lax.ppermute(block, ("site", "vec"), route)


ORDER = (("filter", 0), ("filter", 1), ("finish", 0), ("filter", 2), ("finish", 1), ("finish", 2))


def per_device(eigvecs, links, peramb, block_owner, momenta):
    sites = lax.axis_size("site")
    site, group = lax.axis_index("site"), lax.axis_index("vec")
    block = eigvecs.shape[3]
    own = eigvecs.reshape(6, block * 4, LANES)
    own_links = links.reshape(216, LANES)
    place = jnp.stack([site, group]).astype(jnp.int32)

    received, packed = [], []
    for chunk in range(len(CHUNKS)):
        after = packed[:1]
        if chunk == 1:
            after = received[0][:1]
        if chunk == 2:
            after = [*received[0], packed[0]]
        packed = pack(own, place, chunk, sites, own_links, after)
        received.append([from_place(packed[d - 1], -d, 0) for d in range(1, sites)])

    flat = lax.broadcasted_iota(jnp.int32, (4, LANES), 0) * LANES + lax.broadcasted_iota(jnp.int32, (4, LANES), 1)
    theta = phase_angle(momenta, flat % LX, flat // LX, jnp.full_like(flat, site), sites)
    cosine, sine = jnp.cos(theta), jnp.sin(theta)

    table = link_tables([own_links] + received[0])
    hops, filtered, shifted, other = {}, {}, {}, {}
    last = None
    for kind, chunk in ORDER:
        after = [] if last is None else [last]
        if kind == "filter":
            out = filter_chunk(own, place, chunk, received[chunk], table, after)
            hops[chunk] = [out[0]] + [from_place(out[d], d, 0) for d in range(1, sites)]
            last = out[0]
        else:
            f, s = finish(own, place, chunk, hops[chunk], cosine, sine, after)
            other[chunk] = from_place(f, 0, 1)
            filtered[chunk], shifted[chunk] = f, s
            last = s
    filtered, shifted, other = ([group_of[n] for n in range(len(CHUNKS))] for group_of in (filtered, shifted, other))

    *parts, right = elementals(place, filtered + other[:-1], shifted, None, sites)
    sent = [from_place(parts[d], -d, 0) for d in range(1, sites)]
    early = [parts[0], *sent]
    parts = elementals(place, other[-1:], None, right, sites)
    sent = [from_place(parts[d], -d, 0) for d in range(1, sites)]
    mine = add_parts(early, [parts[0], *sent])

    across = [from_place(mine, 0, 1)]
    pieces = [mine] + [from_place(mine, up, 0) for up in range(1, sites)]
    across += [from_place(piece, 0, 1) for piece in pieces[1:]]
    sinks, spins = peramb.shape[1], peramb.shape[2]
    tau = peramb.reshape(sinks * spins, 2, block, peramb.shape[5])
    first = project_first(tau, place, block_owner, pieces, momenta.shape[0])
    result = project_second(tau, place, block_owner, first, across, momenta.shape[0])
    return result.reshape(1, sinks, spins, momenta.shape[0], 2, block, peramb.shape[5])


def from_behind(block, axis, distance):
    devices = range(lax.axis_size(axis))
    route = [((i - distance) % len(devices), i) for i in devices]
    return lax.ppermute(block, axis, route)


def with_halo(block, sides, width):
    for axis, dim in sides:
        count = lax.axis_size(axis)
        forward = [(i, i + 1) for i in range(count - 1)]
        forward.append((count - 1, 0))
        backward = [(target, source) for source, target in forward]
        low = lax.ppermute(
            lax.slice_in_dim(block, block.shape[dim] - width, None, axis=dim), axis, forward
        )
        high = lax.ppermute(lax.slice_in_dim(block, 0, width, axis=dim), axis, backward)
        block = jnp.concatenate([low, block, high], axis=dim)
    return block


def along(field, direction, sense):
    width = field.shape[-1]
    column = lax.broadcasted_iota(jnp.int32, (width,), 0) % LX
    if direction == 0:
        if sense > 0:
            return jnp.where(column == LX - 1, jnp.roll(field, LX - 1, -1), jnp.roll(field, -1, -1))
        return jnp.where(column == 0, jnp.roll(field, 1 - LX, -1), jnp.roll(field, 1, -1))
    return jnp.roll(field, -sense * LX, -1)


def link_times(link_re, link_im, field_re, field_im, dagger):
    result_re = []
    result_im = []
    for target in range(3):
        summed_re = jnp.zeros_like(field_re[0])
        summed_im = jnp.zeros_like(field_re[0])
        for source in range(3):
            if dagger:
                entry_re = link_re[source, target][None]
                entry_im = -link_im[source, target][None]
            else:
                entry_re = link_re[target, source][None]
                entry_im = link_im[target, source][None]
            summed_re = summed_re + entry_re * field_re[source] - entry_im * field_im[source]
            summed_im = summed_im + entry_re * field_im[source] + entry_im * field_re[source]
        result_re.append(summed_re)
        result_im.append(summed_im)
    return (jnp.stack(result_re), jnp.stack(result_im))


def chebyshev(initial, operate):
    current = operate(initial)
    following = 2.0 * operate(current) - initial
    return following


def general_device(eigvecs, links, peramb, block_owner, momenta):
    vectors = eigvecs[0]
    links_here = links[0]
    block = vectors.shape[2]
    layers = vectors.shape[3]
    plane = vectors.shape[4]
    site_count = lax.axis_size("site")
    group_count = lax.axis_size("vec")
    site_rank = lax.axis_index("site")
    group_rank = lax.axis_index("vec")
    portion = plane // group_count
    top_plane = links_here[2, :, :, :, layers - 1 :, :]
    below = from_behind(top_plane, "site", 1)
    behind_links = jnp.concatenate([below, links_here[2, :, :, :, : layers - 1, :]], axis=3)
    back_links = []
    for direction in range(2):
        back_links.append(
            (
                along(links_here[direction, 0], direction, -1),
                along(links_here[direction, 1], direction, -1),
            )
        )
    back_links.append((behind_links[0], behind_links[1]))

    def operate(field):
        padded = with_halo(field, (("site", 3),), 1)
        total_re = jnp.zeros_like(field[0])
        total_im = jnp.zeros_like(field[0])
        for direction in range(3):
            if direction < 2:
                ahead = along(field, direction, 1)
                behind = along(field, direction, -1)
            else:
                ahead = padded[:, :, :, 2:]
                behind = padded[:, :, :, :-2]
            forward = link_times(
                links_here[direction, 0], links_here[direction, 1], ahead[0], ahead[1], False
            )
            backward = link_times(
                back_links[direction][0], back_links[direction][1], behind[0], behind[1], True
            )
            total_re = total_re + forward[0] + backward[0]
            total_im = total_im + forward[1] + backward[1]
        return jnp.stack([total_re, total_im]) * (-1.0 / 6.0)

    filtered = chebyshev(vectors, operate).astype(jnp.bfloat16)
    received = lax.all_to_all(filtered, "vec", split_axis=4, concat_axis=2, tiled=True)
    grouped = received.reshape(2, 3, group_count, block, layers, portion)
    ranks = jnp.arange(group_count, dtype=jnp.int32)
    inverse = jnp.sum(
        ranks[:, None] * (block_owner[:, None] == ranks[None, :]).astype(jnp.int32), axis=0
    )
    ordered = jnp.take(grouped, inverse, axis=2).reshape(2, 3, group_count * block, layers, portion)
    nvec = group_count * block
    flat = group_rank * portion + lax.broadcasted_iota(jnp.int32, (layers, portion), 1)
    depth = site_rank * layers + lax.broadcasted_iota(jnp.int32, (layers, portion), 0)
    theta = phase_angle(momenta, flat % LX, flat // LX, depth, layers * site_count)
    values = ordered.astype(jnp.float32)
    cosine = jnp.cos(theta)[:, None, None]
    sine = jnp.sin(theta)[:, None, None]
    shift_re = cosine * values[0] + sine * values[1]
    shift_im = cosine * values[1] - sine * values[0]
    shifted = jnp.stack([shift_re, shift_im], axis=1).astype(jnp.bfloat16)
    products = jnp.einsum(
        "acizs,pbckzs->aipbk", ordered, shifted, preferred_element_type=jnp.float32
    )
    real = products[0, :, :, 0] + products[1, :, :, 1]
    imag = products[0, :, :, 1] - products[1, :, :, 0]
    momentum_count = momenta.shape[0]
    partial_sum = jnp.stack([real, imag], axis=2).reshape(nvec, momentum_count * 2 * nvec)
    tau = peramb[0]
    tau_rows = tau.reshape(-1, nvec)
    summed = lax.psum(partial_sum, ("site", "vec")).astype(jnp.bfloat16)
    joined = jnp.dot(tau_rows, summed, preferred_element_type=jnp.float32)
    sinks = tau.shape[0]
    spins = tau.shape[1]
    layout = joined.reshape(sinks, spins, 2, block, momentum_count, 2, nvec)
    real_part = layout[:, :, 0, :, :, 0] - layout[:, :, 1, :, :, 1]
    imag_part = layout[:, :, 0, :, :, 1] + layout[:, :, 1, :, :, 0]
    stacked = jnp.stack([real_part, imag_part], axis=0)
    result = jnp.transpose(stacked, (1, 2, 4, 0, 3, 5))
    return result[None].astype(jnp.bfloat16)


def choose(eigvecs, links, peramb, block_owner, momenta):
    block, layers, plane = eigvecs.shape[3:]
    sites, groups = lax.axis_size("site"), lax.axis_size("vec")
    fits = layers == 1 and plane == LX * LY == 4 * LANES and sites == 4 and groups == 2
    fits = fits and block == sites * sum(CHUNKS) and LANES < block < 2 * LANES
    fits = fits and peramb.shape[1] * peramb.shape[2] % 2 == 0 and (2 * block) % (32 * sites) == 0 and block % (2 * block // sites) == 0
    device = per_device if fits else general_device
    return device(eigvecs, links, peramb, block_owner, momenta)


def solution(mesh):
    placed = (
        P(("cfg", "tslice"), None, None, "vec", "site", None),
        P(("cfg", "tslice"), None, None, None, None, "site", None),
        P(("cfg", "tslice"), "site", None, None, "vec", None),
        P(),
        P(),
    )
    return jax.shard_map(
        choose,
        mesh=mesh,
        in_specs=placed,
        out_specs=P(("cfg", "tslice"), "site", None, None, None, "vec", None),
        check_vma=False,
    )
```

```python
import functools
import math

import jax
import jax.numpy as jnp
from jax import lax
from jax.experimental import pallas as pl
from jax.experimental.pallas import tpu as pltpu
from jax.sharding import PartitionSpec as P


LX = 32
LY = 16
LANES = 128

two_pi = 2.0 * math.pi

CHUNKS = (16, 16, 16)


def phase_angle(momenta, across, upward, depth, extent):
    return two_pi * (
        (momenta[:, 0, None, None] * across[None]).astype(jnp.float32) / LX
        + (momenta[:, 1, None, None] * upward[None]).astype(jnp.float32) / LY
        + (momenta[:, 2, None, None] * depth[None]).astype(jnp.float32) / extent
    )


VMEM = pl.BlockSpec(memory_space=pltpu.VMEM)
SMEM = pl.BlockSpec(memory_space=pltpu.SMEM)
ANY = pl.BlockSpec(memory_space=pl.ANY)
HBM = pl.BlockSpec(memory_space=pltpu.HBM)
GRANT = pltpu.CompilerParams(vmem_limit_bytes=16 * 2**20)


class Shifts:
    def __init__(self):
        lane = lax.broadcasted_iota(jnp.int32, (8, LANES), 1)
        row = lax.broadcasted_iota(jnp.int32, (8, LANES), 0) % 4
        column = lane % LX
        self.x_last = column == LX - 1
        self.x_first = column == 0
        self.y_high = lane >= LANES - LX
        self.y_low = lane < LX
        self.row_last = row == 3
        self.row_first = row == 0

    def ahead_x(self, v):
        return jnp.where(self.x_last, pltpu.roll(v, LX - 1, 1), pltpu.roll(v, LANES - 1, 1))

    def behind_x(self, v):
        return jnp.where(self.x_first, pltpu.roll(v, LANES - LX + 1, 1), pltpu.roll(v, 1, 1))

    def ahead_y(self, v):
        a = pltpu.roll(v, LANES - LX, 1)
        wrapped = jnp.where(self.row_last, pltpu.roll(a, 3, 0), pltpu.roll(a, 7, 0))
        return jnp.where(self.y_high, wrapped, a)

    def behind_y(self, v):
        a = pltpu.roll(v, LX, 1)
        wrapped = jnp.where(self.row_first, pltpu.roll(a, 5, 0), pltpu.roll(a, 1, 0))
        return jnp.where(self.y_low, wrapped, a)


def tables_kernel(*refs):
    table_ref = refs[-1]
    shifts = Shifts()
    scale = jnp.float32(-math.sqrt(2.0) / 6.0)
    size = refs[0].shape[0]
    links = [ref[ref.shape[0] - size :].astype(jnp.float32) for ref in refs[:-1]]
    count = len(links)

    def entry(plane, direction, part, row, col):
        e = direction * 18 + part * 9 + row * 3 + col
        value = links[plane % count][4 * e : 4 * e + 4] * scale
        return jnp.concatenate([value, value], axis=0)

    for plane in range(count):
        for direction in range(3):
            for target in range(3):
                for source in range(3):
                    slot = (2 * direction) * 27 + (target * 3 + source) * 3
                    re = entry(plane, direction, 0, target, source)
                    im = entry(plane, direction, 1, target, source)
                    table_ref[plane, slot] = re
                    table_ref[plane, slot + 1] = im
                    table_ref[plane, slot + 2] = re + im
                    slot = (2 * direction + 1) * 27 + (target * 3 + source) * 3
                    below = plane + 1 if direction == 2 else plane
                    re = entry(below, direction, 0, source, target)
                    im = entry(below, direction, 1, source, target)
                    if direction < 2:
                        move = shifts.behind_x if direction == 0 else shifts.behind_y
                        re, im = move(re), move(im)
                    table_ref[plane, slot] = re
                    table_ref[plane, slot + 1] = -im
                    table_ref[plane, slot + 2] = re - im


def link_tables(links):
    return pl.pallas_call(
        tables_kernel,
        out_shape=pltpu.VMEM((len(links), 162, 8, LANES), jnp.float32),
        in_specs=[VMEM] * len(links),
        out_specs=VMEM,
        compiler_params=GRANT,
        name="link_tables",
    )(*links)


def pack_kernel(sites, chunk, place_ref, own_ref, *refs):
    outs = refs[1 - sites :]
    rows = CHUNKS[chunk] * 4
    for d in range(1, sites):
        start = row_of(lax.rem(place_ref[0] + d, sites), own_ref.shape[1] // sites, chunk)
        out = outs[d - 1]
        for c in range(6):
            out[c * rows : (c + 1) * rows] = own_ref[c, pl.ds(start, rows), :].astype(jnp.bfloat16)


def first_pack_kernel(sites, place_ref, own_ref, links_ref, *refs):
    outs, block_ref, link_ref, sems = refs[: sites - 1], refs[sites - 1], refs[sites], refs[sites + 1]
    rows = CHUNKS[0] * 4
    copies = [pltpu.make_async_copy(links_ref, link_ref, sems.at[0])]
    for d in range(1, sites):
        start = row_of(lax.rem(place_ref[0] + d, sites), own_ref.shape[1] // sites, 0)
        copies.append(pltpu.make_async_copy(own_ref.at[:, pl.ds(start, rows), :], block_ref.at[d - 1], sems.at[d]))
    for copy in copies:
        copy.start()
    copies[0].wait()
    links = link_ref[...].astype(jnp.bfloat16)
    for d in range(1, sites):
        copies[d].wait()
        for c in range(6):
            outs[d - 1][c * rows : (c + 1) * rows] = block_ref[d - 1, c].astype(jnp.bfloat16)
        outs[d - 1][6 * rows :] = links


def first_pack(own, place, sites, links):
    rows = CHUNKS[0] * 4
    return pl.pallas_call(
        functools.partial(first_pack_kernel, sites),
        out_shape=[pltpu.VMEM((6 * rows + links.shape[0], LANES), jnp.bfloat16)] * (sites - 1),
        in_specs=[SMEM, HBM, HBM],
        out_specs=[VMEM] * (sites - 1),
        scratch_shapes=[
            pltpu.VMEM((sites - 1, 6, rows, LANES), jnp.float32),
            pltpu.VMEM(links.shape, jnp.float32),
            pltpu.SemaphoreType.DMA((sites,)),
        ],
        compiler_params=pltpu.CompilerParams(vmem_limit_bytes=66 * 10**6),
        name="pack0",
    )(place, own, links)


def row_of(slot, rows_per_slot, chunk):
    return pl.multiple_of(slot * rows_per_slot + 4 * sum(CHUNKS[:chunk]), 32)


def pack(own, place, chunk, sites, after):
    length = 24 * CHUNKS[chunk]
    return pl.pallas_call(
        functools.partial(pack_kernel, sites, chunk),
        out_shape=[pltpu.VMEM((length, LANES), jnp.bfloat16)] * (sites - 1),
        in_specs=[SMEM, VMEM] + [ANY] * len(after),
        out_specs=[VMEM] * (sites - 1),
        compiler_params=GRANT,
    )(place, own, *after)


def filter_kernel(sites, chunk, place_ref, *refs):
    fields, table_ref = refs[:sites], refs[sites]
    outs, t1_ref = refs[-1 - sites : -1], refs[-1]
    shifts = Shifts()
    rows = CHUNKS[chunk] * 4
    home = row_of(place_ref[0], fields[0].shape[1] // sites, chunk)

    def hop(plane, here, ahead_z, behind_z):
        count = len(here(0))
        sums = [[[None] * count for _ in range(3)] for _ in range(3)]
        moves = (shifts.ahead_x, shifts.behind_x, shifts.ahead_y, shifts.behind_y, None, None)
        for direction in range(6):
            if direction < 4:
                field = [[moves[direction](v) for v in here(c)] for c in range(6)]
            else:
                take = ahead_z if direction == 4 else behind_z
                field = [take(c) for c in range(6)]
            for source in range(3):
                re, im = field[source], field[3 + source]
                factors = ([im[n] - re[n] for n in range(count)], [im[n] + re[n] for n in range(count)], re)
                for target in range(3):
                    slot = direction * 27 + (target * 3 + source) * 3
                    for k in range(3):
                        link = table_ref[plane, slot + k]
                        for n in range(count):
                            add = link * factors[k][n]
                            old = sums[target][k][n]
                            sums[target][k][n] = add if old is None else old + add
        total_re = [[sums[t][2][n] - sums[t][1][n] for n in range(count)] for t in range(3)]
        total_im = [[sums[t][2][n] + sums[t][0][n] for n in range(count)] for t in range(3)]
        return total_re + total_im

    def step(index, carry):
        base = pl.multiple_of(index * 16, 16)

        def start(plane):
            def read(c):
                ref = fields[plane % sites]
                if plane % sites == 0:
                    value = ref[c, pl.ds(pl.multiple_of(home + base, 16), 16), :]
                else:
                    value = ref[pl.ds(pl.multiple_of(c * rows + base, 16), 16), :].astype(jnp.float32)
                return [value[0:8], value[8:16]]

            return read

        def first(plane):
            return lambda c: [t1_ref[plane % sites, c, 0:8], t1_ref[plane % sites, c, 8:16]]

        for plane in range(sites):
            out = hop(plane, start(plane), start(plane - 1), start(plane + 1))
            for c in range(6):
                for n in range(2):
                    t1_ref[plane, c, 8 * n : 8 * n + 8] = out[c][n]
        for plane in range(sites):
            out = hop(plane, first(plane), first(plane - 1), first(plane + 1))
            for c in range(6):
                value = jnp.concatenate(out[c], axis=0)
                outs[plane][c, pl.ds(base, 16), :] = value.astype(jnp.bfloat16)
        return carry

    lax.fori_loop(0, rows // 16, step, 0)


def filter_chunk(own, place, chunk, received, table, after):
    sites = len(received) + 1
    rows = CHUNKS[chunk] * 4
    return pl.pallas_call(
        functools.partial(filter_kernel, sites, chunk),
        out_shape=[pltpu.VMEM((6, rows, LANES), jnp.bfloat16)] * sites,
        in_specs=[SMEM] + [VMEM] * (sites + 1) + [ANY] * len(after),
        out_specs=[VMEM] * sites,
        scratch_shapes=[pltpu.VMEM((sites, 6, 16, LANES), jnp.float32)],
        cost_estimate=pl.CostEstimate(
            flops=432 * 2 * sites * rows * LANES, bytes_accessed=6 * rows * LANES * 4 * sites, transcendentals=0),
        compiler_params=GRANT,
    )(place, own, *received, table, *after)


def finish_kernel(sites, chunk, place_ref, own_ref, *refs):
    hops = refs[:sites]
    cosine_ref, sine_ref = refs[sites : sites + 2]
    filtered_ref, shifted_ref, work_ref = refs[-3:]
    vectors = CHUNKS[chunk]
    momenta = cosine_ref.shape[0]
    for d in range(sites):
        slot = lax.rem(place_ref[0] + d, sites)
        start = row_of(slot, own_ref.shape[1] // sites, chunk)
        for c in range(6):
            work_ref[d, c] = hops[d][c].astype(jnp.float32) - own_ref[c, pl.ds(start, 4 * vectors), :]
        for color in range(3):
            for row in range(4):
                at = slice((color * 4 + row) * LANES, (color * 4 + row + 1) * LANES)
                re = work_ref[d, color, pl.ds(row, vectors, stride=4), :].astype(jnp.bfloat16)
                im = work_ref[d, 3 + color, pl.ds(row, vectors, stride=4), :].astype(jnp.bfloat16)
                filtered_ref[slot, 0, :, at] = re
                filtered_ref[slot, 1, :, at] = im
                re, im = re.astype(jnp.float32), im.astype(jnp.float32)
                for p in range(momenta):
                    cosine = cosine_ref[p, row : row + 1, :]
                    sine = sine_ref[p, row : row + 1, :]
                    shifted_ref[p, slot, 0, :, at] = (cosine * re + sine * im).astype(jnp.bfloat16)
                    shifted_ref[p, slot, 1, :, at] = (cosine * im - sine * re).astype(jnp.bfloat16)


def finish(own, place, chunk, hops, cosine, sine, after):
    sites, momenta, vectors = len(hops), cosine.shape[0], CHUNKS[chunk]
    shapes = ((sites, 2, vectors, 12 * LANES), (momenta, sites, 2, vectors, 12 * LANES))
    return pl.pallas_call(
        functools.partial(finish_kernel, sites, chunk),
        out_shape=[pltpu.VMEM(shape, jnp.bfloat16) for shape in shapes],
        in_specs=[SMEM] + [VMEM] * (sites + 3) + [ANY] * len(after),
        out_specs=[VMEM, VMEM],
        scratch_shapes=[pltpu.VMEM((sites, 6, 4 * vectors, LANES), jnp.float32)],
        cost_estimate=pl.CostEstimate(
            flops=20 * sites * 24 * vectors * LANES, bytes_accessed=sites * 24 * vectors * LANES * 12,
            transcendentals=0),
        compiler_params=GRANT,
    )(place, own, *hops, cosine, sine, *after)


def fill_left(left_ref, chunks):
    slots, _, _, depth = chunks[0].shape
    sizes = [ref.shape[2] for ref in chunks]
    for n, ref in enumerate(chunks):
        for slot in range(slots):
            at = slot * sum(sizes) + sum(sizes[:n])
            for part in range(2):
                left_ref[at : at + sizes[n], part * depth : (part + 1) * depth] = ref[slot, part]


def multiply(left_ref, right_ref, total_ref, place_ref, outs):
    segments, rows, _ = total_ref.shape
    for p in range(right_ref.shape[0]):
        product = lax.dot_general(
            left_ref[...], right_ref[p], (((1,), (1,)), ((), ())), preferred_element_type=jnp.float32)
        width = product.shape[1]
        for s in range(segments):
            total_ref[s, :, p * width : (p + 1) * width] = product[s * rows : (s + 1) * rows]
    for d in range(segments):
        outs[d][...] = total_ref[lax.rem(place_ref[0] + d, segments)].astype(outs[d].dtype)


def early_kernel(segments, count, place_ref, *refs):
    chunks = len(CHUNKS)
    left, shifted = refs[:count], refs[count : count + chunks]
    outs = refs[count + chunks : count + chunks + segments]
    right_ref, left_ref, total_ref = refs[count + chunks + segments :]
    slots, _, _, depth = left[0].shape
    block = right_ref.shape[1] // 2
    fill_left(left_ref, left)
    for p in range(right_ref.shape[0]):
        for n, ref in enumerate(shifted):
            for slot in range(slots):
                re, im = ref[p, slot, 0], ref[p, slot, 1]
                at = slot * sum(CHUNKS) + sum(CHUNKS[:n])
                low, high = slice(at, at + CHUNKS[n]), slice(block + at, block + at + CHUNKS[n])
                right_ref[p, low, :depth] = re
                right_ref[p, low, depth:] = im
                right_ref[p, high, :depth] = im
                right_ref[p, high, depth:] = -re
    multiply(left_ref, right_ref, total_ref, place_ref, outs)


def late_kernel(segments, count, place_ref, *refs):
    left, right_ref = refs[:count], refs[count]
    outs = refs[count + 1 : count + 1 + segments]
    left_ref, total_ref = refs[count + 1 + segments :]
    fill_left(left_ref, left)
    multiply(left_ref, right_ref, total_ref, place_ref, outs)


def elementals(place, left, shifted, right, segments):
    _, _, _, depth = left[0].shape
    block = segments * sum(CHUNKS)
    rows = sum(ref.shape[2] for ref in left)
    early = right is None
    momenta = shifted[0].shape[0] if early else right.shape[0]
    columns = momenta * 2 * block
    shapes = [pltpu.VMEM((rows, columns), jnp.float32 if d == 0 else jnp.bfloat16) for d in range(segments)]
    if early:
        shapes.append(pltpu.VMEM((momenta, 2 * block, 2 * depth), jnp.bfloat16))
    operands = [*left, *shifted] if early else [*left, right]
    return pl.pallas_call(
        functools.partial(early_kernel if early else late_kernel, segments, len(left)),
        out_shape=shapes,
        in_specs=[SMEM] + [VMEM] * len(operands),
        out_specs=[VMEM] * len(shapes),
        scratch_shapes=[
            pltpu.VMEM((segments * rows, 2 * depth), jnp.bfloat16),
            pltpu.VMEM((segments, rows, columns), jnp.float32),
        ],
        cost_estimate=pl.CostEstimate(
            flops=2 * segments * rows * columns * 2 * depth, bytes_accessed=8 * block * depth, transcendentals=0),
        compiler_params=GRANT,
        name="elementals_early" if early else "elementals_late",
    )(place, *operands)


def add_kernel(count, *refs):
    out_ref, at = refs[-1], 0
    for group in (refs[:count], refs[count:-1]):
        total = group[0][...]
        for ref in group[1:]:
            total = total + ref[...].astype(jnp.float32)
        out_ref[at : at + total.shape[0]] = total.astype(jnp.bfloat16)
        at += total.shape[0]


def add_parts(early, late):
    rows = early[0].shape[0] + late[0].shape[0]
    return pl.pallas_call(
        functools.partial(add_kernel, len(early)),
        out_shape=pltpu.VMEM((rows, early[0].shape[1]), jnp.bfloat16),
        in_specs=[VMEM] * (len(early) + len(late)),
        out_specs=VMEM,
        compiler_params=GRANT,
        name="add_parts",
    )(*early, *late)


def fill_right(right_ref, pieces, across, place_ref, owner_ref):
    sites = len(pieces)
    momenta, nvec = right_ref.shape[0], right_ref.shape[1] // 2
    block = nvec // 2
    half = block - LANES
    rows = block // sites
    v = lax.rem(place_ref[1] + across, 2)
    leads = owner_ref[v] == 0

    def tiles(value):
        zeros = jnp.zeros((value.shape[0], LANES - half), value.dtype)
        first = jnp.concatenate([value[:, :LANES], value[:, LANES:], zeros], axis=1)
        second = jnp.concatenate([value[:, half:], zeros, value[:, :half]], axis=1)
        return jnp.where(leads, first, second)

    for up, piece in enumerate(pieces):
        z = lax.rem(place_ref[0] + up, sites)
        for part, owner in ((0, owner_ref[v]), (1, owner_ref[1 - v])):
            row = pl.multiple_of(owner * block + z * rows, 16)
            low = pl.multiple_of(nvec + owner * block + z * rows, 16)
            for p in range(momenta):
                value = piece[part * rows : (part + 1) * rows, p * 2 * block : (p + 1) * 2 * block]
                re, im = tiles(value[:, :block]), tiles(value[:, block:])
                right_ref[p, pl.ds(row, rows), : 2 * LANES] = re
                right_ref[p, pl.ds(row, rows), 2 * LANES :] = im
                right_ref[p, pl.ds(low, rows), : 2 * LANES] = -im
                right_ref[p, pl.ds(low, rows), 2 * LANES :] = re


def pair_of(tau_ref, n):
    left = [jnp.concatenate([tau_ref[n + k, 0], tau_ref[n + k, 1]], axis=1) for k in range(2)]
    return jnp.concatenate(left, axis=0)


def first_kernel(sites, place_ref, owner_ref, tau_ref, *refs):
    pieces, (out_ref, right_ref) = refs[:sites], refs[sites:]
    fill_right(right_ref, pieces, 0, place_ref, owner_ref)

    def step(n, carry):
        left = pair_of(tau_ref, 2 * n)
        for p in range(right_ref.shape[0]):
            product = jnp.dot(left, right_ref[p], preferred_element_type=jnp.float32).astype(jnp.bfloat16)
            for k in range(2):
                out_ref[2 * n + k, p] = product[k * rows : (k + 1) * rows]
        return carry

    rows = tau_ref.shape[2]
    lax.fori_loop(0, tau_ref.shape[0] // 2, step, 0)


def second_kernel(sites, place_ref, owner_ref, tau_ref, first_ref, *refs):
    pieces, (out_ref, right_ref) = refs[:sites], refs[sites:]

    @pl.when(pl.program_id(0) == 0)
    def assemble():
        fill_right(right_ref, pieces, 1, place_ref, owner_ref)

    leads = owner_ref[place_ref[1]] == 0
    left = pair_of(tau_ref, 0)
    rows = tau_ref.shape[2]
    for p in range(right_ref.shape[0]):
        both = jnp.dot(left, right_ref[p], preferred_element_type=jnp.float32).astype(jnp.bfloat16)
        for k in range(2):
            product = both[k * rows : (k + 1) * rows]
            for c in range(2):
                at = 2 * c * LANES
                mine, theirs = first_ref[k, p, :, at : at + LANES], product[:, at : at + LANES]
                middle = first_ref[k, p, :, at + LANES : at + 2 * LANES] + product[:, at + LANES : at + 2 * LANES]
                out_ref[k, p, c, :, :LANES] = jnp.where(leads, mine, theirs)
                out_ref[k, p, c, :, LANES : 2 * LANES] = middle
                out_ref[k, p, c, :, 2 * LANES :] = jnp.where(leads, theirs, mine)


def project_first(tau, place, owner, pieces, momenta):
    outer, _, rows, nvec = tau.shape
    return pl.pallas_call(
        functools.partial(first_kernel, len(pieces)),
        out_shape=pltpu.VMEM((outer, momenta, rows, 4 * LANES), jnp.bfloat16),
        in_specs=[SMEM, SMEM] + [VMEM] * (1 + len(pieces)),
        out_specs=VMEM,
        scratch_shapes=[pltpu.VMEM((momenta, 2 * nvec, 4 * LANES), jnp.bfloat16)],
        cost_estimate=pl.CostEstimate(
            flops=2 * outer * rows * 2 * nvec * nvec * momenta, bytes_accessed=outer * rows * nvec * 8,
            transcendentals=0),
        compiler_params=GRANT,
        name="project_first",
    )(place, owner, tau, *pieces)


def project_second(tau, place, owner, first, pieces, momenta):
    outer, _, rows, nvec = tau.shape
    return pl.pallas_call(
        functools.partial(second_kernel, len(pieces)),
        grid=(outer // 2,),
        out_shape=jax.ShapeDtypeStruct((outer, momenta, 2, rows, nvec), jnp.bfloat16),
        in_specs=[SMEM, SMEM, pl.BlockSpec((2, 2, rows, nvec), lambda i: (i, 0, 0, 0)),
                  pl.BlockSpec((2, *first.shape[1:]), lambda i: (i, 0, 0, 0))] + [VMEM] * len(pieces),
        out_specs=pl.BlockSpec((2, momenta, 2, rows, nvec), lambda i: (i, 0, 0, 0, 0)),
        scratch_shapes=[pltpu.VMEM((momenta, 2 * nvec, 4 * LANES), jnp.bfloat16)],
        cost_estimate=pl.CostEstimate(
            flops=2 * outer * rows * 2 * nvec * nvec * momenta, bytes_accessed=outer * rows * nvec * 12,
            transcendentals=0),
        compiler_params=GRANT,
        name="project_second",
    )(place, owner, tau, first, *pieces)


def from_place(block, up, across):
    sites, groups = lax.axis_size("site"), lax.axis_size("vec")
    route = []
    for z in range(sites):
        for v in range(groups):
            route.append((((z + up) % sites) * groups + (v + across) % groups, z * groups + v))
    return lax.ppermute(block, ("site", "vec"), route)


ORDER = (("filter", 0), ("filter", 1), ("finish", 0), ("filter", 2), ("finish", 1), ("finish", 2))


def per_device(eigvecs, links, peramb, block_owner, momenta):
    sites = lax.axis_size("site")
    site, group = lax.axis_index("site"), lax.axis_index("vec")
    block = eigvecs.shape[3]
    own = eigvecs.reshape(6, block * 4, LANES)
    own_links = links.reshape(216, LANES)
    place = jnp.stack([site, group]).astype(jnp.int32)

    received, packed = [], []
    for chunk in range(len(CHUNKS)):
        after = packed[:1]
        if chunk == 2:
            after = [received[0][0], packed[0]]
        if chunk == 0:
            packed = first_pack(own, place, sites, own_links)
        else:
            packed = pack(own, place, chunk, sites, after)
        received.append([from_place(packed[d - 1], -d, 0) for d in range(1, sites)])

    flat = lax.broadcasted_iota(jnp.int32, (4, LANES), 0) * LANES + lax.broadcasted_iota(jnp.int32, (4, LANES), 1)
    theta = phase_angle(momenta, flat % LX, flat // LX, jnp.full_like(flat, site), sites)
    cosine, sine = jnp.cos(theta), jnp.sin(theta)

    table = link_tables([own_links] + received[0])
    hops, filtered, shifted, other = {}, {}, {}, {}
    last = None
    for kind, chunk in ORDER:
        after = [] if last is None else [last]
        if kind == "filter":
            out = filter_chunk(own, place, chunk, received[chunk], table, after)
            hops[chunk] = [out[0]] + [from_place(out[d], d, 0) for d in range(1, sites)]
            last = out[0]
        else:
            f, s = finish(own, place, chunk, hops[chunk], cosine, sine, after)
            other[chunk] = from_place(f, 0, 1)
            filtered[chunk], shifted[chunk] = f, s
            last = s
    filtered, shifted, other = ([group_of[n] for n in range(len(CHUNKS))] for group_of in (filtered, shifted, other))

    *parts, right = elementals(place, filtered + other[:1], shifted, None, sites)
    sent = [from_place(parts[d], -d, 0) for d in range(1, sites)]
    early = [parts[0], *sent]
    parts = elementals(place, other[1:], None, right, sites)
    sent = [from_place(parts[d], -d, 0) for d in range(1, sites)]
    mine = add_parts(early, [parts[0], *sent])

    across = [from_place(mine, 0, 1)]
    pieces = [mine] + [from_place(mine, up, 0) for up in range(1, sites)]
    across += [from_place(piece, 0, 1) for piece in pieces[1:]]
    sinks, spins = peramb.shape[1], peramb.shape[2]
    tau = peramb.reshape(sinks * spins, 2, block, peramb.shape[5])
    first = project_first(tau, place, block_owner, pieces, momenta.shape[0])
    result = project_second(tau, place, block_owner, first, across, momenta.shape[0])
    return result.reshape(1, sinks, spins, momenta.shape[0], 2, block, peramb.shape[5])


def from_behind(block, axis, distance):
    devices = range(lax.axis_size(axis))
    route = [((i - distance) % len(devices), i) for i in devices]
    return lax.ppermute(block, axis, route)


def with_halo(block, sides, width):
    for axis, dim in sides:
        count = lax.axis_size(axis)
        forward = [(i, i + 1) for i in range(count - 1)]
        forward.append((count - 1, 0))
        backward = [(target, source) for source, target in forward]
        low = lax.ppermute(
            lax.slice_in_dim(block, block.shape[dim] - width, None, axis=dim), axis, forward
        )
        high = lax.ppermute(lax.slice_in_dim(block, 0, width, axis=dim), axis, backward)
        block = jnp.concatenate([low, block, high], axis=dim)
    return block


def along(field, direction, sense):
    width = field.shape[-1]
    column = lax.broadcasted_iota(jnp.int32, (width,), 0) % LX
    if direction == 0:
        if sense > 0:
            return jnp.where(column == LX - 1, jnp.roll(field, LX - 1, -1), jnp.roll(field, -1, -1))
        return jnp.where(column == 0, jnp.roll(field, 1 - LX, -1), jnp.roll(field, 1, -1))
    return jnp.roll(field, -sense * LX, -1)


def link_times(link_re, link_im, field_re, field_im, dagger):
    result_re = []
    result_im = []
    for target in range(3):
        summed_re = jnp.zeros_like(field_re[0])
        summed_im = jnp.zeros_like(field_re[0])
        for source in range(3):
            if dagger:
                entry_re = link_re[source, target][None]
                entry_im = -link_im[source, target][None]
            else:
                entry_re = link_re[target, source][None]
                entry_im = link_im[target, source][None]
            summed_re = summed_re + entry_re * field_re[source] - entry_im * field_im[source]
            summed_im = summed_im + entry_re * field_im[source] + entry_im * field_re[source]
        result_re.append(summed_re)
        result_im.append(summed_im)
    return (jnp.stack(result_re), jnp.stack(result_im))


def chebyshev(initial, operate):
    current = operate(initial)
    following = 2.0 * operate(current) - initial
    return following


def general_device(eigvecs, links, peramb, block_owner, momenta):
    vectors = eigvecs[0]
    links_here = links[0]
    block = vectors.shape[2]
    layers = vectors.shape[3]
    plane = vectors.shape[4]
    site_count = lax.axis_size("site")
    group_count = lax.axis_size("vec")
    site_rank = lax.axis_index("site")
    group_rank = lax.axis_index("vec")
    portion = plane // group_count
    top_plane = links_here[2, :, :, :, layers - 1 :, :]
    below = from_behind(top_plane, "site", 1)
    behind_links = jnp.concatenate([below, links_here[2, :, :, :, : layers - 1, :]], axis=3)
    back_links = []
    for direction in range(2):
        back_links.append(
            (
                along(links_here[direction, 0], direction, -1),
                along(links_here[direction, 1], direction, -1),
            )
        )
    back_links.append((behind_links[0], behind_links[1]))

    def operate(field):
        padded = with_halo(field, (("site", 3),), 1)
        total_re = jnp.zeros_like(field[0])
        total_im = jnp.zeros_like(field[0])
        for direction in range(3):
            if direction < 2:
                ahead = along(field, direction, 1)
                behind = along(field, direction, -1)
            else:
                ahead = padded[:, :, :, 2:]
                behind = padded[:, :, :, :-2]
            forward = link_times(
                links_here[direction, 0], links_here[direction, 1], ahead[0], ahead[1], False
            )
            backward = link_times(
                back_links[direction][0], back_links[direction][1], behind[0], behind[1], True
            )
            total_re = total_re + forward[0] + backward[0]
            total_im = total_im + forward[1] + backward[1]
        return jnp.stack([total_re, total_im]) * (-1.0 / 6.0)

    filtered = chebyshev(vectors, operate).astype(jnp.bfloat16)
    received = lax.all_to_all(filtered, "vec", split_axis=4, concat_axis=2, tiled=True)
    grouped = received.reshape(2, 3, group_count, block, layers, portion)
    ranks = jnp.arange(group_count, dtype=jnp.int32)
    inverse = jnp.sum(
        ranks[:, None] * (block_owner[:, None] == ranks[None, :]).astype(jnp.int32), axis=0
    )
    ordered = jnp.take(grouped, inverse, axis=2).reshape(2, 3, group_count * block, layers, portion)
    nvec = group_count * block
    flat = group_rank * portion + lax.broadcasted_iota(jnp.int32, (layers, portion), 1)
    depth = site_rank * layers + lax.broadcasted_iota(jnp.int32, (layers, portion), 0)
    theta = phase_angle(momenta, flat % LX, flat // LX, depth, layers * site_count)
    values = ordered.astype(jnp.float32)
    cosine = jnp.cos(theta)[:, None, None]
    sine = jnp.sin(theta)[:, None, None]
    shift_re = cosine * values[0] + sine * values[1]
    shift_im = cosine * values[1] - sine * values[0]
    shifted = jnp.stack([shift_re, shift_im], axis=1).astype(jnp.bfloat16)
    products = jnp.einsum(
        "acizs,pbckzs->aipbk", ordered, shifted, preferred_element_type=jnp.float32
    )
    real = products[0, :, :, 0] + products[1, :, :, 1]
    imag = products[0, :, :, 1] - products[1, :, :, 0]
    momentum_count = momenta.shape[0]
    partial_sum = jnp.stack([real, imag], axis=2).reshape(nvec, momentum_count * 2 * nvec)
    tau = peramb[0]
    tau_rows = tau.reshape(-1, nvec)
    summed = lax.psum(partial_sum, ("site", "vec")).astype(jnp.bfloat16)
    joined = jnp.dot(tau_rows, summed, preferred_element_type=jnp.float32)
    sinks = tau.shape[0]
    spins = tau.shape[1]
    layout = joined.reshape(sinks, spins, 2, block, momentum_count, 2, nvec)
    real_part = layout[:, :, 0, :, :, 0] - layout[:, :, 1, :, :, 1]
    imag_part = layout[:, :, 0, :, :, 1] + layout[:, :, 1, :, :, 0]
    stacked = jnp.stack([real_part, imag_part], axis=0)
    result = jnp.transpose(stacked, (1, 2, 4, 0, 3, 5))
    return result[None].astype(jnp.bfloat16)


def choose(eigvecs, links, peramb, block_owner, momenta):
    block, layers, plane = eigvecs.shape[3:]
    sites, groups = lax.axis_size("site"), lax.axis_size("vec")
    fits = layers == 1 and plane == LX * LY == 4 * LANES and sites == 4 and groups == 2
    fits = fits and block == sites * sum(CHUNKS) and LANES < block < 2 * LANES
    fits = fits and peramb.shape[1] * peramb.shape[2] % 2 == 0 and (2 * block) % (32 * sites) == 0 and block % (2 * block // sites) == 0
    device = per_device if fits else general_device
    return device(eigvecs, links, peramb, block_owner, momenta)


def solution(mesh):
    placed = (
        P(("cfg", "tslice"), None, None, "vec", "site", None),
        P(("cfg", "tslice"), None, None, None, None, "site", None),
        P(("cfg", "tslice"), "site", None, None, "vec", None),
        P(),
        P(),
    )
    return jax.shard_map(
        choose,
        mesh=mesh,
        in_specs=placed,
        out_specs=P(("cfg", "tslice"), "site", None, None, None, "vec", None),
        check_vma=False,
    )
```

```python
import functools
import math

import jax
import jax.numpy as jnp
from jax import lax
from jax.experimental import pallas as pl
from jax.experimental.pallas import tpu as pltpu
from jax.sharding import PartitionSpec as P


LX = 32
LY = 16
LANES = 128

two_pi = 2.0 * math.pi

CHUNKS = (16, 16, 16)


def phase_angle(momenta, across, upward, depth, extent):
    return two_pi * (
        (momenta[:, 0, None, None] * across[None]).astype(jnp.float32) / LX
        + (momenta[:, 1, None, None] * upward[None]).astype(jnp.float32) / LY
        + (momenta[:, 2, None, None] * depth[None]).astype(jnp.float32) / extent
    )


VMEM = pl.BlockSpec(memory_space=pltpu.VMEM)
SMEM = pl.BlockSpec(memory_space=pltpu.SMEM)
ANY = pl.BlockSpec(memory_space=pl.ANY)
HBM = pl.BlockSpec(memory_space=pltpu.HBM)
GRANT = pltpu.CompilerParams(vmem_limit_bytes=16 * 2**20)


class Shifts:
    def __init__(self):
        lane = lax.broadcasted_iota(jnp.int32, (8, LANES), 1)
        row = lax.broadcasted_iota(jnp.int32, (8, LANES), 0) % 4
        column = lane % LX
        self.x_last = column == LX - 1
        self.x_first = column == 0
        self.y_high = lane >= LANES - LX
        self.y_low = lane < LX
        self.row_last = row == 3
        self.row_first = row == 0

    def ahead_x(self, v):
        return jnp.where(self.x_last, pltpu.roll(v, LX - 1, 1), pltpu.roll(v, LANES - 1, 1))

    def behind_x(self, v):
        return jnp.where(self.x_first, pltpu.roll(v, LANES - LX + 1, 1), pltpu.roll(v, 1, 1))

    def ahead_y(self, v):
        a = pltpu.roll(v, LANES - LX, 1)
        wrapped = jnp.where(self.row_last, pltpu.roll(a, 3, 0), pltpu.roll(a, 7, 0))
        return jnp.where(self.y_high, wrapped, a)

    def behind_y(self, v):
        a = pltpu.roll(v, LX, 1)
        wrapped = jnp.where(self.row_first, pltpu.roll(a, 5, 0), pltpu.roll(a, 1, 0))
        return jnp.where(self.y_low, wrapped, a)


def tables_kernel(*refs):
    table_ref = refs[-1]
    shifts = Shifts()
    scale = jnp.float32(-math.sqrt(2.0) / 6.0)
    size = refs[0].shape[0]
    links = [ref[ref.shape[0] - size :].astype(jnp.float32) for ref in refs[:-1]]
    count = len(links)

    def entry(plane, direction, part, row, col):
        e = direction * 18 + part * 9 + row * 3 + col
        value = links[plane % count][4 * e : 4 * e + 4] * scale
        return jnp.concatenate([value, value], axis=0)

    for plane in range(count):
        for direction in range(3):
            for target in range(3):
                for source in range(3):
                    slot = (2 * direction) * 27 + (target * 3 + source) * 3
                    re = entry(plane, direction, 0, target, source)
                    im = entry(plane, direction, 1, target, source)
                    table_ref[plane, slot] = re
                    table_ref[plane, slot + 1] = im
                    table_ref[plane, slot + 2] = re + im
                    slot = (2 * direction + 1) * 27 + (target * 3 + source) * 3
                    below = plane + 1 if direction == 2 else plane
                    re = entry(below, direction, 0, source, target)
                    im = entry(below, direction, 1, source, target)
                    if direction < 2:
                        move = shifts.behind_x if direction == 0 else shifts.behind_y
                        re, im = move(re), move(im)
                    table_ref[plane, slot] = re
                    table_ref[plane, slot + 1] = -im
                    table_ref[plane, slot + 2] = re - im


def link_tables(links):
    return pl.pallas_call(
        tables_kernel,
        out_shape=pltpu.VMEM((len(links), 162, 8, LANES), jnp.float32),
        in_specs=[VMEM] * len(links),
        out_specs=VMEM,
        compiler_params=GRANT,
        name="link_tables",
    )(*links)


def pack_kernel(sites, chunk, place_ref, own_ref, *refs):
    outs = refs[1 - sites :]
    rows = CHUNKS[chunk] * 4
    for d in range(1, sites):
        start = row_of(lax.rem(place_ref[0] + d, sites), own_ref.shape[1] // sites, chunk)
        out = outs[d - 1]
        for c in range(6):
            out[c * rows : (c + 1) * rows] = own_ref[c, pl.ds(start, rows), :].astype(jnp.bfloat16)


def first_pack_kernel(sites, own_ref, links_ref, *refs):
    outs, block_ref, link_ref, sems = refs[: sites - 1], refs[sites - 1], refs[sites], refs[sites + 1]
    rows = CHUNKS[0] * 4
    copies = [pltpu.make_async_copy(links_ref, link_ref, sems.at[0])]
    for d in range(1, sites):
        start = row_of(lax.rem(lax.axis_index("site") + d, sites), own_ref.shape[1] // sites, 0)
        copies.append(pltpu.make_async_copy(own_ref.at[:, pl.ds(start, rows), :], block_ref.at[d - 1], sems.at[d]))
    for copy in copies:
        copy.start()
    copies[0].wait()
    links = link_ref[...].astype(jnp.bfloat16)
    for d in range(1, sites):
        copies[d].wait()
        for c in range(6):
            outs[d - 1][c * rows : (c + 1) * rows] = block_ref[d - 1, c].astype(jnp.bfloat16)
        outs[d - 1][6 * rows :] = links


def first_pack(own, sites, links):
    rows = CHUNKS[0] * 4
    return pl.pallas_call(
        functools.partial(first_pack_kernel, sites),
        out_shape=[pltpu.VMEM((6 * rows + links.shape[0], LANES), jnp.bfloat16)] * (sites - 1),
        in_specs=[HBM, HBM],
        out_specs=[VMEM] * (sites - 1),
        scratch_shapes=[
            pltpu.VMEM((sites - 1, 6, rows, LANES), jnp.float32),
            pltpu.VMEM(links.shape, jnp.float32),
            pltpu.SemaphoreType.DMA((sites,)),
        ],
        compiler_params=pltpu.CompilerParams(vmem_limit_bytes=66 * 10**6),
        name="pack0",
    )(own, links)


def row_of(slot, rows_per_slot, chunk):
    return pl.multiple_of(slot * rows_per_slot + 4 * sum(CHUNKS[:chunk]), 32)


def pack(own, place, chunk, sites, after):
    length = 24 * CHUNKS[chunk]
    return pl.pallas_call(
        functools.partial(pack_kernel, sites, chunk),
        out_shape=[pltpu.VMEM((length, LANES), jnp.bfloat16)] * (sites - 1),
        in_specs=[SMEM, VMEM] + [ANY] * len(after),
        out_specs=[VMEM] * (sites - 1),
        compiler_params=GRANT,
    )(place, own, *after)


def filter_kernel(sites, chunk, place_ref, *refs):
    fields, table_ref = refs[:sites], refs[sites]
    outs, t1_ref = refs[-1 - sites : -1], refs[-1]
    shifts = Shifts()
    rows = CHUNKS[chunk] * 4
    home = row_of(place_ref[0], fields[0].shape[1] // sites, chunk)

    def hop(plane, here, ahead_z, behind_z):
        count = len(here(0))
        sums = [[[None] * count for _ in range(3)] for _ in range(3)]
        moves = (shifts.ahead_x, shifts.behind_x, shifts.ahead_y, shifts.behind_y, None, None)
        for direction in range(6):
            if direction < 4:
                field = [[moves[direction](v) for v in here(c)] for c in range(6)]
            else:
                take = ahead_z if direction == 4 else behind_z
                field = [take(c) for c in range(6)]
            for source in range(3):
                re, im = field[source], field[3 + source]
                factors = ([im[n] - re[n] for n in range(count)], [im[n] + re[n] for n in range(count)], re)
                for target in range(3):
                    slot = direction * 27 + (target * 3 + source) * 3
                    for k in range(3):
                        link = table_ref[plane, slot + k]
                        for n in range(count):
                            add = link * factors[k][n]
                            old = sums[target][k][n]
                            sums[target][k][n] = add if old is None else old + add
        total_re = [[sums[t][2][n] - sums[t][1][n] for n in range(count)] for t in range(3)]
        total_im = [[sums[t][2][n] + sums[t][0][n] for n in range(count)] for t in range(3)]
        return total_re + total_im

    def step(index, carry):
        base = pl.multiple_of(index * 16, 16)

        def start(plane):
            def read(c):
                ref = fields[plane % sites]
                if plane % sites == 0:
                    value = ref[c, pl.ds(pl.multiple_of(home + base, 16), 16), :]
                else:
                    value = ref[pl.ds(pl.multiple_of(c * rows + base, 16), 16), :].astype(jnp.float32)
                return [value[0:8], value[8:16]]

            return read

        def first(plane):
            return lambda c: [t1_ref[plane % sites, c, 0:8], t1_ref[plane % sites, c, 8:16]]

        for plane in range(sites):
            out = hop(plane, start(plane), start(plane - 1), start(plane + 1))
            for c in range(6):
                for n in range(2):
                    t1_ref[plane, c, 8 * n : 8 * n + 8] = out[c][n]
        for plane in range(sites):
            out = hop(plane, first(plane), first(plane - 1), first(plane + 1))
            for c in range(6):
                value = jnp.concatenate(out[c], axis=0)
                outs[plane][c, pl.ds(base, 16), :] = value.astype(jnp.bfloat16)
        return carry

    lax.fori_loop(0, rows // 16, step, 0)


def filter_chunk(own, place, chunk, received, table, after):
    sites = len(received) + 1
    rows = CHUNKS[chunk] * 4
    return pl.pallas_call(
        functools.partial(filter_kernel, sites, chunk),
        out_shape=[pltpu.VMEM((6, rows, LANES), jnp.bfloat16)] * sites,
        in_specs=[SMEM] + [VMEM] * (sites + 1) + [ANY] * len(after),
        out_specs=[VMEM] * sites,
        scratch_shapes=[pltpu.VMEM((sites, 6, 16, LANES), jnp.float32)],
        cost_estimate=pl.CostEstimate(
            flops=432 * 2 * sites * rows * LANES, bytes_accessed=6 * rows * LANES * 4 * sites, transcendentals=0),
        compiler_params=GRANT,
    )(place, own, *received, table, *after)


def finish_kernel(sites, chunk, place_ref, own_ref, *refs):
    hops = refs[:sites]
    cosine_ref, sine_ref = refs[sites : sites + 2]
    filtered_ref, shifted_ref, work_ref = refs[-3:]
    vectors = CHUNKS[chunk]
    momenta = cosine_ref.shape[0]
    for d in range(sites):
        slot = lax.rem(place_ref[0] + d, sites)
        start = row_of(slot, own_ref.shape[1] // sites, chunk)
        for c in range(6):
            work_ref[d, c] = hops[d][c].astype(jnp.float32) - own_ref[c, pl.ds(start, 4 * vectors), :]
        for color in range(3):
            for row in range(4):
                at = slice((color * 4 + row) * LANES, (color * 4 + row + 1) * LANES)
                re = work_ref[d, color, pl.ds(row, vectors, stride=4), :].astype(jnp.bfloat16)
                im = work_ref[d, 3 + color, pl.ds(row, vectors, stride=4), :].astype(jnp.bfloat16)
                filtered_ref[slot, 0, :, at] = re
                filtered_ref[slot, 1, :, at] = im
                re, im = re.astype(jnp.float32), im.astype(jnp.float32)
                for p in range(momenta):
                    cosine = cosine_ref[p, row : row + 1, :]
                    sine = sine_ref[p, row : row + 1, :]
                    shifted_ref[p, slot, 0, :, at] = (cosine * re + sine * im).astype(jnp.bfloat16)
                    shifted_ref[p, slot, 1, :, at] = (cosine * im - sine * re).astype(jnp.bfloat16)


def finish(own, place, chunk, hops, cosine, sine, after):
    sites, momenta, vectors = len(hops), cosine.shape[0], CHUNKS[chunk]
    shapes = ((sites, 2, vectors, 12 * LANES), (momenta, sites, 2, vectors, 12 * LANES))
    return pl.pallas_call(
        functools.partial(finish_kernel, sites, chunk),
        out_shape=[pltpu.VMEM(shape, jnp.bfloat16) for shape in shapes],
        in_specs=[SMEM] + [VMEM] * (sites + 3) + [ANY] * len(after),
        out_specs=[VMEM, VMEM],
        scratch_shapes=[pltpu.VMEM((sites, 6, 4 * vectors, LANES), jnp.float32)],
        cost_estimate=pl.CostEstimate(
            flops=20 * sites * 24 * vectors * LANES, bytes_accessed=sites * 24 * vectors * LANES * 12,
            transcendentals=0),
        compiler_params=GRANT,
    )(place, own, *hops, cosine, sine, *after)


def fill_left(left_ref, chunks):
    slots, _, _, depth = chunks[0].shape
    sizes = [ref.shape[2] for ref in chunks]
    for n, ref in enumerate(chunks):
        for slot in range(slots):
            at = slot * sum(sizes) + sum(sizes[:n])
            for part in range(2):
                left_ref[at : at + sizes[n], part * depth : (part + 1) * depth] = ref[slot, part]


def multiply(left_ref, right_ref, total_ref, place_ref, outs):
    segments, rows, _ = total_ref.shape
    for p in range(right_ref.shape[0]):
        product = lax.dot_general(
            left_ref[...], right_ref[p], (((1,), (1,)), ((), ())), preferred_element_type=jnp.float32)
        width = product.shape[1]
        for s in range(segments):
            total_ref[s, :, p * width : (p + 1) * width] = product[s * rows : (s + 1) * rows]
    for d in range(segments):
        outs[d][...] = total_ref[lax.rem(place_ref[0] + d, segments)].astype(outs[d].dtype)


def early_kernel(segments, count, place_ref, *refs):
    chunks = len(CHUNKS)
    left, shifted = refs[:count], refs[count : count + chunks]
    outs = refs[count + chunks : count + chunks + segments]
    right_ref, left_ref, total_ref = refs[count + chunks + segments :]
    slots, _, _, depth = left[0].shape
    block = right_ref.shape[1] // 2
    fill_left(left_ref, left)
    for p in range(right_ref.shape[0]):
        for n, ref in enumerate(shifted):
            for slot in range(slots):
                re, im = ref[p, slot, 0], ref[p, slot, 1]
                at = slot * sum(CHUNKS) + sum(CHUNKS[:n])
                low, high = slice(at, at + CHUNKS[n]), slice(block + at, block + at + CHUNKS[n])
                right_ref[p, low, :depth] = re
                right_ref[p, low, depth:] = im
                right_ref[p, high, :depth] = im
                right_ref[p, high, depth:] = -re
    multiply(left_ref, right_ref, total_ref, place_ref, outs)


def late_kernel(segments, count, place_ref, *refs):
    left, right_ref = refs[:count], refs[count]
    outs = refs[count + 1 : count + 1 + segments]
    left_ref, total_ref = refs[count + 1 + segments :]
    fill_left(left_ref, left)
    multiply(left_ref, right_ref, total_ref, place_ref, outs)


def elementals(place, left, shifted, right, segments):
    _, _, _, depth = left[0].shape
    block = segments * sum(CHUNKS)
    rows = sum(ref.shape[2] for ref in left)
    early = right is None
    momenta = shifted[0].shape[0] if early else right.shape[0]
    columns = momenta * 2 * block
    shapes = [pltpu.VMEM((rows, columns), jnp.float32 if d == 0 else jnp.bfloat16) for d in range(segments)]
    if early:
        shapes.append(pltpu.VMEM((momenta, 2 * block, 2 * depth), jnp.bfloat16))
    operands = [*left, *shifted] if early else [*left, right]
    return pl.pallas_call(
        functools.partial(early_kernel if early else late_kernel, segments, len(left)),
        out_shape=shapes,
        in_specs=[SMEM] + [VMEM] * len(operands),
        out_specs=[VMEM] * len(shapes),
        scratch_shapes=[
            pltpu.VMEM((segments * rows, 2 * depth), jnp.bfloat16),
            pltpu.VMEM((segments, rows, columns), jnp.float32),
        ],
        cost_estimate=pl.CostEstimate(
            flops=2 * segments * rows * columns * 2 * depth, bytes_accessed=8 * block * depth, transcendentals=0),
        compiler_params=GRANT,
        name="elementals_early" if early else "elementals_late",
    )(place, *operands)


def add_kernel(count, *refs):
    out_ref, at = refs[-1], 0
    for group in (refs[:count], refs[count:-1]):
        total = group[0][...]
        for ref in group[1:]:
            total = total + ref[...].astype(jnp.float32)
        out_ref[at : at + total.shape[0]] = total.astype(jnp.bfloat16)
        at += total.shape[0]


def add_parts(early, late):
    rows = early[0].shape[0] + late[0].shape[0]
    return pl.pallas_call(
        functools.partial(add_kernel, len(early)),
        out_shape=pltpu.VMEM((rows, early[0].shape[1]), jnp.bfloat16),
        in_specs=[VMEM] * (len(early) + len(late)),
        out_specs=VMEM,
        compiler_params=GRANT,
        name="add_parts",
    )(*early, *late)


def fill_right(right_ref, pieces, across, place_ref, owner_ref):
    sites = len(pieces)
    nvec = right_ref.shape[0] // 2
    momenta = right_ref.shape[1] // (3 * LANES)
    block = nvec // 2
    half = block - LANES
    rows = block // sites
    v = lax.rem(place_ref[1] + across, 2)
    leads = owner_ref[v] == 0

    def tiles(re, im):
        lead = (re[:, :LANES], im[:, :LANES], jnp.concatenate([re[:, LANES:], im[:, LANES:]], axis=1))
        other = (re[:, half:], im[:, half:], jnp.concatenate([im[:, :half], re[:, :half]], axis=1))
        return [jnp.where(leads, x, y) for x, y in zip(lead, other)]

    for up, piece in enumerate(pieces):
        z = lax.rem(place_ref[0] + up, sites)
        for part, owner in ((0, owner_ref[v]), (1, owner_ref[1 - v])):
            row = pl.multiple_of(owner * block + z * rows, 16)
            low = pl.multiple_of(nvec + owner * block + z * rows, 16)
            for p in range(momenta):
                value = piece[part * rows : (part + 1) * rows, p * 2 * block : (p + 1) * 2 * block]
                re, im = value[:, :block], value[:, block:]
                for at, (first, second, ends) in ((row, tiles(re, im)), (low, tiles(-im, re))):
                    right_ref[pl.ds(at, rows), 2 * p * LANES : (2 * p + 1) * LANES] = first
                    right_ref[pl.ds(at, rows), (2 * p + 1) * LANES : (2 * p + 2) * LANES] = second
                    last = (2 * momenta + p) * LANES
                    right_ref[pl.ds(at, rows), last : last + LANES] = ends


def pair_of(tau_ref, n):
    left = [jnp.concatenate([tau_ref[n + k, 0], tau_ref[n + k, 1]], axis=1) for k in range(2)]
    return jnp.concatenate(left, axis=0)


def first_kernel(sites, place_ref, owner_ref, tau_ref, *refs):
    pieces, (out_ref, right_ref) = refs[:sites], refs[sites:]
    fill_right(right_ref, pieces, 0, place_ref, owner_ref)
    rows = tau_ref.shape[2]

    def step(n, carry):
        product = jnp.dot(pair_of(tau_ref, 2 * n), right_ref[...], preferred_element_type=jnp.float32)
        for k in range(2):
            out_ref[2 * n + k] = product[k * rows : (k + 1) * rows].astype(jnp.bfloat16)
        return carry

    lax.fori_loop(0, tau_ref.shape[0] // 2, step, 0)


def second_kernel(sites, place_ref, owner_ref, tau_ref, first_ref, *refs):
    pieces, (out_ref, right_ref) = refs[:sites], refs[sites:]

    @pl.when(pl.program_id(0) == 0)
    def assemble():
        fill_right(right_ref, pieces, 1, place_ref, owner_ref)

    leads = owner_ref[place_ref[1]] == 0
    rows = tau_ref.shape[2]
    momenta = out_ref.shape[1]
    lower = lax.broadcasted_iota(jnp.int32, (rows, LANES), 1) < LANES // 2
    both = jnp.dot(pair_of(tau_ref, 0), right_ref[...], preferred_element_type=jnp.float32)
    for k in range(2):

        def ordered(tile):
            mine = first_ref[k, :, tile * LANES : (tile + 1) * LANES].astype(jnp.float32)
            theirs = both[k * rows : (k + 1) * rows, tile * LANES : (tile + 1) * LANES]
            return jnp.where(leads, mine, theirs), jnp.where(leads, theirs, mine)

        for p in range(momenta):
            low_ends, high_ends = ordered(2 * momenta + p)
            middles = (jnp.where(lower, low_ends, high_ends),
                       pltpu.roll(jnp.where(lower, high_ends, low_ends), LANES // 2, 1))
            for c in range(2):
                low, high = ordered(2 * p + c)
                out_ref[k, p, c, :, :LANES] = low.astype(jnp.bfloat16)
                out_ref[k, p, c, :, LANES : 2 * LANES] = middles[c].astype(jnp.bfloat16)
                out_ref[k, p, c, :, 2 * LANES :] = high.astype(jnp.bfloat16)


def project_first(tau, place, owner, pieces, momenta):
    outer, _, rows, nvec = tau.shape
    return pl.pallas_call(
        functools.partial(first_kernel, len(pieces)),
        out_shape=pltpu.VMEM((outer, rows, momenta * 3 * LANES), jnp.bfloat16),
        in_specs=[SMEM, SMEM] + [VMEM] * (1 + len(pieces)),
        out_specs=VMEM,
        scratch_shapes=[pltpu.VMEM((2 * nvec, momenta * 3 * LANES), jnp.bfloat16)],
        cost_estimate=pl.CostEstimate(
            flops=2 * outer * rows * 2 * nvec * nvec * momenta, bytes_accessed=outer * rows * nvec * 8,
            transcendentals=0),
        compiler_params=GRANT,
        name="project_first",
    )(place, owner, tau, *pieces)


def project_second(tau, place, owner, first, pieces, momenta):
    outer, _, rows, nvec = tau.shape
    return pl.pallas_call(
        functools.partial(second_kernel, len(pieces)),
        grid=(outer // 2,),
        out_shape=jax.ShapeDtypeStruct((outer, momenta, 2, rows, nvec), jnp.bfloat16),
        in_specs=[SMEM, SMEM, pl.BlockSpec((2, 2, rows, nvec), lambda i: (i, 0, 0, 0)),
                  pl.BlockSpec((2, *first.shape[1:]), lambda i: (i, 0, 0))] + [VMEM] * len(pieces),
        out_specs=pl.BlockSpec((2, momenta, 2, rows, nvec), lambda i: (i, 0, 0, 0, 0)),
        scratch_shapes=[pltpu.VMEM((2 * nvec, momenta * 3 * LANES), jnp.bfloat16)],
        cost_estimate=pl.CostEstimate(
            flops=2 * outer * rows * 2 * nvec * nvec * momenta, bytes_accessed=outer * rows * nvec * 12,
            transcendentals=0),
        compiler_params=GRANT,
        name="project_second",
    )(place, owner, tau, first, *pieces)


def from_place(block, up, across):
    sites, groups = lax.axis_size("site"), lax.axis_size("vec")
    route = []
    for z in range(sites):
        for v in range(groups):
            route.append((((z + up) % sites) * groups + (v + across) % groups, z * groups + v))
    return lax.ppermute(block, ("site", "vec"), route)


ORDER = (("filter", 0), ("filter", 1), ("finish", 0), ("filter", 2), ("finish", 1), ("finish", 2))


def per_device(eigvecs, links, peramb, block_owner, momenta):
    sites = lax.axis_size("site")
    site, group = lax.axis_index("site"), lax.axis_index("vec")
    block = eigvecs.shape[3]
    own = eigvecs.reshape(6, block * 4, LANES)
    own_links = links.reshape(216, LANES)
    place = jnp.stack([site, group]).astype(jnp.int32)

    received, packed = [], []
    for chunk in range(len(CHUNKS)):
        after = packed[:1]
        if chunk == 2:
            after = [received[0][0], packed[0]]
        if chunk == 0:
            packed = first_pack(own, sites, own_links)
        else:
            packed = pack(own, place, chunk, sites, after)
        received.append([from_place(packed[d - 1], -d, 0) for d in range(1, sites)])

    flat = lax.broadcasted_iota(jnp.int32, (4, LANES), 0) * LANES + lax.broadcasted_iota(jnp.int32, (4, LANES), 1)
    theta = phase_angle(momenta, flat % LX, flat // LX, jnp.full_like(flat, site), sites)
    cosine, sine = jnp.cos(theta), jnp.sin(theta)

    table = link_tables([own_links] + received[0])
    hops, filtered, shifted, other = {}, {}, {}, {}
    last = None
    for kind, chunk in ORDER:
        after = [] if last is None else [last]
        if kind == "filter":
            out = filter_chunk(own, place, chunk, received[chunk], table, after)
            hops[chunk] = [out[0]] + [from_place(out[d], d, 0) for d in range(1, sites)]
            last = out[0]
        else:
            f, s = finish(own, place, chunk, hops[chunk], cosine, sine, after)
            other[chunk] = from_place(f, 0, 1)
            filtered[chunk], shifted[chunk] = f, s
            last = s
    filtered, shifted, other = ([group_of[n] for n in range(len(CHUNKS))] for group_of in (filtered, shifted, other))

    *parts, right = elementals(place, filtered + other[:1], shifted, None, sites)
    sent = [from_place(parts[d], -d, 0) for d in range(1, sites)]
    early = [parts[0], *sent]
    parts = elementals(place, other[1:], None, right, sites)
    sent = [from_place(parts[d], -d, 0) for d in range(1, sites)]
    mine = add_parts(early, [parts[0], *sent])

    across = [from_place(mine, 0, 1)]
    pieces = [mine] + [from_place(mine, up, 0) for up in range(1, sites)]
    across += [from_place(piece, 0, 1) for piece in pieces[1:]]
    sinks, spins = peramb.shape[1], peramb.shape[2]
    tau = peramb.reshape(sinks * spins, 2, block, peramb.shape[5])
    first = project_first(tau, place, block_owner, pieces, momenta.shape[0])
    result = project_second(tau, place, block_owner, first, across, momenta.shape[0])
    return result.reshape(1, sinks, spins, momenta.shape[0], 2, block, peramb.shape[5])


def from_behind(block, axis, distance):
    devices = range(lax.axis_size(axis))
    route = [((i - distance) % len(devices), i) for i in devices]
    return lax.ppermute(block, axis, route)


def with_halo(block, sides, width):
    for axis, dim in sides:
        count = lax.axis_size(axis)
        forward = [(i, i + 1) for i in range(count - 1)]
        forward.append((count - 1, 0))
        backward = [(target, source) for source, target in forward]
        low = lax.ppermute(
            lax.slice_in_dim(block, block.shape[dim] - width, None, axis=dim), axis, forward
        )
        high = lax.ppermute(lax.slice_in_dim(block, 0, width, axis=dim), axis, backward)
        block = jnp.concatenate([low, block, high], axis=dim)
    return block


def along(field, direction, sense):
    width = field.shape[-1]
    column = lax.broadcasted_iota(jnp.int32, (width,), 0) % LX
    if direction == 0:
        if sense > 0:
            return jnp.where(column == LX - 1, jnp.roll(field, LX - 1, -1), jnp.roll(field, -1, -1))
        return jnp.where(column == 0, jnp.roll(field, 1 - LX, -1), jnp.roll(field, 1, -1))
    return jnp.roll(field, -sense * LX, -1)


def link_times(link_re, link_im, field_re, field_im, dagger):
    result_re = []
    result_im = []
    for target in range(3):
        summed_re = jnp.zeros_like(field_re[0])
        summed_im = jnp.zeros_like(field_re[0])
        for source in range(3):
            if dagger:
                entry_re = link_re[source, target][None]
                entry_im = -link_im[source, target][None]
            else:
                entry_re = link_re[target, source][None]
                entry_im = link_im[target, source][None]
            summed_re = summed_re + entry_re * field_re[source] - entry_im * field_im[source]
            summed_im = summed_im + entry_re * field_im[source] + entry_im * field_re[source]
        result_re.append(summed_re)
        result_im.append(summed_im)
    return (jnp.stack(result_re), jnp.stack(result_im))


def chebyshev(initial, operate):
    current = operate(initial)
    following = 2.0 * operate(current) - initial
    return following


def general_device(eigvecs, links, peramb, block_owner, momenta):
    vectors = eigvecs[0]
    links_here = links[0]
    block = vectors.shape[2]
    layers = vectors.shape[3]
    plane = vectors.shape[4]
    site_count = lax.axis_size("site")
    group_count = lax.axis_size("vec")
    site_rank = lax.axis_index("site")
    group_rank = lax.axis_index("vec")
    portion = plane // group_count
    top_plane = links_here[2, :, :, :, layers - 1 :, :]
    below = from_behind(top_plane, "site", 1)
    behind_links = jnp.concatenate([below, links_here[2, :, :, :, : layers - 1, :]], axis=3)
    back_links = []
    for direction in range(2):
        back_links.append(
            (
                along(links_here[direction, 0], direction, -1),
                along(links_here[direction, 1], direction, -1),
            )
        )
    back_links.append((behind_links[0], behind_links[1]))

    def operate(field):
        padded = with_halo(field, (("site", 3),), 1)
        total_re = jnp.zeros_like(field[0])
        total_im = jnp.zeros_like(field[0])
        for direction in range(3):
            if direction < 2:
                ahead = along(field, direction, 1)
                behind = along(field, direction, -1)
            else:
                ahead = padded[:, :, :, 2:]
                behind = padded[:, :, :, :-2]
            forward = link_times(
                links_here[direction, 0], links_here[direction, 1], ahead[0], ahead[1], False
            )
            backward = link_times(
                back_links[direction][0], back_links[direction][1], behind[0], behind[1], True
            )
            total_re = total_re + forward[0] + backward[0]
            total_im = total_im + forward[1] + backward[1]
        return jnp.stack([total_re, total_im]) * (-1.0 / 6.0)

    filtered = chebyshev(vectors, operate).astype(jnp.bfloat16)
    received = lax.all_to_all(filtered, "vec", split_axis=4, concat_axis=2, tiled=True)
    grouped = received.reshape(2, 3, group_count, block, layers, portion)
    ranks = jnp.arange(group_count, dtype=jnp.int32)
    inverse = jnp.sum(
        ranks[:, None] * (block_owner[:, None] == ranks[None, :]).astype(jnp.int32), axis=0
    )
    ordered = jnp.take(grouped, inverse, axis=2).reshape(2, 3, group_count * block, layers, portion)
    nvec = group_count * block
    flat = group_rank * portion + lax.broadcasted_iota(jnp.int32, (layers, portion), 1)
    depth = site_rank * layers + lax.broadcasted_iota(jnp.int32, (layers, portion), 0)
    theta = phase_angle(momenta, flat % LX, flat // LX, depth, layers * site_count)
    values = ordered.astype(jnp.float32)
    cosine = jnp.cos(theta)[:, None, None]
    sine = jnp.sin(theta)[:, None, None]
    shift_re = cosine * values[0] + sine * values[1]
    shift_im = cosine * values[1] - sine * values[0]
    shifted = jnp.stack([shift_re, shift_im], axis=1).astype(jnp.bfloat16)
    products = jnp.einsum(
        "acizs,pbckzs->aipbk", ordered, shifted, preferred_element_type=jnp.float32
    )
    real = products[0, :, :, 0] + products[1, :, :, 1]
    imag = products[0, :, :, 1] - products[1, :, :, 0]
    momentum_count = momenta.shape[0]
    partial_sum = jnp.stack([real, imag], axis=2).reshape(nvec, momentum_count * 2 * nvec)
    tau = peramb[0]
    tau_rows = tau.reshape(-1, nvec)
    summed = lax.psum(partial_sum, ("site", "vec")).astype(jnp.bfloat16)
    joined = jnp.dot(tau_rows, summed, preferred_element_type=jnp.float32)
    sinks = tau.shape[0]
    spins = tau.shape[1]
    layout = joined.reshape(sinks, spins, 2, block, momentum_count, 2, nvec)
    real_part = layout[:, :, 0, :, :, 0] - layout[:, :, 1, :, :, 1]
    imag_part = layout[:, :, 0, :, :, 1] + layout[:, :, 1, :, :, 0]
    stacked = jnp.stack([real_part, imag_part], axis=0)
    result = jnp.transpose(stacked, (1, 2, 4, 0, 3, 5))
    return result[None].astype(jnp.bfloat16)


def choose(eigvecs, links, peramb, block_owner, momenta):
    block, layers, plane = eigvecs.shape[3:]
    sites, groups = lax.axis_size("site"), lax.axis_size("vec")
    fits = layers == 1 and plane == LX * LY == 4 * LANES and sites == 4 and groups == 2
    fits = fits and block == sites * sum(CHUNKS) and 2 * block == 3 * LANES
    fits = fits and peramb.shape[1] * peramb.shape[2] % 2 == 0 and (2 * block) % (32 * sites) == 0 and block % (2 * block // sites) == 0
    device = per_device if fits else general_device
    return device(eigvecs, links, peramb, block_owner, momenta)


def solution(mesh):
    placed = (
        P(("cfg", "tslice"), None, None, "vec", "site", None),
        P(("cfg", "tslice"), None, None, None, None, "site", None),
        P(("cfg", "tslice"), "site", None, None, "vec", None),
        P(),
        P(),
    )
    return jax.shard_map(
        choose,
        mesh=mesh,
        in_specs=placed,
        out_specs=P(("cfg", "tslice"), "site", None, None, None, "vec", None),
        check_vma=False,
    )
```

```python
import functools
import math

import jax
import jax.numpy as jnp
from jax import lax
from jax.experimental import pallas as pl
from jax.experimental.pallas import tpu as pltpu
from jax.sharding import PartitionSpec as P


LX = 32
LY = 16
LANES = 128

two_pi = 2.0 * math.pi

CHUNKS = (16, 16, 16)


def phase_angle(momenta, across, upward, depth, extent):
    return two_pi * (
        (momenta[:, 0, None, None] * across[None]).astype(jnp.float32) / LX
        + (momenta[:, 1, None, None] * upward[None]).astype(jnp.float32) / LY
        + (momenta[:, 2, None, None] * depth[None]).astype(jnp.float32) / extent
    )


VMEM = pl.BlockSpec(memory_space=pltpu.VMEM)
SMEM = pl.BlockSpec(memory_space=pltpu.SMEM)
ANY = pl.BlockSpec(memory_space=pl.ANY)
HBM = pl.BlockSpec(memory_space=pltpu.HBM)
GRANT = pltpu.CompilerParams(vmem_limit_bytes=16 * 2**20)


class Shifts:
    def __init__(self):
        lane = lax.broadcasted_iota(jnp.int32, (8, LANES), 1)
        row = lax.broadcasted_iota(jnp.int32, (8, LANES), 0) % 4
        column = lane % LX
        self.x_last = column == LX - 1
        self.x_first = column == 0
        self.y_high = lane >= LANES - LX
        self.y_low = lane < LX
        self.row_last = row == 3
        self.row_first = row == 0

    def ahead_x(self, v):
        return jnp.where(self.x_last, pltpu.roll(v, LX - 1, 1), pltpu.roll(v, LANES - 1, 1))

    def behind_x(self, v):
        return jnp.where(self.x_first, pltpu.roll(v, LANES - LX + 1, 1), pltpu.roll(v, 1, 1))

    def ahead_y(self, v):
        a = pltpu.roll(v, LANES - LX, 1)
        wrapped = jnp.where(self.row_last, pltpu.roll(a, 3, 0), pltpu.roll(a, 7, 0))
        return jnp.where(self.y_high, wrapped, a)

    def behind_y(self, v):
        a = pltpu.roll(v, LX, 1)
        wrapped = jnp.where(self.row_first, pltpu.roll(a, 5, 0), pltpu.roll(a, 1, 0))
        return jnp.where(self.y_low, wrapped, a)


def tables_kernel(*refs):
    table_ref = refs[-1]
    shifts = Shifts()
    scale = jnp.float32(-math.sqrt(2.0) / 6.0)
    size = refs[0].shape[0]
    links = [ref[ref.shape[0] - size :].astype(jnp.float32) for ref in refs[:-1]]
    count = len(links)

    def entry(plane, direction, part, row, col):
        e = direction * 18 + part * 9 + row * 3 + col
        value = links[plane % count][4 * e : 4 * e + 4] * scale
        return jnp.concatenate([value, value], axis=0)

    for plane in range(count):
        for direction in range(3):
            for target in range(3):
                for source in range(3):
                    slot = (2 * direction) * 27 + (target * 3 + source) * 3
                    re = entry(plane, direction, 0, target, source)
                    im = entry(plane, direction, 1, target, source)
                    table_ref[plane, slot] = re
                    table_ref[plane, slot + 1] = im
                    table_ref[plane, slot + 2] = re + im
                    slot = (2 * direction + 1) * 27 + (target * 3 + source) * 3
                    below = plane + 1 if direction == 2 else plane
                    re = entry(below, direction, 0, source, target)
                    im = entry(below, direction, 1, source, target)
                    if direction < 2:
                        move = shifts.behind_x if direction == 0 else shifts.behind_y
                        re, im = move(re), move(im)
                    table_ref[plane, slot] = re
                    table_ref[plane, slot + 1] = -im
                    table_ref[plane, slot + 2] = re - im


def link_tables(links):
    return pl.pallas_call(
        tables_kernel,
        out_shape=pltpu.VMEM((len(links), 162, 8, LANES), jnp.float32),
        in_specs=[VMEM] * len(links),
        out_specs=VMEM,
        compiler_params=GRANT,
        name="link_tables",
    )(*links)


def pack_kernel(sites, chunk, place_ref, own_ref, *refs):
    outs = refs[1 - sites :]
    rows = CHUNKS[chunk] * 4
    for d in range(1, sites):
        start = row_of(lax.rem(place_ref[0] + d, sites), own_ref.shape[1] // sites, chunk)
        out = outs[d - 1]
        for c in range(6):
            out[c * rows : (c + 1) * rows] = own_ref[c, pl.ds(start, rows), :].astype(jnp.bfloat16)


def first_pack_kernel(sites, own_ref, links_ref, *refs):
    outs, block_ref, link_ref, sems = refs[: sites - 1], refs[sites - 1], refs[sites], refs[sites + 1]
    rows = CHUNKS[0] * 4
    copies = [pltpu.make_async_copy(links_ref, link_ref, sems.at[0])]
    for d in range(1, sites):
        start = row_of(lax.rem(lax.axis_index("site") + d, sites), own_ref.shape[1] // sites, 0)
        copies.append(pltpu.make_async_copy(own_ref.at[:, pl.ds(start, rows), :], block_ref.at[d - 1], sems.at[d]))
    for copy in copies:
        copy.start()
    copies[0].wait()
    links = link_ref[...].astype(jnp.bfloat16)
    for d in range(1, sites):
        copies[d].wait()
        for c in range(6):
            outs[d - 1][c * rows : (c + 1) * rows] = block_ref[d - 1, c].astype(jnp.bfloat16)
        outs[d - 1][6 * rows :] = links


def first_pack(own, sites, links):
    rows = CHUNKS[0] * 4
    return pl.pallas_call(
        functools.partial(first_pack_kernel, sites),
        out_shape=[pltpu.VMEM((6 * rows + links.shape[0], LANES), jnp.bfloat16)] * (sites - 1),
        in_specs=[HBM, HBM],
        out_specs=[VMEM] * (sites - 1),
        scratch_shapes=[
            pltpu.VMEM((sites - 1, 6, rows, LANES), jnp.float32),
            pltpu.VMEM(links.shape, jnp.float32),
            pltpu.SemaphoreType.DMA((sites,)),
        ],
        compiler_params=pltpu.CompilerParams(vmem_limit_bytes=66 * 10**6),
        name="pack0",
    )(own, links)


def row_of(slot, rows_per_slot, chunk):
    return pl.multiple_of(slot * rows_per_slot + 4 * sum(CHUNKS[:chunk]), 32)


def pack(own, place, chunk, sites, after):
    length = 24 * CHUNKS[chunk]
    return pl.pallas_call(
        functools.partial(pack_kernel, sites, chunk),
        out_shape=[pltpu.VMEM((length, LANES), jnp.bfloat16)] * (sites - 1),
        in_specs=[SMEM, VMEM] + [ANY] * len(after),
        out_specs=[VMEM] * (sites - 1),
        compiler_params=GRANT,
    )(place, own, *after)


def filter_kernel(sites, chunk, place_ref, *refs):
    fields, table_ref = refs[:sites], refs[sites]
    outs, t1_ref = refs[-1 - sites : -1], refs[-1]
    shifts = Shifts()
    rows = CHUNKS[chunk] * 4
    home = row_of(place_ref[0], fields[0].shape[1] // sites, chunk)

    def hop(plane, here, ahead_z, behind_z):
        count = len(here(0))
        sums = [[[None] * count for _ in range(3)] for _ in range(3)]
        moves = (shifts.ahead_x, shifts.behind_x, shifts.ahead_y, shifts.behind_y, None, None)
        for direction in range(6):
            if direction < 4:
                field = [[moves[direction](v) for v in here(c)] for c in range(6)]
            else:
                take = ahead_z if direction == 4 else behind_z
                field = [take(c) for c in range(6)]
            for source in range(3):
                re, im = field[source], field[3 + source]
                factors = ([im[n] - re[n] for n in range(count)], [im[n] + re[n] for n in range(count)], re)
                for target in range(3):
                    slot = direction * 27 + (target * 3 + source) * 3
                    for k in range(3):
                        link = table_ref[plane, slot + k]
                        for n in range(count):
                            add = link * factors[k][n]
                            old = sums[target][k][n]
                            sums[target][k][n] = add if old is None else old + add
        total_re = [[sums[t][2][n] - sums[t][1][n] for n in range(count)] for t in range(3)]
        total_im = [[sums[t][2][n] + sums[t][0][n] for n in range(count)] for t in range(3)]
        return total_re + total_im

    def step(index, carry):
        base = pl.multiple_of(index * 16, 16)

        def start(plane):
            def read(c):
                ref = fields[plane % sites]
                if plane % sites == 0:
                    value = ref[c, pl.ds(pl.multiple_of(home + base, 16), 16), :]
                else:
                    value = ref[pl.ds(pl.multiple_of(c * rows + base, 16), 16), :].astype(jnp.float32)
                return [value[0:8], value[8:16]]

            return read

        def first(plane):
            return lambda c: [t1_ref[plane % sites, c, 0:8], t1_ref[plane % sites, c, 8:16]]

        for plane in range(sites):
            out = hop(plane, start(plane), start(plane - 1), start(plane + 1))
            for c in range(6):
                for n in range(2):
                    t1_ref[plane, c, 8 * n : 8 * n + 8] = out[c][n]
        for plane in range(sites):
            out = hop(plane, first(plane), first(plane - 1), first(plane + 1))
            for c in range(6):
                value = jnp.concatenate(out[c], axis=0)
                outs[plane][c, pl.ds(base, 16), :] = value.astype(jnp.bfloat16)
        return carry

    lax.fori_loop(0, rows // 16, step, 0)


def filter_chunk(own, place, chunk, received, table, after):
    sites = len(received) + 1
    rows = CHUNKS[chunk] * 4
    return pl.pallas_call(
        functools.partial(filter_kernel, sites, chunk),
        out_shape=[pltpu.VMEM((6, rows, LANES), jnp.bfloat16)] * sites,
        in_specs=[SMEM] + [VMEM] * (sites + 1) + [ANY] * len(after),
        out_specs=[VMEM] * sites,
        scratch_shapes=[pltpu.VMEM((sites, 6, 16, LANES), jnp.float32)],
        cost_estimate=pl.CostEstimate(
            flops=432 * 2 * sites * rows * LANES, bytes_accessed=6 * rows * LANES * 4 * sites, transcendentals=0),
        compiler_params=GRANT,
    )(place, own, *received, table, *after)


def finish_kernel(sites, chunk, place_ref, own_ref, *refs):
    hops = refs[:sites]
    cosine_ref, sine_ref = refs[sites : sites + 2]
    filtered_ref, shifted_ref, work_ref = refs[-3:]
    vectors = CHUNKS[chunk]
    momenta = cosine_ref.shape[0]
    for d in range(sites):
        slot = lax.rem(place_ref[0] + d, sites)
        start = row_of(slot, own_ref.shape[1] // sites, chunk)
        for c in range(6):
            work_ref[d, c] = hops[d][c].astype(jnp.float32) - own_ref[c, pl.ds(start, 4 * vectors), :]
        for color in range(3):
            for row in range(4):
                at = slice((color * 4 + row) * LANES, (color * 4 + row + 1) * LANES)
                re = work_ref[d, color, pl.ds(row, vectors, stride=4), :].astype(jnp.bfloat16)
                im = work_ref[d, 3 + color, pl.ds(row, vectors, stride=4), :].astype(jnp.bfloat16)
                filtered_ref[slot, 0, :, at] = re
                filtered_ref[slot, 1, :, at] = im
                re, im = re.astype(jnp.float32), im.astype(jnp.float32)
                for p in range(momenta):
                    cosine = cosine_ref[p, row : row + 1, :]
                    sine = sine_ref[p, row : row + 1, :]
                    shifted_ref[p, slot, 0, :, at] = (cosine * re + sine * im).astype(jnp.bfloat16)
                    shifted_ref[p, slot, 1, :, at] = (cosine * im - sine * re).astype(jnp.bfloat16)


def finish(own, place, chunk, hops, cosine, sine, after):
    sites, momenta, vectors = len(hops), cosine.shape[0], CHUNKS[chunk]
    shapes = ((sites, 2, vectors, 12 * LANES), (momenta, sites, 2, vectors, 12 * LANES))
    return pl.pallas_call(
        functools.partial(finish_kernel, sites, chunk),
        out_shape=[pltpu.VMEM(shape, jnp.bfloat16) for shape in shapes],
        in_specs=[SMEM] + [VMEM] * (sites + 3) + [ANY] * len(after),
        out_specs=[VMEM, VMEM],
        scratch_shapes=[pltpu.VMEM((sites, 6, 4 * vectors, LANES), jnp.float32)],
        cost_estimate=pl.CostEstimate(
            flops=20 * sites * 24 * vectors * LANES, bytes_accessed=sites * 24 * vectors * LANES * 12,
            transcendentals=0),
        compiler_params=GRANT,
    )(place, own, *hops, cosine, sine, *after)


def fill_left(left_ref, chunks):
    slots, _, _, depth = chunks[0].shape
    sizes = [ref.shape[2] for ref in chunks]
    for n, ref in enumerate(chunks):
        for slot in range(slots):
            at = slot * sum(sizes) + sum(sizes[:n])
            for part in range(2):
                left_ref[at : at + sizes[n], part * depth : (part + 1) * depth] = ref[slot, part]


def multiply(left_ref, right_ref, total_ref, place_ref, outs):
    segments, rows, _ = total_ref.shape
    for p in range(right_ref.shape[0]):
        product = lax.dot_general(
            left_ref[...], right_ref[p], (((1,), (1,)), ((), ())), preferred_element_type=jnp.float32)
        width = product.shape[1]
        for s in range(segments):
            total_ref[s, :, p * width : (p + 1) * width] = product[s * rows : (s + 1) * rows]
    for d in range(segments):
        outs[d][...] = total_ref[lax.rem(place_ref[0] + d, segments)].astype(outs[d].dtype)


def column_of(unit, units, leads):
    tile, half = LANES // 16, LANES // 32
    if unit < tile:
        first = (unit * 16, LANES + unit * 16)
    else:
        first = (2 * LANES + (unit - tile) * 16, 2 * LANES + (unit - tile + half) * 16)
    if unit < units - tile:
        second = (2 * LANES + (unit + half) * 16, 2 * LANES + unit * 16)
    else:
        at = (unit - units + tile) * 16
        second = (at, LANES + at)
    return [pl.multiple_of(jnp.where(leads, x, y), 16) for x, y in zip(first, second)]


def early_kernel(segments, count, place_ref, owner_ref, *refs):
    chunks = len(CHUNKS)
    left, shifted = refs[:count], refs[count : count + chunks]
    outs = refs[count + chunks : count + chunks + segments]
    right_ref, left_ref, total_ref = refs[count + chunks + segments :]
    slots, _, _, depth = left[0].shape
    block = right_ref.shape[1] // 2
    fill_left(left_ref, left)
    leads = owner_ref[place_ref[1]] == 0
    for n, ref in enumerate(shifted):
        for slot in range(slots):
            for part in range(CHUNKS[n] // 16):
                unit = (slot * sum(CHUNKS) + sum(CHUNKS[:n])) // 16 + part
                real, imaginary = column_of(unit, block // 16, leads)
                for p in range(right_ref.shape[0]):
                    re = ref[p, slot, 0, part * 16 : part * 16 + 16]
                    im = ref[p, slot, 1, part * 16 : part * 16 + 16]
                    right_ref[p, pl.ds(real, 16), :depth] = re
                    right_ref[p, pl.ds(real, 16), depth:] = im
                    right_ref[p, pl.ds(imaginary, 16), :depth] = im
                    right_ref[p, pl.ds(imaginary, 16), depth:] = -re
    multiply(left_ref, right_ref, total_ref, place_ref, outs)


def late_kernel(segments, count, place_ref, *refs):
    left, right_ref = refs[:count], refs[count]
    outs = refs[count + 1 : count + 1 + segments]
    left_ref, total_ref = refs[count + 1 + segments :]
    fill_left(left_ref, left)
    multiply(left_ref, right_ref, total_ref, place_ref, outs)


def elementals(place, owner, left, shifted, right, segments):
    _, _, _, depth = left[0].shape
    block = segments * sum(CHUNKS)
    rows = sum(ref.shape[2] for ref in left)
    early = right is None
    momenta = shifted[0].shape[0] if early else right.shape[0]
    columns = momenta * 2 * block
    shapes = [pltpu.VMEM((rows, columns), jnp.float32 if d == 0 else jnp.bfloat16) for d in range(segments)]
    if early:
        shapes.append(pltpu.VMEM((momenta, 2 * block, 2 * depth), jnp.bfloat16))
    operands = [*left, *shifted] if early else [*left, right]
    scalars = [place, owner] if early else [place]
    return pl.pallas_call(
        functools.partial(early_kernel if early else late_kernel, segments, len(left)),
        out_shape=shapes,
        in_specs=[SMEM] * len(scalars) + [VMEM] * len(operands),
        out_specs=[VMEM] * len(shapes),
        scratch_shapes=[
            pltpu.VMEM((segments * rows, 2 * depth), jnp.bfloat16),
            pltpu.VMEM((segments, rows, columns), jnp.float32),
        ],
        cost_estimate=pl.CostEstimate(
            flops=2 * segments * rows * columns * 2 * depth, bytes_accessed=8 * block * depth, transcendentals=0),
        compiler_params=GRANT,
        name="elementals_early" if early else "elementals_late",
    )(*scalars, *operands)


def add_kernel(count, *refs):
    out_ref, at = refs[-1], 0
    for group in (refs[:count], refs[count:-1]):
        total = group[0][...]
        for ref in group[1:]:
            total = total + ref[...].astype(jnp.float32)
        out_ref[at : at + total.shape[0]] = total.astype(jnp.bfloat16)
        at += total.shape[0]


def add_parts(early, late):
    rows = early[0].shape[0] + late[0].shape[0]
    return pl.pallas_call(
        functools.partial(add_kernel, len(early)),
        out_shape=pltpu.VMEM((rows, early[0].shape[1]), jnp.bfloat16),
        in_specs=[VMEM] * (len(early) + len(late)),
        out_specs=VMEM,
        compiler_params=GRANT,
        name="add_parts",
    )(*early, *late)


def fill_right(right_ref, pieces, across, place_ref, owner_ref):
    sites = len(pieces)
    nvec = right_ref.shape[0] // 2
    momenta = right_ref.shape[1] // (3 * LANES)
    block = nvec // 2
    rows = block // sites
    v = lax.rem(place_ref[1] + across, 2)
    leads = owner_ref[v] == 0
    lower = lax.broadcasted_iota(jnp.int32, (rows, LANES), 1) < LANES // 2
    sign = jnp.where(lower == leads, -1.0, 1.0).astype(jnp.bfloat16)
    for up, piece in enumerate(pieces):
        z = lax.rem(place_ref[0] + up, sites)
        for part, owner in ((0, owner_ref[v]), (1, owner_ref[1 - v])):
            row = pl.multiple_of(owner * block + z * rows, 16)
            low = pl.multiple_of(nvec + owner * block + z * rows, 16)
            here = slice(part * rows, (part + 1) * rows)
            right_ref[pl.ds(row, rows), :] = piece[here, :]
            for p in range(momenta):
                first, second, ends = (3 * p * LANES + k * LANES for k in range(3))
                halves = piece[here, ends : ends + LANES]
                swapped = jnp.concatenate([halves[:, LANES // 2 :], halves[:, : LANES // 2]], axis=1)
                right_ref[pl.ds(low, rows), first : first + LANES] = -piece[here, second : second + LANES]
                right_ref[pl.ds(low, rows), second : second + LANES] = piece[here, first : first + LANES]
                right_ref[pl.ds(low, rows), ends : ends + LANES] = swapped * sign


def pair_of(tau_ref, n):
    left = [jnp.concatenate([tau_ref[n + k, 0], tau_ref[n + k, 1]], axis=1) for k in range(2)]
    return jnp.concatenate(left, axis=0)


def first_kernel(sites, place_ref, owner_ref, tau_ref, *refs):
    pieces, (out_ref, right_ref) = refs[:sites], refs[sites:]
    fill_right(right_ref, pieces, 0, place_ref, owner_ref)
    rows = tau_ref.shape[2]

    def step(n, carry):
        product = jnp.dot(pair_of(tau_ref, 2 * n), right_ref[...], preferred_element_type=jnp.float32)
        for k in range(2):
            out_ref[2 * n + k] = product[k * rows : (k + 1) * rows].astype(jnp.bfloat16)
        return carry

    lax.fori_loop(0, tau_ref.shape[0] // 2, step, 0)


def second_kernel(sites, place_ref, owner_ref, tau_ref, first_ref, *refs):
    pieces, (out_ref, right_ref) = refs[:sites], refs[sites:]

    @pl.when(pl.program_id(0) == 0)
    def assemble():
        fill_right(right_ref, pieces, 1, place_ref, owner_ref)

    leads = owner_ref[place_ref[1]] == 0
    rows = tau_ref.shape[2]
    momenta = out_ref.shape[1]
    lower = lax.broadcasted_iota(jnp.int32, (rows, LANES), 1) < LANES // 2
    both = jnp.dot(pair_of(tau_ref, 0), right_ref[...], preferred_element_type=jnp.float32)
    for k in range(2):

        def ordered(tile):
            mine = first_ref[k, :, tile * LANES : (tile + 1) * LANES].astype(jnp.float32)
            theirs = both[k * rows : (k + 1) * rows, tile * LANES : (tile + 1) * LANES]
            return jnp.where(leads, mine, theirs), jnp.where(leads, theirs, mine)

        for p in range(momenta):
            low_ends, high_ends = ordered(3 * p + 2)
            middles = (jnp.where(lower, low_ends, high_ends),
                       pltpu.roll(jnp.where(lower, high_ends, low_ends), LANES // 2, 1))
            for c in range(2):
                low, high = ordered(3 * p + c)
                out_ref[k, p, c, :, :LANES] = low.astype(jnp.bfloat16)
                out_ref[k, p, c, :, LANES : 2 * LANES] = middles[c].astype(jnp.bfloat16)
                out_ref[k, p, c, :, 2 * LANES :] = high.astype(jnp.bfloat16)


def project_first(tau, place, owner, pieces, momenta):
    outer, _, rows, nvec = tau.shape
    return pl.pallas_call(
        functools.partial(first_kernel, len(pieces)),
        out_shape=pltpu.VMEM((outer, rows, momenta * 3 * LANES), jnp.bfloat16),
        in_specs=[SMEM, SMEM] + [VMEM] * (1 + len(pieces)),
        out_specs=VMEM,
        scratch_shapes=[pltpu.VMEM((2 * nvec, momenta * 3 * LANES), jnp.bfloat16)],
        cost_estimate=pl.CostEstimate(
            flops=2 * outer * rows * 2 * nvec * nvec * momenta, bytes_accessed=outer * rows * nvec * 8,
            transcendentals=0),
        compiler_params=GRANT,
        name="project_first",
    )(place, owner, tau, *pieces)


def project_second(tau, place, owner, first, pieces, momenta):
    outer, _, rows, nvec = tau.shape
    return pl.pallas_call(
        functools.partial(second_kernel, len(pieces)),
        grid=(outer // 2,),
        out_shape=jax.ShapeDtypeStruct((outer, momenta, 2, rows, nvec), jnp.bfloat16),
        in_specs=[SMEM, SMEM, pl.BlockSpec((2, 2, rows, nvec), lambda i: (i, 0, 0, 0)),
                  pl.BlockSpec((2, *first.shape[1:]), lambda i: (i, 0, 0))] + [VMEM] * len(pieces),
        out_specs=pl.BlockSpec((2, momenta, 2, rows, nvec), lambda i: (i, 0, 0, 0, 0)),
        scratch_shapes=[pltpu.VMEM((2 * nvec, momenta * 3 * LANES), jnp.bfloat16)],
        cost_estimate=pl.CostEstimate(
            flops=2 * outer * rows * 2 * nvec * nvec * momenta, bytes_accessed=outer * rows * nvec * 12,
            transcendentals=0),
        compiler_params=GRANT,
        name="project_second",
    )(place, owner, tau, first, *pieces)


def from_place(block, up, across):
    sites, groups = lax.axis_size("site"), lax.axis_size("vec")
    route = []
    for z in range(sites):
        for v in range(groups):
            route.append((((z + up) % sites) * groups + (v + across) % groups, z * groups + v))
    return lax.ppermute(block, ("site", "vec"), route)


ORDER = (("filter", 0), ("filter", 1), ("finish", 0), ("filter", 2), ("finish", 1), ("finish", 2))


def per_device(eigvecs, links, peramb, block_owner, momenta):
    sites = lax.axis_size("site")
    site, group = lax.axis_index("site"), lax.axis_index("vec")
    block = eigvecs.shape[3]
    own = eigvecs.reshape(6, block * 4, LANES)
    own_links = links.reshape(216, LANES)
    place = jnp.stack([site, group]).astype(jnp.int32)

    received, packed = [], []
    for chunk in range(len(CHUNKS)):
        after = packed[:1]
        if chunk == 2:
            after = [received[0][0], packed[0]]
        if chunk == 0:
            packed = first_pack(own, sites, own_links)
        else:
            packed = pack(own, place, chunk, sites, after)
        received.append([from_place(packed[d - 1], -d, 0) for d in range(1, sites)])

    flat = lax.broadcasted_iota(jnp.int32, (4, LANES), 0) * LANES + lax.broadcasted_iota(jnp.int32, (4, LANES), 1)
    theta = phase_angle(momenta, flat % LX, flat // LX, jnp.full_like(flat, site), sites)
    cosine, sine = jnp.cos(theta), jnp.sin(theta)

    table = link_tables([own_links] + received[0])
    hops, filtered, shifted, other = {}, {}, {}, {}
    last = None
    for kind, chunk in ORDER:
        after = [] if last is None else [last]
        if kind == "filter":
            out = filter_chunk(own, place, chunk, received[chunk], table, after)
            hops[chunk] = [out[0]] + [from_place(out[d], d, 0) for d in range(1, sites)]
            last = out[0]
        else:
            f, s = finish(own, place, chunk, hops[chunk], cosine, sine, after)
            other[chunk] = from_place(f, 0, 1)
            filtered[chunk], shifted[chunk] = f, s
            last = s
    filtered, shifted, other = ([group_of[n] for n in range(len(CHUNKS))] for group_of in (filtered, shifted, other))

    *parts, right = elementals(place, block_owner, filtered + other[:1], shifted, None, sites)
    sent = [from_place(parts[d], -d, 0) for d in range(1, sites)]
    early = [parts[0], *sent]
    parts = elementals(place, block_owner, other[1:], None, right, sites)
    sent = [from_place(parts[d], -d, 0) for d in range(1, sites)]
    mine = add_parts(early, [parts[0], *sent])

    across = [from_place(mine, 0, 1)]
    pieces = [mine] + [from_place(mine, up, 0) for up in range(1, sites)]
    across += [from_place(piece, 0, 1) for piece in pieces[1:]]
    sinks, spins = peramb.shape[1], peramb.shape[2]
    tau = peramb.reshape(sinks * spins, 2, block, peramb.shape[5])
    first = project_first(tau, place, block_owner, pieces, momenta.shape[0])
    result = project_second(tau, place, block_owner, first, across, momenta.shape[0])
    return result.reshape(1, sinks, spins, momenta.shape[0], 2, block, peramb.shape[5])


def from_behind(block, axis, distance):
    devices = range(lax.axis_size(axis))
    route = [((i - distance) % len(devices), i) for i in devices]
    return lax.ppermute(block, axis, route)


def with_halo(block, sides, width):
    for axis, dim in sides:
        count = lax.axis_size(axis)
        forward = [(i, i + 1) for i in range(count - 1)]
        forward.append((count - 1, 0))
        backward = [(target, source) for source, target in forward]
        low = lax.ppermute(
            lax.slice_in_dim(block, block.shape[dim] - width, None, axis=dim), axis, forward
        )
        high = lax.ppermute(lax.slice_in_dim(block, 0, width, axis=dim), axis, backward)
        block = jnp.concatenate([low, block, high], axis=dim)
    return block


def along(field, direction, sense):
    width = field.shape[-1]
    column = lax.broadcasted_iota(jnp.int32, (width,), 0) % LX
    if direction == 0:
        if sense > 0:
            return jnp.where(column == LX - 1, jnp.roll(field, LX - 1, -1), jnp.roll(field, -1, -1))
        return jnp.where(column == 0, jnp.roll(field, 1 - LX, -1), jnp.roll(field, 1, -1))
    return jnp.roll(field, -sense * LX, -1)


def link_times(link_re, link_im, field_re, field_im, dagger):
    result_re = []
    result_im = []
    for target in range(3):
        summed_re = jnp.zeros_like(field_re[0])
        summed_im = jnp.zeros_like(field_re[0])
        for source in range(3):
            if dagger:
                entry_re = link_re[source, target][None]
                entry_im = -link_im[source, target][None]
            else:
                entry_re = link_re[target, source][None]
                entry_im = link_im[target, source][None]
            summed_re = summed_re + entry_re * field_re[source] - entry_im * field_im[source]
            summed_im = summed_im + entry_re * field_im[source] + entry_im * field_re[source]
        result_re.append(summed_re)
        result_im.append(summed_im)
    return (jnp.stack(result_re), jnp.stack(result_im))


def chebyshev(initial, operate):
    current = operate(initial)
    following = 2.0 * operate(current) - initial
    return following


def general_device(eigvecs, links, peramb, block_owner, momenta):
    vectors = eigvecs[0]
    links_here = links[0]
    block = vectors.shape[2]
    layers = vectors.shape[3]
    plane = vectors.shape[4]
    site_count = lax.axis_size("site")
    group_count = lax.axis_size("vec")
    site_rank = lax.axis_index("site")
    group_rank = lax.axis_index("vec")
    portion = plane // group_count
    top_plane = links_here[2, :, :, :, layers - 1 :, :]
    below = from_behind(top_plane, "site", 1)
    behind_links = jnp.concatenate([below, links_here[2, :, :, :, : layers - 1, :]], axis=3)
    back_links = []
    for direction in range(2):
        back_links.append(
            (
                along(links_here[direction, 0], direction, -1),
                along(links_here[direction, 1], direction, -1),
            )
        )
    back_links.append((behind_links[0], behind_links[1]))

    def operate(field):
        padded = with_halo(field, (("site", 3),), 1)
        total_re = jnp.zeros_like(field[0])
        total_im = jnp.zeros_like(field[0])
        for direction in range(3):
            if direction < 2:
                ahead = along(field, direction, 1)
                behind = along(field, direction, -1)
            else:
                ahead = padded[:, :, :, 2:]
                behind = padded[:, :, :, :-2]
            forward = link_times(
                links_here[direction, 0], links_here[direction, 1], ahead[0], ahead[1], False
            )
            backward = link_times(
                back_links[direction][0], back_links[direction][1], behind[0], behind[1], True
            )
            total_re = total_re + forward[0] + backward[0]
            total_im = total_im + forward[1] + backward[1]
        return jnp.stack([total_re, total_im]) * (-1.0 / 6.0)

    filtered = chebyshev(vectors, operate).astype(jnp.bfloat16)
    received = lax.all_to_all(filtered, "vec", split_axis=4, concat_axis=2, tiled=True)
    grouped = received.reshape(2, 3, group_count, block, layers, portion)
    ranks = jnp.arange(group_count, dtype=jnp.int32)
    inverse = jnp.sum(
        ranks[:, None] * (block_owner[:, None] == ranks[None, :]).astype(jnp.int32), axis=0
    )
    ordered = jnp.take(grouped, inverse, axis=2).reshape(2, 3, group_count * block, layers, portion)
    nvec = group_count * block
    flat = group_rank * portion + lax.broadcasted_iota(jnp.int32, (layers, portion), 1)
    depth = site_rank * layers + lax.broadcasted_iota(jnp.int32, (layers, portion), 0)
    theta = phase_angle(momenta, flat % LX, flat // LX, depth, layers * site_count)
    values = ordered.astype(jnp.float32)
    cosine = jnp.cos(theta)[:, None, None]
    sine = jnp.sin(theta)[:, None, None]
    shift_re = cosine * values[0] + sine * values[1]
    shift_im = cosine * values[1] - sine * values[0]
    shifted = jnp.stack([shift_re, shift_im], axis=1).astype(jnp.bfloat16)
    products = jnp.einsum(
        "acizs,pbckzs->aipbk", ordered, shifted, preferred_element_type=jnp.float32
    )
    real = products[0, :, :, 0] + products[1, :, :, 1]
    imag = products[0, :, :, 1] - products[1, :, :, 0]
    momentum_count = momenta.shape[0]
    partial_sum = jnp.stack([real, imag], axis=2).reshape(nvec, momentum_count * 2 * nvec)
    tau = peramb[0]
    tau_rows = tau.reshape(-1, nvec)
    summed = lax.psum(partial_sum, ("site", "vec")).astype(jnp.bfloat16)
    joined = jnp.dot(tau_rows, summed, preferred_element_type=jnp.float32)
    sinks = tau.shape[0]
    spins = tau.shape[1]
    layout = joined.reshape(sinks, spins, 2, block, momentum_count, 2, nvec)
    real_part = layout[:, :, 0, :, :, 0] - layout[:, :, 1, :, :, 1]
    imag_part = layout[:, :, 0, :, :, 1] + layout[:, :, 1, :, :, 0]
    stacked = jnp.stack([real_part, imag_part], axis=0)
    result = jnp.transpose(stacked, (1, 2, 4, 0, 3, 5))
    return result[None].astype(jnp.bfloat16)


def choose(eigvecs, links, peramb, block_owner, momenta):
    block, layers, plane = eigvecs.shape[3:]
    sites, groups = lax.axis_size("site"), lax.axis_size("vec")
    fits = layers == 1 and plane == LX * LY == 4 * LANES and sites == 4 and groups == 2
    fits = fits and block == sites * sum(CHUNKS) and 2 * block == 3 * LANES and set(CHUNKS) == {16}
    fits = fits and peramb.shape[1] * peramb.shape[2] % 2 == 0 and (2 * block) % (32 * sites) == 0 and block % (2 * block // sites) == 0
    device = per_device if fits else general_device
    return device(eigvecs, links, peramb, block_owner, momenta)


def solution(mesh):
    placed = (
        P(("cfg", "tslice"), None, None, "vec", "site", None),
        P(("cfg", "tslice"), None, None, None, None, "site", None),
        P(("cfg", "tslice"), "site", None, None, "vec", None),
        P(),
        P(),
    )
    return jax.shard_map(
        choose,
        mesh=mesh,
        in_specs=placed,
        out_specs=P(("cfg", "tslice"), "site", None, None, None, "vec", None),
        check_vma=False,
    )
```

```python
import functools
import math

import jax
import jax.numpy as jnp
from jax import lax
from jax.experimental import pallas as pl
from jax.experimental.pallas import tpu as pltpu
from jax.sharding import PartitionSpec as P


LX = 32
LY = 16
LANES = 128

two_pi = 2.0 * math.pi

CHUNKS = (16, 16, 16)


def phase_angle(momenta, across, upward, depth, extent):
    return two_pi * (
        (momenta[:, 0, None, None] * across[None]).astype(jnp.float32) / LX
        + (momenta[:, 1, None, None] * upward[None]).astype(jnp.float32) / LY
        + (momenta[:, 2, None, None] * depth[None]).astype(jnp.float32) / extent
    )


VMEM = pl.BlockSpec(memory_space=pltpu.VMEM)
SMEM = pl.BlockSpec(memory_space=pltpu.SMEM)
ANY = pl.BlockSpec(memory_space=pl.ANY)
HBM = pl.BlockSpec(memory_space=pltpu.HBM)
GRANT = pltpu.CompilerParams(vmem_limit_bytes=16 * 2**20)


class Shifts:
    def __init__(self):
        lane = lax.broadcasted_iota(jnp.int32, (8, LANES), 1)
        row = lax.broadcasted_iota(jnp.int32, (8, LANES), 0) % 4
        column = lane % LX
        self.x_last = column == LX - 1
        self.x_first = column == 0
        self.y_high = lane >= LANES - LX
        self.y_low = lane < LX
        self.row_last = row == 3
        self.row_first = row == 0

    def ahead_x(self, v):
        return jnp.where(self.x_last, pltpu.roll(v, LX - 1, 1), pltpu.roll(v, LANES - 1, 1))

    def behind_x(self, v):
        return jnp.where(self.x_first, pltpu.roll(v, LANES - LX + 1, 1), pltpu.roll(v, 1, 1))

    def ahead_y(self, v):
        a = pltpu.roll(v, LANES - LX, 1)
        wrapped = jnp.where(self.row_last, pltpu.roll(a, 3, 0), pltpu.roll(a, 7, 0))
        return jnp.where(self.y_high, wrapped, a)

    def behind_y(self, v):
        a = pltpu.roll(v, LX, 1)
        wrapped = jnp.where(self.row_first, pltpu.roll(a, 5, 0), pltpu.roll(a, 1, 0))
        return jnp.where(self.y_low, wrapped, a)


def tables_kernel(*refs):
    table_ref = refs[-1]
    shifts = Shifts()
    scale = jnp.float32(-math.sqrt(2.0) / 6.0)
    size = refs[0].shape[0]
    links = [ref[ref.shape[0] - size :].astype(jnp.float32) for ref in refs[:-1]]
    count = len(links)

    def entry(plane, direction, part, row, col):
        e = direction * 18 + part * 9 + row * 3 + col
        value = links[plane % count][4 * e : 4 * e + 4] * scale
        return jnp.concatenate([value, value], axis=0)

    for plane in range(count):
        for direction in range(3):
            for target in range(3):
                for source in range(3):
                    slot = (2 * direction) * 27 + (target * 3 + source) * 3
                    re = entry(plane, direction, 0, target, source)
                    im = entry(plane, direction, 1, target, source)
                    table_ref[plane, slot] = re
                    table_ref[plane, slot + 1] = im
                    table_ref[plane, slot + 2] = re + im
                    slot = (2 * direction + 1) * 27 + (target * 3 + source) * 3
                    below = plane + 1 if direction == 2 else plane
                    re = entry(below, direction, 0, source, target)
                    im = entry(below, direction, 1, source, target)
                    if direction < 2:
                        move = shifts.behind_x if direction == 0 else shifts.behind_y
                        re, im = move(re), move(im)
                    table_ref[plane, slot] = re
                    table_ref[plane, slot + 1] = -im
                    table_ref[plane, slot + 2] = re - im


def link_tables(links):
    return pl.pallas_call(
        tables_kernel,
        out_shape=pltpu.VMEM((len(links), 162, 8, LANES), jnp.float32),
        in_specs=[VMEM] * len(links),
        out_specs=VMEM,
        compiler_params=GRANT,
        name="link_tables",
    )(*links)


def pack_kernel(sites, chunk, place_ref, own_ref, *refs):
    outs = refs[1 - sites :]
    rows = CHUNKS[chunk] * 4
    for d in range(1, sites):
        start = row_of(lax.rem(place_ref[0] + d, sites), own_ref.shape[1] // sites, chunk)
        out = outs[d - 1]
        for c in range(6):
            out[c * rows : (c + 1) * rows] = own_ref[c, pl.ds(start, rows), :].astype(jnp.bfloat16)


def first_pack_kernel(sites, own_ref, links_ref, *refs):
    outs, block_ref, link_ref, sems = refs[: sites - 1], refs[sites - 1], refs[sites], refs[sites + 1]
    rows = CHUNKS[0] * 4
    copies = [pltpu.make_async_copy(links_ref, link_ref, sems.at[0])]
    for d in range(1, sites):
        start = row_of(lax.rem(lax.axis_index("site") + d, sites), own_ref.shape[1] // sites, 0)
        copies.append(pltpu.make_async_copy(own_ref.at[:, pl.ds(start, rows), :], block_ref.at[d - 1], sems.at[d]))
    for copy in copies:
        copy.start()
    copies[0].wait()
    links = link_ref[...].astype(jnp.bfloat16)
    for d in range(1, sites):
        copies[d].wait()
        for c in range(6):
            outs[d - 1][c * rows : (c + 1) * rows] = block_ref[d - 1, c].astype(jnp.bfloat16)
        outs[d - 1][6 * rows :] = links


def first_pack(own, sites, links):
    rows = CHUNKS[0] * 4
    return pl.pallas_call(
        functools.partial(first_pack_kernel, sites),
        out_shape=[pltpu.VMEM((6 * rows + links.shape[0], LANES), jnp.bfloat16)] * (sites - 1),
        in_specs=[HBM, HBM],
        out_specs=[VMEM] * (sites - 1),
        scratch_shapes=[
            pltpu.VMEM((sites - 1, 6, rows, LANES), jnp.float32),
            pltpu.VMEM(links.shape, jnp.float32),
            pltpu.SemaphoreType.DMA((sites,)),
        ],
        compiler_params=pltpu.CompilerParams(vmem_limit_bytes=66 * 10**6),
        name="pack0",
    )(own, links)


def row_of(slot, rows_per_slot, chunk):
    return pl.multiple_of(slot * rows_per_slot + 4 * sum(CHUNKS[:chunk]), 32)


def pack(own, place, chunk, sites, after):
    length = 24 * CHUNKS[chunk]
    return pl.pallas_call(
        functools.partial(pack_kernel, sites, chunk),
        out_shape=[pltpu.VMEM((length, LANES), jnp.bfloat16)] * (sites - 1),
        in_specs=[SMEM, VMEM] + [ANY] * len(after),
        out_specs=[VMEM] * (sites - 1),
        compiler_params=GRANT,
    )(place, own, *after)


def filter_kernel(sites, chunk, place_ref, *refs):
    fields, table_ref = refs[:sites], refs[sites]
    outs, t1_ref = refs[-1 - sites : -1], refs[-1]
    shifts = Shifts()
    rows = CHUNKS[chunk] * 4
    home = row_of(place_ref[0], fields[0].shape[1] // sites, chunk)

    def hop(plane, here, ahead_z, behind_z):
        count = len(here(0))
        sums = [[[None] * count for _ in range(3)] for _ in range(3)]
        moves = (shifts.ahead_x, shifts.behind_x, shifts.ahead_y, shifts.behind_y, None, None)
        for direction in range(6):
            if direction < 4:
                field = [[moves[direction](v) for v in here(c)] for c in range(6)]
            else:
                take = ahead_z if direction == 4 else behind_z
                field = [take(c) for c in range(6)]
            for source in range(3):
                re, im = field[source], field[3 + source]
                factors = ([im[n] - re[n] for n in range(count)], [im[n] + re[n] for n in range(count)], re)
                for target in range(3):
                    slot = direction * 27 + (target * 3 + source) * 3
                    for k in range(3):
                        link = table_ref[plane, slot + k]
                        for n in range(count):
                            add = link * factors[k][n]
                            old = sums[target][k][n]
                            sums[target][k][n] = add if old is None else old + add
        total_re = [[sums[t][2][n] - sums[t][1][n] for n in range(count)] for t in range(3)]
        total_im = [[sums[t][2][n] + sums[t][0][n] for n in range(count)] for t in range(3)]
        return total_re + total_im

    def step(index, carry):
        base = pl.multiple_of(index * 16, 16)

        def start(plane):
            def read(c):
                ref = fields[plane % sites]
                if plane % sites == 0:
                    value = ref[c, pl.ds(pl.multiple_of(home + base, 16), 16), :]
                else:
                    value = ref[pl.ds(pl.multiple_of(c * rows + base, 16), 16), :].astype(jnp.float32)
                return [value[0:8], value[8:16]]

            return read

        def first(plane):
            return lambda c: [t1_ref[plane % sites, c, 0:8], t1_ref[plane % sites, c, 8:16]]

        for plane in range(sites):
            out = hop(plane, start(plane), start(plane - 1), start(plane + 1))
            for c in range(6):
                for n in range(2):
                    t1_ref[plane, c, 8 * n : 8 * n + 8] = out[c][n]
        for plane in range(sites):
            out = hop(plane, first(plane), first(plane - 1), first(plane + 1))
            for c in range(6):
                value = jnp.concatenate(out[c], axis=0)
                outs[plane][c, pl.ds(base, 16), :] = value.astype(jnp.bfloat16)
        return carry

    lax.fori_loop(0, rows // 16, step, 0)


def filter_chunk(own, place, chunk, received, table, after):
    sites = len(received) + 1
    rows = CHUNKS[chunk] * 4
    return pl.pallas_call(
        functools.partial(filter_kernel, sites, chunk),
        out_shape=[pltpu.VMEM((6, rows, LANES), jnp.bfloat16)] * sites,
        in_specs=[SMEM] + [VMEM] * (sites + 1) + [ANY] * len(after),
        out_specs=[VMEM] * sites,
        scratch_shapes=[pltpu.VMEM((sites, 6, 16, LANES), jnp.float32)],
        cost_estimate=pl.CostEstimate(
            flops=432 * 2 * sites * rows * LANES, bytes_accessed=6 * rows * LANES * 4 * sites, transcendentals=0),
        compiler_params=GRANT,
    )(place, own, *received, table, *after)


def finish_kernel(sites, chunk, place_ref, own_ref, *refs):
    hops = refs[:sites]
    cosine_ref, sine_ref = refs[sites : sites + 2]
    filtered_ref, shifted_ref, work_ref = refs[-3:]
    vectors = CHUNKS[chunk]
    momenta = cosine_ref.shape[0]
    for d in range(sites):
        slot = lax.rem(place_ref[0] + d, sites)
        start = row_of(slot, own_ref.shape[1] // sites, chunk)
        for c in range(6):
            work_ref[d, c] = hops[d][c].astype(jnp.float32) - own_ref[c, pl.ds(start, 4 * vectors), :]
        for color in range(3):
            for row in range(4):
                at = slice((color * 4 + row) * LANES, (color * 4 + row + 1) * LANES)
                re = work_ref[d, color, pl.ds(row, vectors, stride=4), :].astype(jnp.bfloat16)
                im = work_ref[d, 3 + color, pl.ds(row, vectors, stride=4), :].astype(jnp.bfloat16)
                filtered_ref[slot, 0, :, at] = re
                filtered_ref[slot, 1, :, at] = im
                re, im = re.astype(jnp.float32), im.astype(jnp.float32)
                for p in range(momenta):
                    cosine = cosine_ref[p, row : row + 1, :]
                    sine = sine_ref[p, row : row + 1, :]
                    shifted_ref[p, slot, 0, :, at] = (cosine * re + sine * im).astype(jnp.bfloat16)
                    shifted_ref[p, slot, 1, :, at] = (cosine * im - sine * re).astype(jnp.bfloat16)


def finish(own, place, chunk, hops, cosine, sine, after):
    sites, momenta, vectors = len(hops), cosine.shape[0], CHUNKS[chunk]
    shapes = ((sites, 2, vectors, 12 * LANES), (momenta, sites, 2, vectors, 12 * LANES))
    return pl.pallas_call(
        functools.partial(finish_kernel, sites, chunk),
        out_shape=[pltpu.VMEM(shape, jnp.bfloat16) for shape in shapes],
        in_specs=[SMEM] + [VMEM] * (sites + 3) + [ANY] * len(after),
        out_specs=[VMEM, VMEM],
        scratch_shapes=[pltpu.VMEM((sites, 6, 4 * vectors, LANES), jnp.float32)],
        cost_estimate=pl.CostEstimate(
            flops=20 * sites * 24 * vectors * LANES, bytes_accessed=sites * 24 * vectors * LANES * 12,
            transcendentals=0),
        compiler_params=GRANT,
    )(place, own, *hops, cosine, sine, *after)


def fill_left(left_ref, chunks):
    slots, _, _, depth = chunks[0].shape
    sizes = [ref.shape[2] for ref in chunks]
    for n, ref in enumerate(chunks):
        for slot in range(slots):
            at = slot * sum(sizes) + sum(sizes[:n])
            for part in range(2):
                left_ref[at : at + sizes[n], part * depth : (part + 1) * depth] = ref[slot, part]


def multiply(left_ref, right_ref, total_ref, place_ref, outs):
    segments, rows, _ = total_ref.shape
    for p in range(right_ref.shape[0]):
        product = lax.dot_general(
            left_ref[...], right_ref[p], (((1,), (1,)), ((), ())), preferred_element_type=jnp.float32)
        width = product.shape[1]
        for s in range(segments):
            total_ref[s, :, p * width : (p + 1) * width] = product[s * rows : (s + 1) * rows]
    for d in range(segments):
        outs[d][...] = total_ref[lax.rem(place_ref[0] + d, segments)].astype(outs[d].dtype)


def column_of(unit, units, leads):
    tile, half = LANES // 16, LANES // 32
    if unit < tile:
        first = (unit * 16, LANES + unit * 16)
    else:
        first = (2 * LANES + (unit - tile) * 16, 2 * LANES + (unit - tile + half) * 16)
    if unit < units - tile:
        second = (2 * LANES + (unit + half) * 16, 2 * LANES + unit * 16)
    else:
        at = (unit - units + tile) * 16
        second = (at, LANES + at)
    return [pl.multiple_of(jnp.where(leads, x, y), 16) for x, y in zip(first, second)]


def early_kernel(segments, count, place_ref, owner_ref, *refs):
    chunks = len(CHUNKS)
    left, shifted = refs[:count], refs[count : count + chunks]
    outs = refs[count + chunks : count + chunks + segments]
    right_ref, left_ref, total_ref = refs[count + chunks + segments :]
    slots, _, _, depth = left[0].shape
    block = right_ref.shape[1] // 2
    fill_left(left_ref, left)
    leads = owner_ref[place_ref[1]] == 0
    for n, ref in enumerate(shifted):
        for slot in range(slots):
            for part in range(CHUNKS[n] // 16):
                unit = (slot * sum(CHUNKS) + sum(CHUNKS[:n])) // 16 + part
                real, imaginary = column_of(unit, block // 16, leads)
                for p in range(right_ref.shape[0]):
                    re = ref[p, slot, 0, part * 16 : part * 16 + 16]
                    im = ref[p, slot, 1, part * 16 : part * 16 + 16]
                    right_ref[p, pl.ds(real, 16), :depth] = re
                    right_ref[p, pl.ds(real, 16), depth:] = im
                    right_ref[p, pl.ds(imaginary, 16), :depth] = im
                    right_ref[p, pl.ds(imaginary, 16), depth:] = -re
    multiply(left_ref, right_ref, total_ref, place_ref, outs)


def late_kernel(segments, count, place_ref, *refs):
    left, right_ref = refs[:count], refs[count]
    outs = refs[count + 1 : count + 1 + segments]
    left_ref, total_ref = refs[count + 1 + segments :]
    fill_left(left_ref, left)
    multiply(left_ref, right_ref, total_ref, place_ref, outs)


def elementals(place, owner, left, shifted, right, segments):
    _, _, _, depth = left[0].shape
    block = segments * sum(CHUNKS)
    rows = sum(ref.shape[2] for ref in left)
    early = right is None
    momenta = shifted[0].shape[0] if early else right.shape[0]
    columns = momenta * 2 * block
    shapes = [pltpu.VMEM((rows, columns), jnp.float32 if d == 0 else jnp.bfloat16) for d in range(segments)]
    if early:
        shapes.append(pltpu.VMEM((momenta, 2 * block, 2 * depth), jnp.bfloat16))
    operands = [*left, *shifted] if early else [*left, right]
    scalars = [place, owner] if early else [place]
    return pl.pallas_call(
        functools.partial(early_kernel if early else late_kernel, segments, len(left)),
        out_shape=shapes,
        in_specs=[SMEM] * len(scalars) + [VMEM] * len(operands),
        out_specs=[VMEM] * len(shapes),
        scratch_shapes=[
            pltpu.VMEM((segments * rows, 2 * depth), jnp.bfloat16),
            pltpu.VMEM((segments, rows, columns), jnp.float32),
        ],
        cost_estimate=pl.CostEstimate(
            flops=2 * segments * rows * columns * 2 * depth, bytes_accessed=8 * block * depth, transcendentals=0),
        compiler_params=GRANT,
        name="elementals_early" if early else "elementals_late",
    )(*scalars, *operands)


def add_kernel(count, *refs):
    out_ref, at = refs[-1], 0
    for group in (refs[:count], refs[count:-1]):
        total = group[0][...]
        for ref in group[1:]:
            total = total + ref[...].astype(jnp.float32)
        out_ref[at : at + total.shape[0]] = total.astype(jnp.bfloat16)
        at += total.shape[0]


def add_parts(early, late):
    rows = early[0].shape[0] + late[0].shape[0]
    return pl.pallas_call(
        functools.partial(add_kernel, len(early)),
        out_shape=pltpu.VMEM((rows, early[0].shape[1]), jnp.bfloat16),
        in_specs=[VMEM] * (len(early) + len(late)),
        out_specs=VMEM,
        compiler_params=GRANT,
        name="add_parts",
    )(*early, *late)


def fill_right(right_ref, pieces, across, place_ref, owner_ref):
    sites = len(pieces)
    nvec = right_ref.shape[0] // 2
    momenta = right_ref.shape[1] // (3 * LANES)
    block = nvec // 2
    rows = block // sites
    v = lax.rem(place_ref[1] + across, 2)
    leads = owner_ref[v] == 0
    lower = lax.broadcasted_iota(jnp.int32, (rows, LANES), 1) < LANES // 2
    sign = jnp.where(lower == leads, -1.0, 1.0).astype(jnp.bfloat16)
    for up, piece in enumerate(pieces):
        z = lax.rem(place_ref[0] + up, sites)
        for part, owner in ((0, owner_ref[v]), (1, owner_ref[1 - v])):
            row = pl.multiple_of(owner * block + z * rows, 16)
            low = pl.multiple_of(nvec + owner * block + z * rows, 16)
            here = slice(part * rows, (part + 1) * rows)
            right_ref[pl.ds(row, rows), :] = piece[here, :]
            for p in range(momenta):
                first, second, ends = (3 * p * LANES + k * LANES for k in range(3))
                halves = piece[here, ends : ends + LANES]
                swapped = jnp.concatenate([halves[:, LANES // 2 :], halves[:, : LANES // 2]], axis=1)
                right_ref[pl.ds(low, rows), first : first + LANES] = -piece[here, second : second + LANES]
                right_ref[pl.ds(low, rows), second : second + LANES] = piece[here, first : first + LANES]
                right_ref[pl.ds(low, rows), ends : ends + LANES] = swapped * sign


def pair_of(tau_ref, n):
    left = [jnp.concatenate([tau_ref[n + k, 0], tau_ref[n + k, 1]], axis=1) for k in range(2)]
    return jnp.concatenate(left, axis=0)


def first_kernel(sites, place_ref, owner_ref, tau_ref, *refs):
    pieces, (out_ref, right_ref) = refs[:sites], refs[sites:]
    fill_right(right_ref, pieces, 0, place_ref, owner_ref)
    rows = tau_ref.shape[2]

    def step(n, carry):
        product = jnp.dot(pair_of(tau_ref, 2 * n), right_ref[...], preferred_element_type=jnp.float32)
        for k in range(2):
            out_ref[2 * n + k] = product[k * rows : (k + 1) * rows].astype(jnp.bfloat16)
        return carry

    lax.fori_loop(0, tau_ref.shape[0] // 2, step, 0)


def second_kernel(sites, place_ref, owner_ref, tau_ref, first_ref, *refs):
    pieces, (out_ref, right_ref) = refs[:sites], refs[sites:]

    @pl.when(pl.program_id(0) == 0)
    def assemble():
        fill_right(right_ref, pieces, 1, place_ref, owner_ref)

    leads = owner_ref[place_ref[1]] == 0
    rows = tau_ref.shape[2]
    momenta = out_ref.shape[1]
    lower = lax.broadcasted_iota(jnp.int32, (rows, LANES), 1) < LANES // 2
    both = jnp.dot(pair_of(tau_ref, 0), right_ref[...], preferred_element_type=jnp.float32)
    for k in range(2):

        def ordered(tile):
            mine = first_ref[k, :, tile * LANES : (tile + 1) * LANES].astype(jnp.float32)
            theirs = both[k * rows : (k + 1) * rows, tile * LANES : (tile + 1) * LANES]
            return jnp.where(leads, mine, theirs), jnp.where(leads, theirs, mine)

        for p in range(momenta):
            low_ends, high_ends = ordered(3 * p + 2)
            middles = (jnp.where(lower, low_ends, high_ends),
                       pltpu.roll(jnp.where(lower, high_ends, low_ends), LANES // 2, 1))
            for c in range(2):
                low, high = ordered(3 * p + c)
                out_ref[k, p, c, :, :LANES] = low.astype(jnp.bfloat16)
                out_ref[k, p, c, :, LANES : 2 * LANES] = middles[c].astype(jnp.bfloat16)
                out_ref[k, p, c, :, 2 * LANES :] = high.astype(jnp.bfloat16)


def project_first(tau, place, owner, pieces, momenta):
    outer, _, rows, nvec = tau.shape
    return pl.pallas_call(
        functools.partial(first_kernel, len(pieces)),
        out_shape=pltpu.VMEM((outer, rows, momenta * 3 * LANES), jnp.bfloat16),
        in_specs=[SMEM, SMEM] + [VMEM] * (1 + len(pieces)),
        out_specs=VMEM,
        scratch_shapes=[pltpu.VMEM((2 * nvec, momenta * 3 * LANES), jnp.bfloat16)],
        cost_estimate=pl.CostEstimate(
            flops=2 * outer * rows * 2 * nvec * nvec * momenta, bytes_accessed=outer * rows * nvec * 8,
            transcendentals=0),
        compiler_params=GRANT,
        name="project_first",
    )(place, owner, tau, *pieces)


def project_second(tau, place, owner, first, pieces, momenta):
    outer, _, rows, nvec = tau.shape
    return pl.pallas_call(
        functools.partial(second_kernel, len(pieces)),
        grid=(outer // 2,),
        out_shape=jax.ShapeDtypeStruct((outer, momenta, 2, rows, nvec), jnp.bfloat16),
        in_specs=[SMEM, SMEM, pl.BlockSpec((2, 2, rows, nvec), lambda i: (i, 0, 0, 0)),
                  pl.BlockSpec((2, *first.shape[1:]), lambda i: (i, 0, 0))] + [VMEM] * len(pieces),
        out_specs=pl.BlockSpec((2, momenta, 2, rows, nvec), lambda i: (i, 0, 0, 0, 0)),
        scratch_shapes=[pltpu.VMEM((2 * nvec, momenta * 3 * LANES), jnp.bfloat16)],
        cost_estimate=pl.CostEstimate(
            flops=2 * outer * rows * 2 * nvec * nvec * momenta, bytes_accessed=outer * rows * nvec * 12,
            transcendentals=0),
        compiler_params=GRANT,
        name="project_second",
    )(place, owner, tau, first, *pieces)


def permuted(block, up, across):
    sites, groups = lax.axis_size("site"), lax.axis_size("vec")
    route = []
    for z in range(sites):
        for v in range(groups):
            route.append((((z + up) % sites) * groups + (v + across) % groups, z * groups + v))
    return lax.ppermute(block, ("site", "vec"), route)


ORDER = (("filter", 0), ("filter", 1), ("finish", 0), ("filter", 2), ("finish", 1), ("finish", 2))


def per_device(eigvecs, links, peramb, block_owner, momenta):
    sites = lax.axis_size("site")
    site, group = lax.axis_index("site"), lax.axis_index("vec")
    block = eigvecs.shape[3]
    own = eigvecs.reshape(6, block * 4, LANES)
    own_links = links.reshape(216, LANES)
    place = jnp.stack([site, group]).astype(jnp.int32)

    received, packed = [], []
    for chunk in range(len(CHUNKS)):
        after = packed[:1]
        if chunk == 2:
            after = [received[0][0], packed[0]]
        if chunk == 0:
            packed = first_pack(own, sites, own_links)
        else:
            packed = pack(own, place, chunk, sites, after)
        received.append([permuted(packed[d - 1], -d, 0) for d in range(1, sites)])

    flat = lax.broadcasted_iota(jnp.int32, (4, LANES), 0) * LANES + lax.broadcasted_iota(jnp.int32, (4, LANES), 1)
    theta = phase_angle(momenta, flat % LX, flat // LX, jnp.full_like(flat, site), sites)
    cosine, sine = jnp.cos(theta), jnp.sin(theta)

    table = link_tables([own_links] + received[0])
    hops, filtered, shifted, other = {}, {}, {}, {}
    last = None
    for kind, chunk in ORDER:
        after = [] if last is None else [last]
        if kind == "filter":
            out = filter_chunk(own, place, chunk, received[chunk], table, after)
            hops[chunk] = [out[0]] + [permuted(out[d], d, 0) for d in range(1, sites)]
            last = out[0]
        else:
            f, s = finish(own, place, chunk, hops[chunk], cosine, sine, after)
            other[chunk] = permuted(f, 0, 1)
            filtered[chunk], shifted[chunk] = f, s
            last = s
    filtered, shifted, other = ([group_of[n] for n in range(len(CHUNKS))] for group_of in (filtered, shifted, other))

    *parts, right = elementals(place, block_owner, filtered + other[:1], shifted, None, sites)
    sent = [permuted(parts[d], -d, 0) for d in range(1, sites)]
    early = [parts[0], *sent]
    parts = elementals(place, block_owner, other[1:], None, right, sites)
    sent = [permuted(parts[d], -d, 0) for d in range(1, sites)]
    mine = add_parts(early, [parts[0], *sent])

    across = [permuted(mine, 0, 1)]
    pieces = [mine] + [permuted(mine, up, 0) for up in range(1, sites)]
    across += [permuted(piece, 0, 1) for piece in pieces[1:]]
    sinks, spins = peramb.shape[1], peramb.shape[2]
    tau = peramb.reshape(sinks * spins, 2, block, peramb.shape[5])
    first = project_first(tau, place, block_owner, pieces, momenta.shape[0])
    result = project_second(tau, place, block_owner, first, across, momenta.shape[0])
    return result.reshape(1, sinks, spins, momenta.shape[0], 2, block, peramb.shape[5])


def from_behind(block, axis, distance):
    devices = range(lax.axis_size(axis))
    route = [((i - distance) % len(devices), i) for i in devices]
    return lax.ppermute(block, axis, route)


def with_halo(block, sides, width):
    for axis, dim in sides:
        count = lax.axis_size(axis)
        forward = [(i, i + 1) for i in range(count - 1)]
        forward.append((count - 1, 0))
        backward = [(target, source) for source, target in forward]
        low = lax.ppermute(
            lax.slice_in_dim(block, block.shape[dim] - width, None, axis=dim), axis, forward
        )
        high = lax.ppermute(lax.slice_in_dim(block, 0, width, axis=dim), axis, backward)
        block = jnp.concatenate([low, block, high], axis=dim)
    return block


def along(field, direction, sense):
    width = field.shape[-1]
    column = lax.broadcasted_iota(jnp.int32, (width,), 0) % LX
    if direction == 0:
        if sense > 0:
            return jnp.where(column == LX - 1, jnp.roll(field, LX - 1, -1), jnp.roll(field, -1, -1))
        return jnp.where(column == 0, jnp.roll(field, 1 - LX, -1), jnp.roll(field, 1, -1))
    return jnp.roll(field, -sense * LX, -1)


def link_times(link_re, link_im, field_re, field_im, dagger):
    result_re = []
    result_im = []
    for target in range(3):
        summed_re = jnp.zeros_like(field_re[0])
        summed_im = jnp.zeros_like(field_re[0])
        for source in range(3):
            if dagger:
                entry_re = link_re[source, target][None]
                entry_im = -link_im[source, target][None]
            else:
                entry_re = link_re[target, source][None]
                entry_im = link_im[target, source][None]
            summed_re = summed_re + entry_re * field_re[source] - entry_im * field_im[source]
            summed_im = summed_im + entry_re * field_im[source] + entry_im * field_re[source]
        result_re.append(summed_re)
        result_im.append(summed_im)
    return (jnp.stack(result_re), jnp.stack(result_im))


def chebyshev(initial, operate):
    current = operate(initial)
    following = 2.0 * operate(current) - initial
    return following


def general_device(eigvecs, links, peramb, block_owner, momenta):
    vectors = eigvecs[0]
    links_here = links[0]
    block = vectors.shape[2]
    layers = vectors.shape[3]
    plane = vectors.shape[4]
    site_count = lax.axis_size("site")
    group_count = lax.axis_size("vec")
    site_rank = lax.axis_index("site")
    group_rank = lax.axis_index("vec")
    portion = plane // group_count
    top_plane = links_here[2, :, :, :, layers - 1 :, :]
    below = from_behind(top_plane, "site", 1)
    behind_links = jnp.concatenate([below, links_here[2, :, :, :, : layers - 1, :]], axis=3)
    back_links = []
    for direction in range(2):
        back_links.append(
            (
                along(links_here[direction, 0], direction, -1),
                along(links_here[direction, 1], direction, -1),
            )
        )
    back_links.append((behind_links[0], behind_links[1]))

    def operate(field):
        padded = with_halo(field, (("site", 3),), 1)
        total_re = jnp.zeros_like(field[0])
        total_im = jnp.zeros_like(field[0])
        for direction in range(3):
            if direction < 2:
                ahead = along(field, direction, 1)
                behind = along(field, direction, -1)
            else:
                ahead = padded[:, :, :, 2:]
                behind = padded[:, :, :, :-2]
            forward = link_times(
                links_here[direction, 0], links_here[direction, 1], ahead[0], ahead[1], False
            )
            backward = link_times(
                back_links[direction][0], back_links[direction][1], behind[0], behind[1], True
            )
            total_re = total_re + forward[0] + backward[0]
            total_im = total_im + forward[1] + backward[1]
        return jnp.stack([total_re, total_im]) * (-1.0 / 6.0)

    filtered = chebyshev(vectors, operate).astype(jnp.bfloat16)
    received = lax.all_to_all(filtered, "vec", split_axis=4, concat_axis=2, tiled=True)
    grouped = received.reshape(2, 3, group_count, block, layers, portion)
    ranks = jnp.arange(group_count, dtype=jnp.int32)
    inverse = jnp.sum(
        ranks[:, None] * (block_owner[:, None] == ranks[None, :]).astype(jnp.int32), axis=0
    )
    ordered = jnp.take(grouped, inverse, axis=2).reshape(2, 3, group_count * block, layers, portion)
    nvec = group_count * block
    flat = group_rank * portion + lax.broadcasted_iota(jnp.int32, (layers, portion), 1)
    depth = site_rank * layers + lax.broadcasted_iota(jnp.int32, (layers, portion), 0)
    theta = phase_angle(momenta, flat % LX, flat // LX, depth, layers * site_count)
    values = ordered.astype(jnp.float32)
    cosine = jnp.cos(theta)[:, None, None]
    sine = jnp.sin(theta)[:, None, None]
    shift_re = cosine * values[0] + sine * values[1]
    shift_im = cosine * values[1] - sine * values[0]
    shifted = jnp.stack([shift_re, shift_im], axis=1).astype(jnp.bfloat16)
    products = jnp.einsum(
        "acizs,pbckzs->aipbk", ordered, shifted, preferred_element_type=jnp.float32
    )
    real = products[0, :, :, 0] + products[1, :, :, 1]
    imag = products[0, :, :, 1] - products[1, :, :, 0]
    momentum_count = momenta.shape[0]
    partial_sum = jnp.stack([real, imag], axis=2).reshape(nvec, momentum_count * 2 * nvec)
    tau = peramb[0]
    tau_rows = tau.reshape(-1, nvec)
    summed = lax.psum(partial_sum, ("site", "vec")).astype(jnp.bfloat16)
    joined = jnp.dot(tau_rows, summed, preferred_element_type=jnp.float32)
    sinks = tau.shape[0]
    spins = tau.shape[1]
    layout = joined.reshape(sinks, spins, 2, block, momentum_count, 2, nvec)
    real_part = layout[:, :, 0, :, :, 0] - layout[:, :, 1, :, :, 1]
    imag_part = layout[:, :, 0, :, :, 1] + layout[:, :, 1, :, :, 0]
    stacked = jnp.stack([real_part, imag_part], axis=0)
    result = jnp.transpose(stacked, (1, 2, 4, 0, 3, 5))
    return result[None].astype(jnp.bfloat16)


def choose(eigvecs, links, peramb, block_owner, momenta):
    block, layers, plane = eigvecs.shape[3:]
    sites, groups = lax.axis_size("site"), lax.axis_size("vec")
    fits = layers == 1 and plane == LX * LY == 4 * LANES and sites == 4 and groups == 2
    fits = fits and block == sites * sum(CHUNKS) and 2 * block == 3 * LANES and set(CHUNKS) == {16}
    fits = fits and peramb.shape[1] * peramb.shape[2] % 2 == 0 and (2 * block) % (32 * sites) == 0 and block % (2 * block // sites) == 0
    device = per_device if fits else general_device
    return device(eigvecs, links, peramb, block_owner, momenta)


def solution(mesh):
    placed = (
        P(("cfg", "tslice"), None, None, "vec", "site", None),
        P(("cfg", "tslice"), None, None, None, None, "site", None),
        P(("cfg", "tslice"), "site", None, None, "vec", None),
        P(),
        P(),
    )
    return jax.shard_map(
        choose,
        mesh=mesh,
        in_specs=placed,
        out_specs=P(("cfg", "tslice"), "site", None, None, None, "vec", None),
        check_vma=False,
    )
```
